32 devices in a mesh: dp: 4 (over y, x), fsdp: 8 (over z, core).
Axes of the slice: x: 2, y: 2, z: 4, core: 2. Of those that a mesh axis runs over, the one named last changes fastest.
Arguments:
- hidden: bfloat16 [16384, 1536], P(('dp', 'fsdp')), may hold values from -6 to 6
- lengths: int32 [512], P(('dp', 'fsdp')), may hold values from 1 to 32
- norm_gain: float32 [1536], replicated, may hold values from 0.1 to 1.9
- up_weight: bfloat16 [1536, 3072], P('fsdp'), may hold values from -0.15625 to 0.15625
- down_weight: bfloat16 [3072, 1536], P('fsdp'), may hold values from -0.109375 to 0.109375
- pool_gain: float32 [1536], replicated, may hold values from 0.1 to 1.9
- proj_weight: bfloat16 [1536, 768], P('fsdp'), may hold values from -1 to 1
- owners: int32 [512, 1], P(('dp', 'fsdp')), may hold values from 0 to 3; in each aligned block of 16 rows (0 to 15, 16 to 31, ...) at most 8 rows name the same one
Outputs:
- owned: bfloat16 [1024, 768], P(('dp', 'fsdp'))
The draws below stay inside these ranges and needn't reach their ends.
Inputs may be any that keep to these rules, and one draw needn't show every extreme that they name: `owners`: in each aligned block of 16 passages no owner is named by more than 8 passages, a bound that some block reaches.
All inputs are finite; a program needn't handle non-finite values.
Results may differ from the reference program's by a relative error of at most 0.014.
Values may be sent and summed in bfloat16 or wider, within the bound.
A program may use at most 128 MiB of HBM per device.

```python
import math
import jax
import jax.numpy as jnp
import numpy as np
from jax import lax

D = 1536
FF = 3072
E = 768
LEN = 32
PASS_DEV = 16
ITERS = 4
PASSAGES = 512
CAP = 8
N_DP = 4
N_FSDP = 8


def draw_proj_weight(key, part):
    entry_key, scale_key = jax.random.split(jax.random.fold_in(key, 7))
    entries = jax.random.truncated_normal(entry_key, -3.0, 3.0, (D, E), jnp.float32)
    column_scale = jnp.exp(jax.random.uniform(scale_key, (E,), jnp.float32, math.log(0.3), math.log(3.0)))
    scaled = entries * column_scale[None, :] * (1.0 / math.sqrt(D))
    return jnp.clip(scaled, -1.0, 1.0).astype(jnp.bfloat16)


def place_ends(values, key, least, top_value):
    extent = values.shape
    index_at = [jax.random.randint(jax.random.fold_in(key, axis), (), 0, extent[axis]) for axis in range(len(extent))]
    values = values.at[tuple(index_at)].set(least)
    longest = extent.index(max(extent))
    index_at[longest] = (index_at[longest] + 1) % extent[longest]
    return values.at[tuple(index_at)].set(top_value)


def level_of(rng, shape, cuts, least, top_value):
    factor_of = 1.0
    for dim, parts in cuts:
        heights = jax.random.uniform(jax.random.fold_in(jax.random.fold_in(rng, 6), dim), (parts,), jnp.float32, least / len(cuts), top_value / len(cuts))
        factor_of = factor_of * jnp.repeat(jnp.exp(heights), shape[dim] // parts).reshape((-1,) + (1,) * (len(shape) - 1 - dim))
    return factor_of


def assign_block(own_key, own, number, rows, count, top, limit, slope):
    ranking = jax.random.permutation(own_key, count)
    crowded, usual = portions_of(count, rows * top, limit, slope, True), portions_of(count, rows * top, limit, slope, False)
    places = jnp.arange(count)

    def named(sizes, rotation):
        used = int((sizes > 0).sum())
        fixed = max(1, used // 4)
        shifted = fixed + (places - fixed + rotation * (used - fixed)) % max(1, count - fixed)
        return jnp.zeros((count,), jnp.int32).at[ranking[jnp.where(places < fixed, places, shifted)]].set(jnp.asarray(sizes, jnp.int32))

    sizes = jnp.where(number % 4 == 0, named(crowded, number // 4), named(usual, number - number // 4 - 1))
    mixed = jax.random.permutation(jax.random.fold_in(own, 3), count)
    giver, receiver = mixed[0:count // 2 * 2:2], mixed[1:count // 2 * 2:2]
    slack = jnp.minimum(sizes[giver] - 1, limit - sizes[receiver]) // 2
    slack = jnp.where((giver == ranking[0]) | (receiver == ranking[0]) | (sizes[receiver] == 0), 0, jnp.maximum(slack, 0))
    shifted = jax.random.randint(jax.random.fold_in(own, 4), (count // 2,), 0, 1 << 20) % (slack + 1)
    sizes = sizes.at[giver].add(-shifted).at[receiver].add(shifted)
    labels = jnp.searchsorted(jnp.cumsum(sizes), jnp.arange(rows * top), side="right").astype(jnp.int32)
    grid = labels.reshape(top, rows).T
    grid = grid[jax.random.permutation(jax.random.fold_in(own, 1), rows)]
    rotation = jax.random.randint(jax.random.fold_in(own, 2), (rows, 1), 0, top)
    return jnp.take_along_axis(grid, (jnp.arange(top)[None, :] + rotation) % top, axis=1)


def portions_of(count, total, reach, lean, full):
    loads = [(1 << 20) // math.isqrt(grade ** lean) + 1 for grade in range(1, count + 1)]
    largest = reach if full else min(reach, max(-(-total // count), total * loads[0] // sum(loads)))
    least = 1 if total - largest >= count - 1 else 0
    counts, spare = [largest] + [least] * (count - 1), total - largest - least * (count - 1)
    while spare > 0:
        candidates = [i for i in range(1, count) if counts[i] < largest] or [i for i in range(1, count) if counts[i] < reach]
        mass, left = sum([loads[i] for i in candidates]), spare
        for i in candidates:
            addition = min(reach - counts[i], max(1, left * loads[i] // mass), spare)
            counts[i] = counts[i] + addition
            spare = spare - addition
    return np.array(counts)


def gaussian(own_key, dims, scale, reach, shards=(), kind=jnp.bfloat16):
    values = jax.random.normal(own_key, dims, jnp.float32) * scale
    if len(shards) > 0:
        values = level_of(own_key, dims, shards, -0.22, 0.18) * values
    return jnp.clip(values, min=-reach, max=reach).astype(kind)


def setup_inputs(seed: int = 0) -> dict:
    splits = jax.random.split(jax.random.key(seed), 9)
    hidden = gaussian(splits[0], (PASSAGES * LEN, D), 1.0, 6.0, ((0, 32),))
    lengths = place_ends(jax.random.randint(splits[1], (PASSAGES,), 1, LEN + 1), jax.random.fold_in(splits[1], 1), 1, LEN).astype(jnp.int32)
    norm_gain = jnp.clip(1.0 + 0.18 * jax.random.normal(splits[2], (D,), jnp.float32), 0.1, 1.9)
    up_weight = gaussian(splits[3], (D, FF), D ** -0.5, 0.15625, ((0, 8),))
    down_weight = gaussian(splits[4], (FF, D), FF ** -0.5, 0.109375, ((0, 8),))
    pool_gain = jnp.clip(1.0 + 0.18 * jax.random.normal(splits[5], (D,), jnp.float32), 0.1, 1.9)
    proj_weight = draw_proj_weight(jax.random.fold_in(splits[8], 71), 0)
    owners_keys = jax.random.split(jax.random.fold_in(splits[7], 1), PASSAGES // PASS_DEV)
    owners_turns = jax.random.permutation(jax.random.fold_in(splits[7], 3), PASSAGES // PASS_DEV)
    owners = jax.vmap(lambda own, number: assign_block(jax.random.fold_in(splits[7], 2), own, number, PASS_DEV, N_DP, 1, CAP, 1))(owners_keys, owners_turns).reshape((PASSAGES, 1))
    return dict(hidden=hidden, lengths=lengths, norm_gain=norm_gain, up_weight=up_weight, down_weight=down_weight, pool_gain=pool_gain, proj_weight=proj_weight, owners=owners)


RIDGE_TERM = 1.0
EPSILON = 1e-06
PRECISE = lax.Precision.HIGHEST

def rms_scale(values, gain_vector):
    return values * lax.rsqrt(lax.optimization_barrier(jnp.mean(values * values, axis=-1, keepdims=True)) + EPSILON) * gain_vector

def build_covariance(full_sums, average_sum, row_count):
    average = average_sum / row_count
    eye_matrix = jnp.eye(full_sums.shape[0], dtype=full_sums.dtype)
    covariance = full_sums / row_count - average[:, None] * average[None, :] + RIDGE_TERM * eye_matrix
    magnitude = jnp.sqrt(jnp.sum(covariance * covariance))
    initial = 4.0 / magnitude * eye_matrix - 4.0 * covariance / (magnitude * magnitude)
    return (covariance, average, initial)

def newton_update(iterate_rows, covariance, iterate_full):
    mixed = jnp.dot(jnp.dot(iterate_rows, covariance, precision=PRECISE, preferred_element_type=jnp.float32), iterate_full, precision=PRECISE, preferred_element_type=jnp.float32)
    return 2.0 * iterate_rows - mixed

def reference(hidden, lengths, norm_gain, up_weight, down_weight, pool_gain, proj_weight, owners):
    group_pass = PASS_DEV * N_FSDP

    def pool_block(inputs):
        row_block, block_lengths = inputs
        normed = rms_scale(row_block.astype(jnp.float32), norm_gain).astype(jnp.bfloat16)
        hidden_pre = jnp.dot(normed, up_weight, preferred_element_type=jnp.float32)
        activated = jax.nn.gelu(hidden_pre, approximate=True).astype(jnp.bfloat16)
        layer_out = (row_block.astype(jnp.float32) + jnp.dot(activated, down_weight, preferred_element_type=jnp.float32)).astype(jnp.bfloat16)
        grouped = layer_out.astype(jnp.float32).reshape(group_pass, LEN, D)
        keep_mask = (jnp.arange(LEN)[None, :] < block_lengths[:, None]).astype(jnp.float32)
        summed = lax.optimization_barrier(jnp.sum(grouped * keep_mask[:, :, None], axis=1))
        return summed / block_lengths.astype(jnp.float32)[:, None]
    pooled = lax.map(pool_block, (hidden.reshape(N_DP, group_pass * LEN, D), lengths.reshape(N_DP, group_pass)))
    pooled = pooled.reshape(PASSAGES, D)
    pool_normed = rms_scale(pooled, pool_gain).astype(jnp.bfloat16)
    embedded = jnp.dot(pool_normed, proj_weight, preferred_element_type=jnp.float32)
    products = jnp.dot(embedded.T, embedded, precision=PRECISE, preferred_element_type=jnp.float32)
    column_sum = lax.optimization_barrier(jnp.sum(embedded, axis=0))
    covariance, average, iterate_full = build_covariance(products, column_sum, float(PASSAGES))
    for iteration in range(ITERS - 1):
        iterate_full = newton_update(iterate_full, covariance, iterate_full)
    whitened = jnp.dot(embedded - average, iterate_full, precision=PRECISE, preferred_element_type=jnp.float32).astype(jnp.bfloat16)

    def route_block(row_values, target_owner):
        position = jnp.arange(PASS_DEV)
        earlier = (target_owner[:, None] == target_owner[None, :]) & (position[None, :] < position[:, None])
        target = target_owner * CAP + lax.optimization_barrier(jnp.sum(earlier.astype(jnp.int32), axis=1))
        selector = (jnp.arange(N_DP * CAP)[:, None] == target[None, :]).astype(jnp.bfloat16)
        return jnp.dot(selector, row_values, preferred_element_type=jnp.float32).astype(jnp.bfloat16)
    row_groups = whitened.reshape(N_DP * N_FSDP, PASS_DEV, E)
    owner_groups = owners.reshape(N_DP * N_FSDP, PASS_DEV)
    buffers = jax.vmap(route_block)(row_groups, owner_groups)
    buffers = buffers.reshape(N_DP, N_FSDP, N_DP, CAP, E).transpose(2, 1, 0, 3, 4)
    return buffers.reshape(N_DP * N_FSDP * N_DP * CAP, E)
```

```python
import functools

import jax
import jax.numpy as jnp
from jax import lax
from jax.experimental import pallas as pl
from jax.experimental.pallas import tpu as pltpu
from jax.sharding import PartitionSpec as P

RIDGE_TERM = 1.0
EPSILON = 1e-06
HIGH = lax.Precision.HIGH
MESH = pl.DeviceIdType.MESH
PLANE = 4
LANES = 128
LAG = 2


def fdot(a, b):
    return jnp.dot(a, b, precision=HIGH, preferred_element_type=jnp.float32)


def remote(src, dst, send, recv, device):
    return pltpu.make_async_remote_copy(
        src_ref=src, dst_ref=dst, send_sem=send, recv_sem=recv, device_id=device, device_id_type=MESH
    )


def meet(devices):
    barrier = pltpu.get_barrier_semaphore()
    for device in devices:
        pl.semaphore_signal(barrier, inc=1, device_id=device, device_id_type=MESH)
    return barrier


def gelu(v):
    return 0.5 * v * (1.0 + jnp.tanh(0.7978845608028654 * (v + 0.044715 * (v * v * v))))


def nearest(nz):
    return [sorted((l for l in range(nz) if l != v), key=lambda l: (abs(l - v), l)) for v in range(nz)]


def pick(index, table):
    value = table[0]
    for v in range(1, len(table)):
        value = jnp.where(index == v, table[v], value)
    return value


def embed_kernel(
    n_dp, n_fsdp, width,
    hid_ref, len_ref, ngain_ref, up_ref, down_ref, pgain_ref, proj_ref,
    emb_ref, all_ref,
    hid, nrm, upb, down2, pj, sa, ra, hs, s2, r2, s3, r3, gsel,
    h_sem, lo_sem, ps, pr, zu, zd, zr, xs, xr, ys, yr, ns, nr,
    dl, dns, dnr, as_, ar, s2s, r2s, s3s, r3s, es, er, fs, fr, qs, qr,
):
    i = lax.axis_index("dp")
    j = lax.axis_index("fsdp")
    nz = n_fsdp // 2
    z = j // 2
    c = j % 2
    q = i % PLANE
    base = i - q
    rows = up_ref.shape[0]
    level_rows = 2 * rows
    chunks = upb.shape[0]
    subs = chunks // PLANE
    wide = chunks // nz
    per = subs // wide
    pass_rows, seq = hs.shape[0] // nz, hid.shape[0] // (hs.shape[0] // nz)
    half = nz * pass_rows
    ff_rows = down_ref.shape[0]
    cols = s2.shape[2]
    emb = proj_ref.shape[1]
    qx = q + 1 - 2 * (q % 2)
    qy = q + 2 - 4 * (q // 2)
    qd = 3 - q
    partner = (i, z * 2 + 1 - c)
    near_x = (base + qx, j)
    near_y = (base + qy, j)
    peers = [(j + d) % n_fsdp for d in range(1, n_fsdp)]
    levels = [(z + d) % nz for d in range(1, nz)]
    planes = [(i + e) % n_dp for e in range(1, n_dp)]
    order = nearest(nz)
    near = [pick(z, [order[v][s] for v in range(nz)]) for s in range(nz - 1)]
    pending = []

    def along(level):
        return (i, level * 2 + c)

    def send(src, dst, ssem, rsem, device):
        copy = remote(src, dst, ssem, rsem, device)
        copy.start()
        pending.append(copy)
        return copy

    barrier = meet([(i, p) for p in peers] + [(p, j) for p in planes])

    hid_copy = pltpu.make_async_copy(hid_ref, hid, h_sem)
    hid_copy.start()

    own_k = [q * subs + s for s in range(subs)]
    x_k = [qx * subs + s for s in range(subs)]
    y_k = [qy * subs + s for s in range(subs)]
    d_k = [qd * subs + s for s in range(subs)]
    by_z = [s for s in range(subs) if s % 3 == 0]
    by_x = [s for s in range(subs) if s % 3 == 1]
    by_y = [s for s in range(subs) if s % 3 == 2]
    z_k = own_k + [d_k[s] for s in by_z]
    first = z_k + x_k + y_k + [d_k[s] for s in by_x + by_y]

    def source(core, k):
        at = ((k // wide * 2 + core) * wide + k % wide) * LANES
        return up_ref.at[:, pl.ds(pl.multiple_of(at, LANES), LANES)]

    def mine(k):
        return upb.at[k, pl.ds(pl.multiple_of(j * rows, rows), rows), :]

    def piece(k, level):
        return upb.at[k, pl.ds(pl.multiple_of(level * level_rows, level_rows), level_rows), :]

    local = []
    for n, k in enumerate(first):
        copy = pltpu.make_async_copy(source(c, k), mine(k), lo_sem.at[n])
        copy.start()
        local.append(copy)
    down_copy = pltpu.make_async_copy(down_ref, down2.at[c], dl.at[0])
    down_copy.start()
    proj_copy = pltpu.make_async_copy(proj_ref, pj.at[c], dl.at[1])
    proj_copy.start()
    pl.semaphore_wait(barrier, len(peers) + len(planes))
    swapped = [
        send(source(1 - c, k), mine(k), ps.at[n], pr.at[n], partner) for n, k in enumerate(first)
    ]

    def z_copy(t, level, upward):
        part = piece(z_k[t], level)
        at = t * nz + level
        if upward:
            return remote(part, part, zu.at[at], zr.at[at], (i, (z + 1) * 2 + c))
        return remote(part, part, zd.at[at], zr.at[at], (i, (z - 1) * 2 + c))

    def start_z(t):
        local[t].wait()
        swapped[t].wait_recv()

        @pl.when(z < nz - 1)
        def _():
            z_copy(t, z, True).start()

        @pl.when(z > 0)
        def _():
            z_copy(t, z, False).start()

    start_z(0)
    start_z(1)

    hid_copy.wait()
    gain = ngain_ref[...].reshape(1, width)
    hs[...] = jnp.zeros_like(hs)

    def norm_block(p, carry):
        at = pl.ds(pl.multiple_of(p * seq, seq), seq)
        x = hid[at, :].astype(jnp.float32)
        keep = lax.broadcasted_iota(jnp.int32, (seq, 1), 0) < len_ref[p]
        scale = lax.rsqrt(jnp.sum(x * x, axis=1, keepdims=True) / width + EPSILON)
        scale = jnp.where(keep, scale, 0.0)
        nrm[c, at, :] = (x * scale * gain).astype(nrm.dtype)
        total = jnp.sum(jnp.where(keep, x, 0.0), axis=0, keepdims=True)
        hs[pl.ds(z * pass_rows + p, 1), :] = total
        return carry

    lax.fori_loop(0, pass_rows, norm_block, 0)
    nrm_copy = send(nrm.at[c], nrm.at[c], ns, nr, partner)
    down_swap = send(down_ref, down2.at[c], dns.at[0], dnr.at[0], partner)
    proj_swap = send(proj_ref, pj.at[c], dns.at[1], dnr.at[1], partner)
    pgain = pgain_ref[...].reshape(1, width)
    picked = pgain[:, :cols]
    for v in range(1, nz):
        picked = jnp.where(z == v, pgain[:, v * cols : (v + 1) * cols], picked)
    gsel[...] = picked

    def along_x(slot, k, level):
        part = piece(k, level)
        return send(part, part, xs.at[slot * nz + level], xr.at[slot * nz + level], near_x)

    def along_y(slot, k, level):
        part = piece(k, level)
        return send(part, part, ys.at[slot * nz + level], yr.at[slot * nz + level], near_y)

    done = []
    x_sent, y_sent, x_relay, y_relay = {}, {}, {}, {}

    def z_step(t, s):
        level = near[s]
        z_copy(t, level, True).wait_recv()

        @pl.when(jnp.logical_and(level < z, z < nz - 1))
        def _():
            z_copy(t, level, True).start()

        @pl.when(jnp.logical_and(level > z, z > 0))
        def _():
            z_copy(t, level, False).start()

        if t < subs:
            x_sent[t, s] = along_x(t, own_k[t], level)
            y_sent[t, s] = along_y(t, own_k[t], level)

    def xy_step(t, s):
        level = near[s]
        x_sent[t, s].wait_recv()
        y_sent[t, s].wait_recv()
        if t in by_x:
            x_relay[t, s] = along_x(subs + by_x.index(t), y_k[t], level)
        if t in by_y:
            y_relay[t, s] = along_y(subs + by_y.index(t), x_k[t], level)

    def compute(quarter, s):
        k = quarter * subs + s
        v = quarter * per + s // wide
        o = s % wide

        def slot(core, carry):
            pre = jnp.dot(nrm[core], upb[k], preferred_element_type=jnp.float32)
            total = jnp.sum(gelu(pre).reshape(pass_rows, seq, LANES), axis=1)
            sa[v, core, :, o * LANES : (o + 1) * LANES] = total.astype(sa.dtype)
            return carry

        lax.fori_loop(0, 2, slot, 0)

    def act_copy(v, e):
        core = c if e == 0 else 1 - c
        return remote(
            sa.at[v, core], ra.at[c, z], as_.at[v * 2 + e], ar.at[c * nz + z], (i, v * 2 + core)
        )

    def send_acts(quarter):
        for b in range(per):
            v = quarter * per + b

            @pl.when(v == z)
            def _():
                ra[c, z] = sa[v, c]

            @pl.when(v != z)
            def _():
                act_copy(v, 0).start()

            act_copy(v, 1).start()

    ready = []
    left = {}

    def run_one():
        if ready:
            name, quarter, s = ready.pop(0)
            compute(quarter, s)
            left[name] = left.get(name, subs) - 1
            if left[name] == 0:
                send_acts(quarter)

    z_steps = [(t, s) for t in range(len(z_k)) for s in range(nz - 1)]
    xy_steps = [(t, s) for t in range(subs) for s in range(nz - 1)]
    started = 2
    waited_n = 0
    for n in range(max(len(z_steps), len(xy_steps) + LAG)):
        if n < len(z_steps):
            t, s = z_steps[n]
            z_step(t, s)
            if s == nz - 2:
                if started < len(z_k):
                    start_z(started)
                    started += 1
                if t < subs:
                    ready.append(("own", q, t))
                else:
                    ready.append(("diag", qd, by_z[t - subs]))
        if 0 <= n - LAG < len(xy_steps):
            t, s = xy_steps[n - LAG]
            xy_step(t, s)
            if s == nz - 2:
                if t == 0:
                    for copy, arrived in list(zip(local, swapped))[len(z_k) :]:
                        copy.wait()
                        arrived.wait_recv()
                ready.append(("x", qx, t))
                ready.append(("y", qy, t))
        if ready and waited_n == 0:
            nrm_copy.wait_recv()
            waited_n = 1
        run_one()
    while ready:
        run_one()
    for t in by_x:
        for s in range(nz - 1):
            x_relay[t, s].wait_recv()
        ready.append(("diag", qd, t))
        run_one()
    for t in by_y:
        for s in range(nz - 1):
            y_relay[t, s].wait_recv()
        ready.append(("diag", qd, t))
        run_one()

    down_copy.wait()
    down_swap.wait_recv()
    for v in range(nz):
        for e in range(2):
            core = c if e == 0 else 1 - c
            arrival = remote(
                sa.at[v, core], ra.at[core, v], as_.at[v * 2 + e], ar.at[core * nz + v], partner
            )
            if e == 0:

                @pl.when(v != z)
                def _():
                    arrival.wait_recv()

            else:
                arrival.wait_recv()

    acts = [ra[core].reshape(half, wide * LANES)[:, :ff_rows] for core in range(2)]

    def part_copy(v):
        return remote(s2.at[v], r2.at[z], s2s.at[v], r2s.at[z], along(v))

    for v in range(nz):
        at = slice(v * cols, (v + 1) * cols)
        part = hs[:, at]
        for core in range(2):
            part = part + jnp.dot(acts[core], down2[core, :, at], preferred_element_type=jnp.float32)
        s2[v] = part.astype(s2.dtype)

        @pl.when(v != z)
        def _():
            part_copy(v).start()

    proj_copy.wait()
    proj_swap.wait_recv()
    pooled = s2[z].astype(jnp.float32)
    for v in levels:
        remote(s2.at[v], r2.at[v], s2s.at[v], r2s.at[v], along(v)).wait_recv()
        pooled = pooled + r2[v].astype(jnp.float32)
    squares = jnp.sum(pooled * pooled, axis=1, keepdims=True)
    scaled = (pooled * gsel[...]).astype(proj_ref.dtype)
    part = jnp.dot(scaled, pj[...].reshape(cols, emb), preferred_element_type=jnp.float32)
    s3[:, :, :emb] = part.astype(s3.dtype).reshape(nz, pass_rows, emb)
    spread = jnp.broadcast_to(squares, (half, LANES))
    high = spread.astype(s3.dtype)
    low = (spread - high.astype(jnp.float32)).astype(s3.dtype)
    lane = lax.broadcasted_iota(jnp.int32, (half, LANES), 1)
    both = jnp.where(lane < LANES // 2, high.astype(jnp.float32), low.astype(jnp.float32))
    s3[:, :, emb:] = both.astype(s3.dtype).reshape(nz, pass_rows, LANES)
    third = [send(s3.at[v], r3.at[d], s3s.at[d], r3s.at[d], along(v)) for d, v in enumerate(levels)]
    total = s3[z].astype(jnp.float32)
    row = lax.broadcasted_iota(jnp.int32, (pass_rows, LANES), 0)
    counts = jnp.zeros((pass_rows, LANES), jnp.float32)
    for p in range(pass_rows):
        counts = jnp.where(row == p, len_ref[p].astype(jnp.float32), counts)
    counts = counts[:, :1]
    for d, copy in enumerate(third):
        copy.wait_recv()
        total = total + r3[d].astype(jnp.float32)
    norm = (total[:, emb : emb + 1] + total[:, emb + LANES // 2 : emb + LANES // 2 + 1]) / width
    embedded = total[:, :emb] * lax.rsqrt(norm + EPSILON * (counts * counts))
    emb_ref[...] = embedded
    all_ref[i, c, z] = embedded.astype(all_ref.dtype)
    mine_rows = all_ref.at[i, c, z]
    fourth = [
        send(mine_rows, mine_rows, es.at[d], er.at[d], along(v)) for d, v in enumerate(levels)
    ]
    for copy in fourth:
        copy.wait_recv()
    block = all_ref.at[i, c]
    fifth = [send(block, block, fs.at[e], fr.at[e], (p, j)) for e, p in enumerate(planes)]
    last = [send(block, block, qs.at[0], qr.at[0], partner)]
    for e, copy in enumerate(fifth):
        copy.wait_recv()
        part = all_ref.at[(i + n_dp - e - 1) % n_dp, c]
        last.append(send(part, part, qs.at[e + 1], qr.at[e + 1], partner))
    for copy in last:
        copy.wait_recv()

    for copy in pending:
        copy.wait_send()
    for t in range(len(z_k)):
        for level in range(nz):

            @pl.when(jnp.logical_and(level <= z, z < nz - 1))
            def _():
                z_copy(t, level, True).wait_send()

            @pl.when(jnp.logical_and(level >= z, z > 0))
            def _():
                z_copy(t, level, False).wait_send()

    for v in range(nz):

        @pl.when(v != z)
        def _():
            act_copy(v, 0).wait_send()
            part_copy(v).wait_send()

        act_copy(v, 1).wait_send()


def embed(hidden, lengths, norm_gain, up, down, pool_gain, proj, n_dp, n_fsdp):
    tok_rows, width = hidden.shape
    pass_rows = lengths.shape[0]
    nz = n_fsdp // 2
    ff_rows = down.shape[0]
    d_rows, emb = proj.shape
    cols = 2 * d_rows
    half = nz * pass_rows
    wide = -(-ff_rows // LANES)
    chunks = nz * wide
    subs = chunks // PLANE
    relays = [len([s for s in range(subs) if s % 3 == r]) for r in range(3)]
    if up.shape[1] != 2 * chunks * LANES:
        up = jnp.pad(
            up.reshape(up.shape[0], n_fsdp, ff_rows), ((0, 0), (0, 0), (0, wide * LANES - ff_rows))
        ).reshape(up.shape[0], n_fsdp * wide * LANES)
    bf = jnp.bfloat16
    f32 = jnp.float32
    dma = pltpu.SemaphoreType.DMA
    vmem = pl.BlockSpec(memory_space=pltpu.VMEM)
    hbm = pl.BlockSpec(memory_space=pl.ANY)
    smem = pl.BlockSpec(memory_space=pltpu.SMEM)
    in_z = (subs + relays[0]) * nz
    return pl.pallas_call(
        functools.partial(embed_kernel, n_dp, n_fsdp, width),
        out_shape=(
            jax.ShapeDtypeStruct((pass_rows, emb), f32),
            jax.ShapeDtypeStruct((n_dp, 2, nz, pass_rows, emb), bf),
        ),
        in_specs=[hbm, smem, vmem, hbm, hbm, vmem, hbm],
        out_specs=(vmem, vmem),
        scratch_shapes=[
            pltpu.VMEM((tok_rows, width), bf),
            pltpu.VMEM((2, tok_rows, width), bf),
            pltpu.VMEM((chunks, width, LANES), bf),
            pltpu.VMEM((2, ff_rows, width), bf),
            pltpu.VMEM((2, d_rows, emb), bf),
            pltpu.VMEM((nz, 2, pass_rows, wide * LANES), bf),
            pltpu.VMEM((2, nz, pass_rows, wide * LANES), bf),
            pltpu.VMEM((half, width), f32),
            pltpu.VMEM((nz, half, cols), bf),
            pltpu.VMEM((nz, half, cols), bf),
            pltpu.VMEM((nz, pass_rows, emb + LANES), bf),
            pltpu.VMEM((nz - 1, pass_rows, emb + LANES), bf),
            pltpu.VMEM((1, cols), f32),
            dma,
            dma((chunks,)),
            dma((chunks,)),
            dma((chunks,)),
            dma((in_z,)),
            dma((in_z,)),
            dma((in_z,)),
            dma(((subs + relays[1]) * nz,)),
            dma(((subs + relays[1]) * nz,)),
            dma(((subs + relays[2]) * nz,)),
            dma(((subs + relays[2]) * nz,)),
            dma,
            dma,
            dma((2,)),
            dma((2,)),
            dma((2,)),
            dma((n_fsdp,)),
            dma((n_fsdp,)),
        ]
        + [dma((nz,))] * 2
        + [dma((nz - 1,))] * 4
        + [dma((n_dp - 1,))] * 2
        + [dma((n_dp,))] * 2,
        compiler_params=pltpu.CompilerParams(
            collective_id=0, has_side_effects=True, vmem_limit_bytes=48 * 1024 * 1024
        ),
        name="embed",
    )(hidden, lengths, norm_gain, up, down, pool_gain, proj)


def route_kernel(n_dp, out_ref, in_ref, ssem, rsem):
    i = lax.axis_index("dp")
    j = lax.axis_index("fsdp")
    planes = [(i + e) % n_dp for e in range(1, n_dp)]
    pl.semaphore_wait(meet([(p, j) for p in planes]), len(planes))
    copies = []
    for e, p in enumerate(planes):
        copy = remote(out_ref.at[p], in_ref.at[i], ssem.at[e], rsem.at[e], (p, j))
        copy.start()
        copies.append(copy)
    in_ref[i] = out_ref[i]
    for copy in copies:
        copy.wait()


def route(outgoing, n_dp):
    vmem = pl.BlockSpec(memory_space=pltpu.VMEM)
    return pl.pallas_call(
        functools.partial(route_kernel, n_dp),
        out_shape=jax.ShapeDtypeStruct(outgoing.shape, outgoing.dtype),
        in_specs=[vmem],
        out_specs=vmem,
        scratch_shapes=[pltpu.SemaphoreType.DMA((n_dp - 1,))] * 2,
        compiler_params=pltpu.CompilerParams(collective_id=2, has_side_effects=True),
        name="route",
    )(outgoing)


def on_device(hidden, lengths, norm_gain, up_weight, down_weight, pool_gain, proj_weight, owners):
    pass_rows = lengths.shape[0]
    n_fsdp = lax.axis_size("fsdp")
    n_dp = lax.axis_size("dp")
    emb = proj_weight.shape[1]
    group = n_fsdp * pass_rows
    embedded, everyone = embed(
        hidden, lengths, norm_gain, up_weight, down_weight, pool_gain, proj_weight, n_dp, n_fsdp
    )
    everyone = everyone.reshape(n_dp * group, emb)
    total_rows = float(everyone.shape[0])
    average = jnp.sum(everyone.astype(jnp.float32), axis=0) / total_rows
    eye = jnp.eye(emb, dtype=jnp.float32)
    covariance = (
        jnp.dot(everyone.T, everyone, preferred_element_type=jnp.float32) / total_rows
        - average[:, None] * average[None, :]
        + RIDGE_TERM * eye
    )
    magnitude = jnp.sqrt(jnp.sum(covariance * covariance))
    s1 = eye - (2.0 / magnitude) * covariance
    s2 = fdot(s1, s1)
    s4 = fdot(s2, s2)
    rows = (embedded - average) * (2.0 / magnitude)
    rows = rows + fdot(rows, s1)
    rows = rows + fdot(rows, s2)
    rows = rows + fdot(rows, s4)
    rows = rows + fdot(fdot(rows, s4), s4)
    whitened = rows.astype(jnp.bfloat16)
    capacity = 2 * pass_rows // n_dp
    target_owner = owners[:, 0]
    position = lax.broadcasted_iota(jnp.int32, (pass_rows, pass_rows), 0)
    previous = lax.broadcasted_iota(jnp.int32, (pass_rows, pass_rows), 1)
    earlier = (target_owner[:, None] == target_owner[None, :]) & (previous < position)
    target = target_owner * capacity + jnp.sum(earlier.astype(jnp.int32), axis=1)
    slot_index = lax.broadcasted_iota(jnp.int32, (n_dp * capacity, pass_rows), 0)
    selector = (slot_index == target[None, :]).astype(jnp.bfloat16)
    outgoing = jnp.dot(selector, whitened, preferred_element_type=jnp.float32).astype(jnp.bfloat16)
    owned = route(outgoing.reshape(n_dp, capacity, emb), n_dp)
    return owned.reshape(n_dp * capacity, emb)


def solution(mesh):
    placed = (
        P(("dp", "fsdp"), None),
        P(("dp", "fsdp")),
        P(),
        P("fsdp", None),
        P("fsdp", None),
        P(),
        P("fsdp", None),
        P(("dp", "fsdp"), None),
    )
    return jax.shard_map(
        on_device, mesh=mesh, in_specs=placed, out_specs=P(("dp", "fsdp"), None), check_vma=False
    )
```

```python
import functools

import jax
import jax.numpy as jnp
from jax import lax
from jax.experimental import pallas as pl
from jax.experimental.pallas import tpu as pltpu
from jax.sharding import PartitionSpec as P

RIDGE_TERM = 1.0
EPSILON = 1e-06
MESH = pl.DeviceIdType.MESH
PLANE = 4
LANES = 128
LAG = 4
REACH = 2
HOPS = (1, -1, 2, -2)


def remote(src, dst, send, recv, device):
    return pltpu.make_async_remote_copy(
        src_ref=src, dst_ref=dst, send_sem=send, recv_sem=recv, device_id=device, device_id_type=MESH
    )


def meet(devices):
    barrier = pltpu.get_barrier_semaphore()
    for device in devices:
        pl.semaphore_signal(barrier, inc=1, device_id=device, device_id_type=MESH)
    return barrier


def gelu(v):
    return 0.5 * v * (1.0 + jnp.tanh(0.7978845608028654 * (v + 0.044715 * (v * v * v))))


def nearest(nz):
    return [sorted((l for l in range(nz) if l != v), key=lambda l: (abs(l - v), l)) for v in range(nz)]


def pick(index, table):
    value = table[0]
    for v in range(1, len(table)):
        value = jnp.where(index == v, table[v], value)
    return value


def embed_kernel(
    n_dp, n_fsdp, width,
    hid_ref, len_ref, ngain_ref, up_ref, down_ref, pgain_ref, proj_ref, own_ref,
    out_ref,
    hid, nrm, upb, down2, pj, sa, ra, hs, s2, r2, s3, r3, gsel, every, u1, outgoing,
    h_sem, lo_sem, ps, pr, zu, zd, zu2, zd2, zr, xs, xr, ys, yr, ns, nr,
    dl, dns, dnr, as_, ar, s2s, r2s, s3s, r3s, es, er, fs, fr, gs, gr, qs, qr, ts, tr,
):
    i = lax.axis_index("dp")
    j = lax.axis_index("fsdp")
    nz = n_fsdp // 2
    z = j // 2
    c = j % 2
    q = i % PLANE
    base = i - q
    rows = up_ref.shape[0]
    level_rows = 2 * rows
    chunks = upb.shape[0]
    subs = chunks // PLANE
    wide = chunks // nz
    per = subs // wide
    pass_rows, seq = hs.shape[0] // nz, hid.shape[0] // (hs.shape[0] // nz)
    half = nz * pass_rows
    ff_rows = down_ref.shape[0]
    cols = s2.shape[2]
    emb = proj_ref.shape[1]
    qx = q + 1 - 2 * (q % 2)
    qy = q + 2 - 4 * (q // 2)
    qd = 3 - q
    partner = (i, z * 2 + 1 - c)
    near_x = (base + qx, j)
    near_y = (base + qy, j)
    peers = [(j + d) % n_fsdp for d in range(1, n_fsdp)]
    levels = [(z + d) % nz for d in range(1, nz)]
    planes = [(i + e) % n_dp for e in range(1, n_dp)]
    order = nearest(nz)
    near = [pick(z, [order[v][s] for v in range(nz)]) for s in range(nz - 1)]
    pending = []

    def along(level):
        return (i, level * 2 + c)

    def send(src, dst, ssem, rsem, device):
        copy = remote(src, dst, ssem, rsem, device)
        copy.start()
        pending.append(copy)
        return copy

    barrier = meet([(i, p) for p in peers] + [(p, j) for p in planes])

    own_k = [q * subs + s for s in range(subs)]
    x_k = [qx * subs + s for s in range(subs)]
    y_k = [qy * subs + s for s in range(subs)]
    d_k = [qd * subs + s for s in range(subs)]
    by_x = [s for s in range(subs) if s % 3 == 0]
    by_y = [s for s in range(subs) if s % 3 == 1]
    by_z = [s for s in range(subs) if s % 3 == 2]
    z_k = own_k + [d_k[s] for s in by_z]
    first = z_k + x_k + y_k + [d_k[s] for s in by_x + by_y]

    def source(core, k):
        at = ((k // wide * 2 + core) * wide + k % wide) * LANES
        return up_ref.at[:, pl.ds(pl.multiple_of(at, LANES), LANES)]

    def mine(k):
        return upb.at[k, pl.ds(pl.multiple_of(j * rows, rows), rows), :]

    def piece(k, level):
        return upb.at[k, pl.ds(pl.multiple_of(level * level_rows, level_rows), level_rows), :]

    local = []
    for n, k in enumerate(first):
        copy = pltpu.make_async_copy(source(c, k), mine(k), lo_sem.at[n])
        copy.start()
        local.append(copy)
    hid_copy = pltpu.make_async_copy(hid_ref, hid, h_sem)
    hid_copy.start()
    pl.semaphore_wait(barrier, len(peers) + len(planes))
    swapped = []

    def swap(n):
        swapped.append(send(source(1 - c, first[n]), mine(first[n]), ps.at[n], pr.at[n], partner))

    swap(0)
    swap(1)

    def z_copy(t, level, hop):
        part = piece(z_k[t], level)
        sems = {1: zu, -1: zd, 2: zu2, -2: zd2}[hop]
        return remote(part, part, sems.at[t * nz + level], zr.at[t * nz + level], along(z + hop))

    def reaches(hop):
        return z + hop < nz if hop > 0 else z + hop >= 0

    def relays(level, hop):
        beyond = level <= z - REACH if hop > 0 else level >= z + REACH
        return jnp.logical_and(beyond, reaches(hop))

    def start_z(t):
        local[t].wait()
        swapped[t].wait_recv()
        for hop in HOPS:

            @pl.when(reaches(hop))
            def _():
                z_copy(t, z, hop).start()

    start_z(0)
    start_z(1)
    for n in range(2, chunks):
        swap(n)
    down_copy = pltpu.make_async_copy(down_ref, down2.at[c], dl.at[0])
    down_copy.start()
    proj_copy = pltpu.make_async_copy(proj_ref, pj.at[c], dl.at[1])
    proj_copy.start()
    hid_copy.wait()
    gain = ngain_ref[...].reshape(1, width)
    hs[...] = jnp.zeros_like(hs)

    def norm_block(p, carry):
        at = pl.ds(pl.multiple_of(p * seq, seq), seq)
        x = hid[at, :].astype(jnp.float32)
        keep = lax.broadcasted_iota(jnp.int32, (seq, 1), 0) < len_ref[p]
        scale = lax.rsqrt(jnp.sum(x * x, axis=1, keepdims=True) / width + EPSILON)
        scale = jnp.where(keep, scale, 0.0)
        nrm[c, at, :] = (x * scale * gain).astype(nrm.dtype)
        total = jnp.sum(jnp.where(keep, x, 0.0), axis=0, keepdims=True)
        hs[pl.ds(z * pass_rows + p, 1), :] = total
        return carry

    lax.fori_loop(0, pass_rows, norm_block, 0)
    nrm_copy = send(nrm.at[c], nrm.at[c], ns, nr, partner)
    down_swap = send(down_ref, down2.at[c], dns.at[0], dnr.at[0], partner)
    proj_swap = send(proj_ref, pj.at[c], dns.at[1], dnr.at[1], partner)
    pgain = pgain_ref[...].reshape(1, width)
    picked = pgain[:, :cols]
    for v in range(1, nz):
        picked = jnp.where(z == v, pgain[:, v * cols : (v + 1) * cols], picked)
    gsel[...] = picked

    def along_x(slot, k, level):
        part = piece(k, level)
        return send(part, part, xs.at[slot * nz + level], xr.at[slot * nz + level], near_x)

    def along_y(slot, k, level):
        part = piece(k, level)
        return send(part, part, ys.at[slot * nz + level], yr.at[slot * nz + level], near_y)

    done = []
    x_sent, y_sent, x_relay, y_relay = {}, {}, {}, {}

    def z_step(t, s):
        level = near[s]
        z_copy(t, level, 1).wait_recv()
        for hop in (1, -1):

            @pl.when(relays(level, hop))
            def _():
                z_copy(t, level, hop).start()

        if t < subs:
            x_sent[t, s] = along_x(t, own_k[t], level)
            y_sent[t, s] = along_y(t, own_k[t], level)

    def xy_step(t, s):
        level = near[s]
        x_sent[t, s].wait_recv()
        y_sent[t, s].wait_recv()
        if t in by_x:
            x_relay[t, s] = along_x(subs + by_x.index(t), y_k[t], level)
        if t in by_y:
            y_relay[t, s] = along_y(subs + by_y.index(t), x_k[t], level)

    def compute(quarter, s):
        k = quarter * subs + s
        v = quarter * per + s // wide
        o = s % wide

        def slot(core, carry):
            pre = jnp.dot(nrm[core], upb[k], preferred_element_type=jnp.float32)
            total = jnp.sum(gelu(pre).reshape(pass_rows, seq, LANES), axis=1)
            sa[v, core, :, o * LANES : (o + 1) * LANES] = total.astype(sa.dtype)
            return carry

        lax.fori_loop(0, 2, slot, 0)

    def act_copy(v, e):
        core = c if e == 0 else 1 - c
        return remote(
            sa.at[v, core], ra.at[c, z], as_.at[v * 2 + e], ar.at[c * nz + z], (i, v * 2 + core)
        )

    def send_acts(quarter):
        for b in range(per):
            v = quarter * per + b

            @pl.when(v == z)
            def _():
                ra[c, z] = sa[v, c]

            @pl.when(v != z)
            def _():
                act_copy(v, 0).start()

            act_copy(v, 1).start()

    ready = []
    left = {}

    def run_one():
        if ready:
            name, quarter, s = ready.pop(0)
            compute(quarter, s)
            left[name] = left.get(name, subs) - 1
            if left[name] == 0:
                send_acts(quarter)

    z_steps = [(t, s) for t in range(len(z_k)) for s in range(nz - 1)]
    xy_steps = [(t, s) for t in range(subs) for s in range(nz - 1)]
    started = 2
    waited_n = 0
    for n in range(max(len(z_steps), len(xy_steps) + LAG)):
        if n < len(z_steps):
            t, s = z_steps[n]
            z_step(t, s)
            if s == nz - 2:
                if started < len(z_k):
                    start_z(started)
                    started += 1
                if t < subs:
                    ready.append(("own", q, t))
                else:
                    ready.append(("diag", qd, by_z[t - subs]))
        if 0 <= n - LAG < len(xy_steps):
            t, s = xy_steps[n - LAG]
            xy_step(t, s)
            if s == nz - 2:
                if t == 0:
                    for copy, arrived in list(zip(local, swapped))[len(z_k) :]:
                        copy.wait()
                        arrived.wait_recv()
                ready.append(("x", qx, t))
                ready.append(("y", qy, t))
        if ready and waited_n == 0:
            nrm_copy.wait_recv()
            waited_n = 1
        run_one()
    while ready:
        run_one()
    for t in by_x:
        for s in range(nz - 1):
            x_relay[t, s].wait_recv()
        ready.append(("diag", qd, t))
        run_one()
    for t in by_y:
        for s in range(nz - 1):
            y_relay[t, s].wait_recv()
        ready.append(("diag", qd, t))
        run_one()

    down_copy.wait()
    down_swap.wait_recv()
    for v in range(nz):
        for e in range(2):
            core = c if e == 0 else 1 - c
            arrival = remote(
                sa.at[v, core], ra.at[core, v], as_.at[v * 2 + e], ar.at[core * nz + v], partner
            )
            if e == 0:

                @pl.when(v != z)
                def _():
                    arrival.wait_recv()

            else:
                arrival.wait_recv()

    acts = [ra[core].reshape(half, wide * LANES)[:, :ff_rows] for core in range(2)]

    def part_copy(v):
        return remote(s2.at[v], r2.at[z], s2s.at[v], r2s.at[z], along(v))

    for v in range(nz):
        at = slice(v * cols, (v + 1) * cols)
        part = hs[:, at]
        for core in range(2):
            part = part + jnp.dot(acts[core], down2[core, :, at], preferred_element_type=jnp.float32)
        s2[v] = part.astype(s2.dtype)

        @pl.when(v != z)
        def _():
            part_copy(v).start()

    proj_copy.wait()
    proj_swap.wait_recv()
    pooled = s2[z].astype(jnp.float32)
    for v in levels:
        remote(s2.at[v], r2.at[v], s2s.at[v], r2s.at[v], along(v)).wait_recv()
        pooled = pooled + r2[v].astype(jnp.float32)
    squares = jnp.sum(pooled * pooled, axis=1, keepdims=True)
    scaled = (pooled * gsel[...]).astype(proj_ref.dtype)
    part = jnp.dot(scaled, pj[...].reshape(cols, emb), preferred_element_type=jnp.float32)
    s3[:, :, :emb] = part.astype(s3.dtype).reshape(nz, pass_rows, emb)
    spread = jnp.broadcast_to(squares, (half, LANES))
    high = spread.astype(s3.dtype)
    low = (spread - high.astype(jnp.float32)).astype(s3.dtype)
    lane = lax.broadcasted_iota(jnp.int32, (half, LANES), 1)
    both = jnp.where(lane < LANES // 2, high.astype(jnp.float32), low.astype(jnp.float32))
    s3[:, :, emb:] = both.astype(s3.dtype).reshape(nz, pass_rows, LANES)
    third = [send(s3.at[v], r3.at[d], s3s.at[d], r3s.at[d], along(v)) for d, v in enumerate(levels)]
    total = s3[z].astype(jnp.float32)
    row = lax.broadcasted_iota(jnp.int32, (pass_rows, LANES), 0)
    counts = jnp.zeros((pass_rows, LANES), jnp.float32)
    for p in range(pass_rows):
        counts = jnp.where(row == p, len_ref[p].astype(jnp.float32), counts)
    counts = counts[:, :1]
    for d, copy in enumerate(third):
        copy.wait_recv()
        total = total + r3[d].astype(jnp.float32)
    norm = (total[:, emb : emb + 1] + total[:, emb + LANES // 2 : emb + LANES // 2 + 1]) / width
    embedded = total[:, :emb] * lax.rsqrt(norm + EPSILON * (counts * counts))
    every[i, c, z] = embedded.astype(every.dtype)

    def to_level(v):
        part = every.at[i, c, z]
        return remote(part, part, es.at[v], er.at[z], along(v))

    def from_level(v):
        part = every.at[i, c, v]
        return remote(part, part, es.at[v], er.at[v], along(v))

    for v in levels:
        copy = to_level(v)
        copy.start()
        pending.append(copy)
    last = []

    def to_partner(part, n):
        last.append(send(part, part, qs.at[n], qr.at[n], partner))

    if n_dp == PLANE:
        seen = [z] + near
        across = {}

        def pass_on(plane, e, kind, slot):
            part = every.at[plane, c, seen[e]]
            sems = (fs, fr, near_x) if kind == "x" else (gs, gr, near_y)
            at = slot * nz + seen[e]
            across[kind, slot, e] = send(part, part, sems[0].at[at], sems[1].at[at], sems[2])

        for e in range(nz):
            if e > 0:
                from_level(seen[e]).wait_recv()
            pass_on(i, e, "x", 0)
            pass_on(i, e, "y", 0)
        to_partner(every.at[i, c], 0)
        for e in range(nz):
            across["x", 0, e].wait_recv()
            across["y", 0, e].wait_recv()
            if e % 2 == 0:
                pass_on(qx, e, "y", 1)
            else:
                pass_on(qy, e, "x", 1)
        to_partner(every.at[qx, c], 1)
        to_partner(every.at[qy, c], 2)
        for e in range(nz):
            across["y" if e % 2 == 0 else "x", 1, e].wait_recv()
        to_partner(every.at[qd, c], 3)
    else:
        for v in levels:
            from_level(v).wait_recv()
        part = every.at[i, c]
        fifth = [send(part, part, fs.at[e], fr.at[e], (p, j)) for e, p in enumerate(planes)]
        to_partner(part, 0)
        for e, copy in enumerate(fifth):
            copy.wait_recv()
            to_partner(every.at[(i + n_dp - e - 1) % n_dp, c], e + 1)

    capacity = outgoing.shape[1]
    targets = []
    for p in range(pass_rows):
        earlier = [(own_ref[p] == own_ref[o]).astype(jnp.int32) for o in range(p)]
        targets.append(own_ref[p] * capacity + sum(earlier))
    slot_at = lax.broadcasted_iota(jnp.int32, (n_dp * capacity, pass_rows), 0)
    pass_at = lax.broadcasted_iota(jnp.int32, (n_dp * capacity, pass_rows), 1)
    wanted = jnp.full((n_dp * capacity, pass_rows), -1, jnp.int32)
    for p in range(pass_rows):
        wanted = jnp.where(pass_at == p, targets[p], wanted)
    selector = (slot_at == wanted).astype(jnp.float32).astype(jnp.bfloat16)

    for copy in last:
        copy.wait_recv()

    bf = jnp.bfloat16
    n_rows = n_dp * n_fsdp * pass_rows
    mark = ((i * 2 + c) * nz + z) * pass_rows
    rounded = every[i, c, z].astype(jnp.float32)

    def mul(a, b):
        return jnp.dot(a.astype(bf), b, preferred_element_type=jnp.float32)

    def mul2(a, b):
        high = a.astype(bf)
        return mul(high, b) + mul(a - high.astype(jnp.float32), b)

    def eye(n):
        at = lax.broadcasted_iota(jnp.int32, (n, n), 0)
        return (at == lax.broadcasted_iota(jnp.int32, (n, n), 1)).astype(jnp.float32)

    if n_rows < emb:
        rows_all = every[...].reshape(n_rows, emb)
        average = jnp.sum(rows_all.astype(jnp.float32), axis=0, keepdims=True) / n_rows
        gram = lax.dot_general(
            rows_all, rows_all, (((1,), (1,)), ((), ())), preferred_element_type=jnp.float32
        ) / n_rows
        by_col = jnp.mean(gram, axis=0, keepdims=True)
        by_row = jnp.mean(gram, axis=1, keepdims=True)
        ridged = gram - by_col - by_row + jnp.mean(by_col) + RIDGE_TERM * eye(n_rows)
        squared = jnp.sum(ridged * ridged) + RIDGE_TERM * RIDGE_TERM * (emb - n_rows)
    else:
        def add(b, carry):
            part = every[b // 2, b % 2].reshape(half, emb)
            moment = lax.dot_general(
                part, part, (((0,), (0,)), ((), ())), preferred_element_type=jnp.float32
            )
            u1[...] += moment
            return carry + jnp.sum(part.astype(jnp.float32), axis=0, keepdims=True)

        u1[...] = jnp.zeros_like(u1)
        average = lax.fori_loop(0, n_dp * 2, add, jnp.zeros((1, emb), jnp.float32)) / n_rows
        tall = jnp.transpose(jnp.broadcast_to(average, (emb, emb)))
        ridged = u1[...] / n_rows - tall * average + RIDGE_TERM * eye(emb)
        squared = jnp.sum(ridged * ridged)
    doubled = 2.0 * lax.rsqrt(squared)
    t1 = ridged * doubled
    u1[...] = t1
    t1b = t1.astype(bf)
    t2 = 2.0 * t1 - mul(t1, t1b)
    t2b = t2.astype(bf)
    t4 = 2.0 * t2 - mul(t2, t2b)
    t4b = t4.astype(bf)
    if n_rows < emb:
        lane = lax.broadcasted_iota(jnp.int32, (pass_rows, n_rows), 1)
        here = (lane == mark + lax.broadcasted_iota(jnp.int32, (pass_rows, n_rows), 0)).astype(jnp.float32)
        mix = 2.0 * here - u1[pl.ds(pl.multiple_of(mark, pass_rows), pass_rows), :]
        times = mul
    else:
        mix = embedded - average
        mix = 2.0 * mix - mul2(mix, t1b)
        times = mul2
    mix = 2.0 * mix - times(mix, t2b)
    mix = 2.0 * mix - times(mix, t4b)
    rest = mix - times(mix, t4b)
    mix = mix + (rest - times(rest, t4b))
    if n_rows < emb:
        mixed = mul2(mix, rows_all) - jnp.sum(mix, axis=1, keepdims=True) * average
        mix = mixed + jnp.sum(mix * here, axis=1, keepdims=True) * (embedded - rounded)
    whitened = (mix * doubled).astype(bf)
    routed = jnp.dot(selector, whitened, preferred_element_type=jnp.float32)
    for p in range(n_dp):
        outgoing[p] = routed[p * capacity : (p + 1) * capacity].astype(bf)
    sixth = [send(outgoing.at[p], out_ref.at[i], ts.at[e], tr.at[e], (p, j)) for e, p in enumerate(planes)]
    out_ref[i] = outgoing[i]
    for copy in sixth:
        copy.wait_recv()

    for copy in pending:
        copy.wait_send()
    for t in range(len(z_k)):
        for hop in HOPS:

            @pl.when(reaches(hop))
            def _():
                z_copy(t, z, hop).wait_send()

        for level in range(nz):
            for hop in (1, -1):

                @pl.when(relays(level, hop))
                def _():
                    z_copy(t, level, hop).wait_send()

    for v in range(nz):

        @pl.when(v != z)
        def _():
            act_copy(v, 0).wait_send()
            part_copy(v).wait_send()

        act_copy(v, 1).wait_send()


def encode(hidden, lengths, norm_gain, up, down, pool_gain, proj, owners, n_dp, n_fsdp):
    tok_rows, width = hidden.shape
    pass_rows = lengths.shape[0]
    nz = n_fsdp // 2
    ff_rows = down.shape[0]
    d_rows, emb = proj.shape
    cols = 2 * d_rows
    half = nz * pass_rows
    wide = -(-ff_rows // LANES)
    chunks = nz * wide
    subs = chunks // PLANE
    legs = [len([s for s in range(subs) if s % 3 == r]) for r in range(3)]
    if up.shape[1] != 2 * chunks * LANES:
        up = jnp.pad(
            up.reshape(up.shape[0], n_fsdp, ff_rows), ((0, 0), (0, 0), (0, wide * LANES - ff_rows))
        ).reshape(up.shape[0], n_fsdp * wide * LANES)
    capacity = 2 * pass_rows // n_dp
    side = min(emb, n_dp * n_fsdp * pass_rows)
    bf = jnp.bfloat16
    f32 = jnp.float32
    dma = pltpu.SemaphoreType.DMA
    vmem = pl.BlockSpec(memory_space=pltpu.VMEM)
    hbm = pl.BlockSpec(memory_space=pl.ANY)
    smem = pl.BlockSpec(memory_space=pltpu.SMEM)
    in_z = (subs + legs[2]) * nz
    return pl.pallas_call(
        functools.partial(embed_kernel, n_dp, n_fsdp, width),
        out_shape=jax.ShapeDtypeStruct((n_dp, capacity, emb), bf),
        in_specs=[hbm, smem, vmem, hbm, hbm, vmem, hbm, smem],
        out_specs=vmem,
        scratch_shapes=[
            pltpu.VMEM((tok_rows, width), bf),
            pltpu.VMEM((2, tok_rows, width), bf),
            pltpu.VMEM((chunks, width, LANES), bf),
            pltpu.VMEM((2, ff_rows, width), bf),
            pltpu.VMEM((2, d_rows, emb), bf),
            pltpu.VMEM((nz, 2, pass_rows, wide * LANES), bf),
            pltpu.VMEM((2, nz, pass_rows, wide * LANES), bf),
            pltpu.VMEM((half, width), f32),
            pltpu.VMEM((nz, half, cols), bf),
            pltpu.VMEM((nz, half, cols), bf),
            pltpu.VMEM((nz, pass_rows, emb + LANES), bf),
            pltpu.VMEM((nz - 1, pass_rows, emb + LANES), bf),
            pltpu.VMEM((1, cols), f32),
            pltpu.VMEM((n_dp, 2, nz, pass_rows, emb), bf),
            pltpu.VMEM((side, side), f32),
            pltpu.VMEM((n_dp, capacity, emb), bf),
            dma,
            dma((chunks,)),
            dma((chunks,)),
            dma((chunks,)),
            dma((in_z,)),
            dma((in_z,)),
            dma((in_z,)),
            dma((in_z,)),
            dma((in_z,)),
            dma(((subs + legs[0]) * nz,)),
            dma(((subs + legs[0]) * nz,)),
            dma(((subs + legs[1]) * nz,)),
            dma(((subs + legs[1]) * nz,)),
            dma,
            dma,
            dma((2,)),
            dma((2,)),
            dma((2,)),
            dma((n_fsdp,)),
            dma((n_fsdp,)),
        ]
        + [dma((nz,))] * 2
        + [dma((nz - 1,))] * 2
        + [dma((nz,))] * 2
        + [dma((max(2 * nz, n_dp),))] * 4
        + [dma((n_dp,))] * 2
        + [dma((n_dp - 1,))] * 2,
        compiler_params=pltpu.CompilerParams(
            collective_id=0, has_side_effects=True, vmem_limit_bytes=60 * 1024 * 1024
        ),
        name="embed",
    )(hidden, lengths, norm_gain, up, down, pool_gain, proj, owners)


def on_device(hidden, lengths, norm_gain, up_weight, down_weight, pool_gain, proj_weight, owners):
    n_dp, n_fsdp = lax.axis_size("dp"), lax.axis_size("fsdp")
    owned = encode(
        hidden, lengths, norm_gain, up_weight, down_weight, pool_gain, proj_weight,
        owners.reshape(-1), n_dp, n_fsdp,
    )
    return owned.reshape(-1, owned.shape[2])


def solution(mesh):
    placed = (
        P(("dp", "fsdp"), None),
        P(("dp", "fsdp")),
        P(),
        P("fsdp", None),
        P("fsdp", None),
        P(),
        P("fsdp", None),
        P(("dp", "fsdp"), None),
    )
    return jax.shard_map(
        on_device, mesh=mesh, in_specs=placed, out_specs=P(("dp", "fsdp"), None), check_vma=False
    )
```

```python
import functools

import jax
import jax.numpy as jnp
from jax import lax
from jax.experimental import pallas as pl
from jax.experimental.pallas import tpu as pltpu
from jax.sharding import PartitionSpec as P

RIDGE_TERM = 1.0
EPSILON = 1e-06
MESH = pl.DeviceIdType.MESH
PLANE = 4
LANES = 128
LAG = 4
RELAY_LAG = 4
REACH = 2
HOPS = (1, -1, 2, -2)


def remote(src, dst, send, recv, device):
    return pltpu.make_async_remote_copy(
        src_ref=src, dst_ref=dst, send_sem=send, recv_sem=recv, device_id=device, device_id_type=MESH
    )


def meet(devices):
    barrier = pltpu.get_barrier_semaphore()
    for device in devices:
        pl.semaphore_signal(barrier, inc=1, device_id=device, device_id_type=MESH)
    return barrier


def gelu(v):
    return 0.5 * v * (1.0 + jnp.tanh(0.7978845608028654 * (v + 0.044715 * (v * v * v))))


def nearest(nz):
    return [sorted((l for l in range(nz) if l != v), key=lambda l: (abs(l - v), l)) for v in range(nz)]


def pick(index, table):
    value = table[0]
    for v in range(1, len(table)):
        value = jnp.where(index == v, table[v], value)
    return value


def embed_kernel(
    n_dp, n_fsdp, width,
    hid_ref, len_ref, ngain_ref, up_ref, down_ref, pgain_ref, proj_ref, own_ref,
    out_ref,
    hid, nrm, upb, down2, pj, sa, ra, hs, s2, r2, s3, r3, gsel, every, u1, outgoing, choose, sizes,
    h_sem, lo_sem, ps, pr, zu, zd, zo, zr, xs, xr, ys, yr, ns, nr,
    dl, dns, dnr, as_, ar, s2s, r2s, s3s, r3s, es, er, fs, fr, qs, qr, ts, tr,
):
    i = lax.axis_index("dp")
    j = lax.axis_index("fsdp")
    nz = n_fsdp // 2
    z = j // 2
    c = j % 2
    q = i % PLANE
    base = i - q
    rows = up_ref.shape[0]
    level_rows = 2 * rows
    chunks = upb.shape[0]
    subs = chunks // PLANE
    wide = chunks // nz
    per = subs // wide
    pass_rows, seq = hs.shape[0] // nz, hid.shape[0] // (hs.shape[0] // nz)
    half = nz * pass_rows
    ff_rows = down_ref.shape[0]
    cols = s2.shape[2]
    emb = proj_ref.shape[1]
    qx = q + 1 - 2 * (q % 2)
    qy = q + 2 - 4 * (q // 2)
    qd = 3 - q
    partner = (i, z * 2 + 1 - c)
    near_x = (base + qx, j)
    near_y = (base + qy, j)
    peers = [(j + d) % n_fsdp for d in range(1, n_fsdp)]
    levels = [(z + d) % nz for d in range(1, nz)]
    planes = [(i + e) % n_dp for e in range(1, n_dp)]
    order = nearest(nz)
    near = [pick(z, [order[v][s] for v in range(nz)]) for s in range(nz - 1)]
    pending = []

    def along(level):
        return (i, level * 2 + c)

    def send(src, dst, ssem, rsem, device):
        copy = remote(src, dst, ssem, rsem, device)
        copy.start()
        pending.append(copy)
        return copy

    barrier = meet([(i, p) for p in peers] + [(p, j) for p in planes])

    own_k = [q * subs + s for s in range(subs)]
    x_k = [qx * subs + s for s in range(subs)]
    y_k = [qy * subs + s for s in range(subs)]
    d_k = [qd * subs + s for s in range(subs)]
    by_x = [s for s in range(subs) if s % 3 == 0]
    by_y = [s for s in range(subs) if s % 3 == 1]
    by_z = [s for s in range(subs) if s % 3 == 2]
    z_k = own_k + [d_k[s] for s in by_z]
    first = z_k + x_k + y_k + [d_k[s] for s in by_x + by_y]

    def source(core, k):
        at = ((k // wide * 2 + core) * wide + k % wide) * LANES
        return up_ref.at[:, pl.ds(pl.multiple_of(at, LANES), LANES)]

    def mine(k):
        return upb.at[k, pl.ds(pl.multiple_of(j * rows, rows), rows), :]

    def piece(k, level):
        return upb.at[k, pl.ds(pl.multiple_of(level * level_rows, level_rows), level_rows), :]

    local = []
    for n, k in enumerate(first):
        copy = pltpu.make_async_copy(source(c, k), mine(k), lo_sem.at[n])
        copy.start()
        local.append(copy)
    hid_copy = pltpu.make_async_copy(hid_ref, hid, h_sem)
    hid_copy.start()
    pl.semaphore_wait(barrier, len(peers) + len(planes))
    swapped = []

    def swap(n):
        swapped.append(send(source(1 - c, first[n]), mine(first[n]), ps.at[n], pr.at[n], partner))

    def z_copy(t, level, hop):
        part = piece(z_k[t], level)
        sems = zu if hop == 1 else zd
        return remote(part, part, sems.at[t * nz + level], zr.at[t * nz + level], along(z + hop))

    def reaches(hop):
        return z + hop < nz if hop > 0 else z + hop >= 0

    def relays(level, hop):
        beyond = level <= z - REACH if hop > 0 else level >= z + REACH
        return jnp.logical_and(beyond, reaches(hop))

    def first_hop(t, h, e):
        core = c if e == 0 else 1 - c
        at = (t * len(HOPS) + h) * 2 + e
        return remote(
            source(core, z_k[t]), mine(z_k[t]), zo.at[at], zr.at[t * nz + z],
            (i, (z + HOPS[h]) * 2 + core),
        )

    def start_z(t):
        for h, hop in enumerate(HOPS):

            @pl.when(reaches(hop))
            def _():
                first_hop(t, h, 0).start()
                first_hop(t, h, 1).start()

    start_z(0)
    start_z(1)
    for n in range(chunks):
        swap(n)
    down_copy = pltpu.make_async_copy(down_ref, down2.at[c], dl.at[0])
    down_copy.start()
    proj_copy = pltpu.make_async_copy(proj_ref, pj.at[c], dl.at[1])
    proj_copy.start()
    hid_copy.wait()
    gain = ngain_ref[...].reshape(1, width)
    hs[...] = jnp.zeros_like(hs)

    def norm_block(p, carry):
        at = pl.ds(pl.multiple_of(p * seq, seq), seq)
        x = hid[at, :].astype(jnp.float32)
        keep = lax.broadcasted_iota(jnp.int32, (seq, 1), 0) < len_ref[p]
        scale = lax.rsqrt(jnp.sum(x * x, axis=1, keepdims=True) / width + EPSILON)
        scale = jnp.where(keep, scale, 0.0)
        nrm[c, at, :] = (x * scale * gain).astype(nrm.dtype)
        total = jnp.sum(jnp.where(keep, x, 0.0), axis=0, keepdims=True)
        hs[pl.ds(z * pass_rows + p, 1), :] = total
        return carry

    lax.fori_loop(0, pass_rows, norm_block, 0)
    nrm_copy = send(nrm.at[c], nrm.at[c], ns, nr, partner)
    down_swap = send(down_ref, down2.at[c], dns.at[0], dnr.at[0], partner)
    proj_swap = send(proj_ref, pj.at[c], dns.at[1], dnr.at[1], partner)
    pgain = pgain_ref[...].reshape(1, width)
    picked = pgain[:, :cols]
    for v in range(1, nz):
        picked = jnp.where(z == v, pgain[:, v * cols : (v + 1) * cols], picked)
    gsel[...] = picked
    row = lax.broadcasted_iota(jnp.int32, (pass_rows, LANES), 0)
    counts = jnp.zeros((pass_rows, LANES), jnp.float32)
    for p in range(pass_rows):
        counts = jnp.where(row == p, len_ref[p].astype(jnp.float32), counts)
    sizes[...] = counts
    capacity = outgoing.shape[1]
    targets = []
    for p in range(pass_rows):
        earlier = [(own_ref[p] == own_ref[o]).astype(jnp.int32) for o in range(p)]
        targets.append(own_ref[p] * capacity + sum(earlier))
    slot_at = lax.broadcasted_iota(jnp.int32, (n_dp * capacity, pass_rows), 0)
    pass_at = lax.broadcasted_iota(jnp.int32, (n_dp * capacity, pass_rows), 1)
    wanted = jnp.full((n_dp * capacity, pass_rows), -1, jnp.int32)
    for p in range(pass_rows):
        wanted = jnp.where(pass_at == p, targets[p], wanted)
    choose[...] = (slot_at == wanted).astype(jnp.float32).astype(choose.dtype)


    def along_x(slot, k, level):
        part = piece(k, level)
        return send(part, part, xs.at[slot * nz + level], xr.at[slot * nz + level], near_x)

    def along_y(slot, k, level):
        part = piece(k, level)
        return send(part, part, ys.at[slot * nz + level], yr.at[slot * nz + level], near_y)

    done = []
    x_sent, y_sent, x_relay, y_relay = {}, {}, {}, {}

    def z_step(t, s):
        level = near[s]
        z_copy(t, level, 1).wait_recv()
        for hop in (1, -1):

            @pl.when(relays(level, hop))
            def _():
                z_copy(t, level, hop).start()

        if t < subs:
            x_sent[t, s] = along_x(t, own_k[t], level)
            y_sent[t, s] = along_y(t, own_k[t], level)

    def xy_step(t, s):
        level = near[s]
        x_sent[t, s].wait_recv()
        y_sent[t, s].wait_recv()
        if t in by_x:
            x_relay[t, s] = along_x(subs + by_x.index(t), y_k[t], level)
        if t in by_y:
            y_relay[t, s] = along_y(subs + by_y.index(t), x_k[t], level)

    def compute(items):
        def slot(core, carry):
            block = [upb[quarter * subs + s] for quarter, s in items]
            block = jnp.concatenate(block, axis=1) if len(block) > 1 else block[0]
            pre = jnp.dot(nrm[core], block, preferred_element_type=jnp.float32)
            total = jnp.sum(gelu(pre).reshape(pass_rows, seq, block.shape[1]), axis=1)
            for n, (quarter, s) in enumerate(items):
                o = s % wide
                sa[quarter * per + s // wide, core, :, o * LANES : (o + 1) * LANES] = total[
                    :, n * LANES : (n + 1) * LANES
                ].astype(sa.dtype)
            return carry

        lax.fori_loop(0, 2, slot, 0)

    def act_copy(v, e):
        core = c if e == 0 else 1 - c
        return remote(
            sa.at[v, core], ra.at[c, z], as_.at[v * 2 + e], ar.at[c * nz + z], (i, v * 2 + core)
        )

    def send_acts(quarter):
        for b in range(per):
            v = quarter * per + b

            @pl.when(v == z)
            def _():
                ra[c, z] = sa[v, c]

            @pl.when(v != z)
            def _():
                act_copy(v, 0).start()

            act_copy(v, 1).start()

    ready = []
    left = {}

    def run(least):
        if len(ready) < least:
            return
        batch = [ready.pop(0) for _ in range(min(2, len(ready)))]
        compute([(quarter, s) for _, quarter, s in batch])
        for name, quarter, _ in batch:
            left[name] = left.get(name, subs) - 1
            if left[name] == 0:
                send_acts(quarter)

    last_slot = nz - 2
    z_steps = [(t, s) for t in range(len(z_k)) for s in range(nz - 1)]
    xy_steps = [(t, s) for t in range(subs) for s in range(nz - 1)]
    ends = [("x", t, s) for t in by_x for s in range(nz - 1)] + [("y", t, s) for t in by_y for s in range(nz - 1)]
    ends = sorted(ends, key=lambda r: (r[1], r[2]))
    at_step = {r: r[1] * (nz - 1) + r[2] + LAG + RELAY_LAG for r in ends}
    started = 2
    for n in range(max([len(z_steps), len(xy_steps) + LAG] + [m + 1 for m in at_step.values()])):
        if n < len(z_steps):
            t, s = z_steps[n]
            z_step(t, s)
            if s == last_slot:
                if started < len(z_k):
                    start_z(started)
                    started += 1
                local[t].wait()
                swapped[t].wait_recv()
                ready.append(("own", q, t) if t < subs else ("diag", qd, by_z[t - subs]))
        if 0 <= n - LAG < len(xy_steps):
            t, s = xy_steps[n - LAG]
            xy_step(t, s)
            if s == last_slot:
                if t == 0:
                    for copy, arrived in list(zip(local, swapped))[len(z_k) :]:
                        copy.wait()
                        arrived.wait_recv()
                ready.append(("x", qx, t))
                ready.append(("y", qy, t))
        for kind, t, s in ends:
            if at_step[kind, t, s] == n:
                (x_relay if kind == "x" else y_relay)[t, s].wait_recv()
                if s == last_slot:
                    ready.append(("diag", qd, t))
        if n == nz - 1:
            nrm_copy.wait_recv()
        if n >= nz - 1:
            run(2)
    while ready:
        run(1)

    down_copy.wait()
    down_swap.wait_recv()
    for v in range(nz):
        for e in range(2):
            core = c if e == 0 else 1 - c
            arrival = remote(
                sa.at[v, core], ra.at[core, v], as_.at[v * 2 + e], ar.at[core * nz + v], partner
            )
            if e == 0:

                @pl.when(v != z)
                def _():
                    arrival.wait_recv()

            else:
                arrival.wait_recv()

    acts = [ra[core].reshape(half, wide * LANES)[:, :ff_rows] for core in range(2)]

    def part_copy(v):
        return remote(s2.at[v], r2.at[z], s2s.at[v], r2s.at[z], along(v))

    for v in range(nz):
        at = slice(v * cols, (v + 1) * cols)
        part = hs[:, at]
        for core in range(2):
            part = part + jnp.dot(acts[core], down2[core, :, at], preferred_element_type=jnp.float32)
        s2[v] = part.astype(s2.dtype)

        @pl.when(v != z)
        def _():
            part_copy(v).start()

    proj_copy.wait()
    proj_swap.wait_recv()
    pooled = s2[z].astype(jnp.float32)
    for v in levels:
        remote(s2.at[v], r2.at[v], s2s.at[v], r2s.at[v], along(v)).wait_recv()
        pooled = pooled + r2[v].astype(jnp.float32)
    squares = jnp.sum(pooled * pooled, axis=1, keepdims=True)
    scaled = (pooled * gsel[...]).astype(proj_ref.dtype)
    part = jnp.dot(scaled, pj[...].reshape(cols, emb), preferred_element_type=jnp.float32)
    s3[:, :, :emb] = part.astype(s3.dtype).reshape(nz, pass_rows, emb)
    spread = jnp.broadcast_to(squares, (half, LANES))
    high = spread.astype(s3.dtype)
    low = (spread - high.astype(jnp.float32)).astype(s3.dtype)
    lane = lax.broadcasted_iota(jnp.int32, (half, LANES), 1)
    both = jnp.where(lane < LANES // 2, high.astype(jnp.float32), low.astype(jnp.float32))
    s3[:, :, emb:] = both.astype(s3.dtype).reshape(nz, pass_rows, LANES)
    third = [send(s3.at[v], r3.at[d], s3s.at[d], r3s.at[d], along(v)) for d, v in enumerate(levels)]
    total = s3[z].astype(jnp.float32)
    counts = sizes[:, :1]
    for d, copy in enumerate(third):
        copy.wait_recv()
        total = total + r3[d].astype(jnp.float32)
    norm = (total[:, emb : emb + 1] + total[:, emb + LANES // 2 : emb + LANES // 2 + 1]) / width
    embedded = total[:, :emb] * lax.rsqrt(norm + EPSILON * (counts * counts))
    every[i, c, z] = embedded.astype(every.dtype)

    def to_level(v):
        part = every.at[i, c, z]
        return remote(part, part, es.at[v], er.at[z], along(v))

    def from_level(v):
        part = every.at[i, c, v]
        return remote(part, part, es.at[v], er.at[v], along(v))

    for v in levels:
        copy = to_level(v)
        copy.start()
        pending.append(copy)
    last = []

    def to_partner(part, n):
        last.append(send(part, part, qs.at[n], qr.at[n], partner))

    if n_dp == PLANE:
        seen = [z] + near
        beside = [(qx, near_x), (qy, near_y), (qd, (base + qd, j))]
        across = {}
        for e in range(nz):
            if e > 0:
                from_level(seen[e]).wait_recv()
            part = every.at[i, c, seen[e]]
            for n, (_, device) in enumerate(beside):
                at = n * nz + seen[e]
                across[n, e] = send(part, part, fs.at[at], fr.at[at], device)
        to_partner(every.at[i, c], 0)
        for n, (plane, _) in enumerate(beside):
            for e in range(nz):
                across[n, e].wait_recv()
            to_partner(every.at[plane, c], n + 1)
    else:
        for v in levels:
            from_level(v).wait_recv()
        part = every.at[i, c]
        fifth = [send(part, part, fs.at[e], fr.at[e], (p, j)) for e, p in enumerate(planes)]
        to_partner(part, 0)
        for e, copy in enumerate(fifth):
            copy.wait_recv()
            to_partner(every.at[(i + n_dp - e - 1) % n_dp, c], e + 1)

    for copy in last:
        copy.wait_recv()

    bf = jnp.bfloat16
    n_rows = n_dp * n_fsdp * pass_rows
    mark = ((i * 2 + c) * nz + z) * pass_rows
    rounded = every[i, c, z].astype(jnp.float32)

    def mul(a, b):
        return jnp.dot(a.astype(bf), b, preferred_element_type=jnp.float32)

    def mul2(a, b):
        high = a.astype(bf)
        return mul(high, b) + mul(a - high.astype(jnp.float32), b)

    def eye(n):
        at = lax.broadcasted_iota(jnp.int32, (n, n), 0)
        return (at == lax.broadcasted_iota(jnp.int32, (n, n), 1)).astype(jnp.float32)

    if n_rows < emb:
        rows_all = every[...].reshape(n_rows, emb)
        average = jnp.sum(rows_all.astype(jnp.float32), axis=0, keepdims=True) / n_rows
        gram = lax.dot_general(
            rows_all, rows_all, (((1,), (1,)), ((), ())), preferred_element_type=jnp.float32
        ) / n_rows
        by_col = jnp.mean(gram, axis=0, keepdims=True)
        by_row = jnp.mean(gram, axis=1, keepdims=True)
        ridged = gram - by_col - by_row + jnp.mean(by_col) + RIDGE_TERM * eye(n_rows)
        squared = jnp.sum(ridged * ridged) + RIDGE_TERM * RIDGE_TERM * (emb - n_rows)
    else:
        def add(b, carry):
            part = every[b // 2, b % 2].reshape(half, emb)
            moment = lax.dot_general(
                part, part, (((0,), (0,)), ((), ())), preferred_element_type=jnp.float32
            )
            u1[...] += moment
            return carry + jnp.sum(part.astype(jnp.float32), axis=0, keepdims=True)

        u1[...] = jnp.zeros_like(u1)
        average = lax.fori_loop(0, n_dp * 2, add, jnp.zeros((1, emb), jnp.float32)) / n_rows
        tall = jnp.transpose(jnp.broadcast_to(average, (emb, emb)))
        ridged = u1[...] / n_rows - tall * average + RIDGE_TERM * eye(emb)
        squared = jnp.sum(ridged * ridged)
    doubled = 2.0 * lax.rsqrt(squared)
    t1 = ridged * doubled
    u1[...] = t1
    t1b = t1.astype(bf)
    t2 = 2.0 * t1 - mul(t1, t1b)
    t2b = t2.astype(bf)
    t4 = 2.0 * t2 - mul(t2, t2b)
    t4b = t4.astype(bf)
    if n_rows < emb:
        lane = lax.broadcasted_iota(jnp.int32, (pass_rows, n_rows), 1)
        here = (lane == mark + lax.broadcasted_iota(jnp.int32, (pass_rows, n_rows), 0)).astype(jnp.float32)
        mix = 2.0 * here - u1[pl.ds(pl.multiple_of(mark, pass_rows), pass_rows), :]
        times = mul
    else:
        mix = embedded - average
        mix = 2.0 * mix - mul2(mix, t1b)
        times = mul2
    mix = 2.0 * mix - times(mix, t2b)
    mix = 2.0 * mix - times(mix, t4b)
    rest = mix - times(mix, t4b)
    mix = mix + (rest - times(rest, t4b))
    if n_rows < emb:
        mixed = mul2(mix, rows_all) - jnp.sum(mix, axis=1, keepdims=True) * average
        mix = mixed + jnp.sum(mix * here, axis=1, keepdims=True) * (embedded - rounded)
    whitened = (mix * doubled).astype(bf)
    routed = jnp.dot(choose[...], whitened, preferred_element_type=jnp.float32)
    for p in range(n_dp):
        outgoing[p] = routed[p * capacity : (p + 1) * capacity].astype(bf)
    sixth = [send(outgoing.at[p], out_ref.at[i], ts.at[e], tr.at[e], (p, j)) for e, p in enumerate(planes)]
    out_ref[i] = outgoing[i]
    for copy in sixth:
        copy.wait_recv()

    for copy in pending:
        copy.wait_send()
    for t in range(len(z_k)):
        for h, hop in enumerate(HOPS):

            @pl.when(reaches(hop))
            def _():
                first_hop(t, h, 0).wait_send()
                first_hop(t, h, 1).wait_send()

        for level in range(nz):
            for hop in (1, -1):

                @pl.when(relays(level, hop))
                def _():
                    z_copy(t, level, hop).wait_send()

    for v in range(nz):

        @pl.when(v != z)
        def _():
            act_copy(v, 0).wait_send()
            part_copy(v).wait_send()

        act_copy(v, 1).wait_send()


def encode(hidden, lengths, norm_gain, up, down, pool_gain, proj, owners, n_dp, n_fsdp):
    tok_rows, width = hidden.shape
    pass_rows = lengths.shape[0]
    nz = n_fsdp // 2
    ff_rows = down.shape[0]
    d_rows, emb = proj.shape
    cols = 2 * d_rows
    half = nz * pass_rows
    wide = -(-ff_rows // LANES)
    chunks = nz * wide
    subs = chunks // PLANE
    legs = [len([s for s in range(subs) if s % 3 == r]) for r in range(3)]
    if up.shape[1] != 2 * chunks * LANES:
        up = jnp.pad(
            up.reshape(up.shape[0], n_fsdp, ff_rows), ((0, 0), (0, 0), (0, wide * LANES - ff_rows))
        ).reshape(up.shape[0], n_fsdp * wide * LANES)
    capacity = 2 * pass_rows // n_dp
    side = min(emb, n_dp * n_fsdp * pass_rows)
    bf = jnp.bfloat16
    f32 = jnp.float32
    dma = pltpu.SemaphoreType.DMA
    vmem = pl.BlockSpec(memory_space=pltpu.VMEM)
    hbm = pl.BlockSpec(memory_space=pl.ANY)
    smem = pl.BlockSpec(memory_space=pltpu.SMEM)
    in_z = (subs + legs[2]) * nz
    return pl.pallas_call(
        functools.partial(embed_kernel, n_dp, n_fsdp, width),
        out_shape=jax.ShapeDtypeStruct((n_dp, capacity, emb), bf),
        in_specs=[hbm, smem, vmem, hbm, hbm, vmem, hbm, smem],
        out_specs=vmem,
        scratch_shapes=[
            pltpu.VMEM((tok_rows, width), bf),
            pltpu.VMEM((2, tok_rows, width), bf),
            pltpu.VMEM((chunks, width, LANES), bf),
            pltpu.VMEM((2, ff_rows, width), bf),
            pltpu.VMEM((2, d_rows, emb), bf),
            pltpu.VMEM((nz, 2, pass_rows, wide * LANES), bf),
            pltpu.VMEM((2, nz, pass_rows, wide * LANES), bf),
            pltpu.VMEM((half, width), f32),
            pltpu.VMEM((nz, half, cols), bf),
            pltpu.VMEM((nz, half, cols), bf),
            pltpu.VMEM((nz, pass_rows, emb + LANES), bf),
            pltpu.VMEM((nz - 1, pass_rows, emb + LANES), bf),
            pltpu.VMEM((1, cols), f32),
            pltpu.VMEM((n_dp, 2, nz, pass_rows, emb), bf),
            pltpu.VMEM((side, side), f32),
            pltpu.VMEM((n_dp, capacity, emb), bf),
            pltpu.VMEM((n_dp * capacity, pass_rows), bf),
            pltpu.VMEM((pass_rows, LANES), f32),
            dma,
            dma((chunks,)),
            dma((chunks,)),
            dma((chunks,)),
            dma((in_z,)),
            dma((in_z,)),
            dma((in_z // nz * len(HOPS) * 2,)),
            dma((in_z,)),
            dma(((subs + legs[0]) * nz,)),
            dma(((subs + legs[0]) * nz,)),
            dma(((subs + legs[1]) * nz,)),
            dma(((subs + legs[1]) * nz,)),
            dma,
            dma,
            dma((2,)),
            dma((2,)),
            dma((2,)),
            dma((n_fsdp,)),
            dma((n_fsdp,)),
        ]
        + [dma((nz,))] * 2
        + [dma((nz - 1,))] * 2
        + [dma((nz,))] * 2
        + [dma((max(3 * nz, n_dp),))] * 2
        + [dma((n_dp,))] * 2
        + [dma((n_dp - 1,))] * 2,
        compiler_params=pltpu.CompilerParams(
            collective_id=0, has_side_effects=True, vmem_limit_bytes=60 * 1024 * 1024
        ),
        name="embed",
    )(hidden, lengths, norm_gain, up, down, pool_gain, proj, owners)


def on_device(hidden, lengths, norm_gain, up_weight, down_weight, pool_gain, proj_weight, owners):
    n_dp, n_fsdp = lax.axis_size("dp"), lax.axis_size("fsdp")
    owned = encode(
        hidden, lengths, norm_gain, up_weight, down_weight, pool_gain, proj_weight,
        owners.reshape(-1), n_dp, n_fsdp,
    )
    return owned.reshape(-1, owned.shape[2])


def solution(mesh):
    placed = (
        P(("dp", "fsdp"), None),
        P(("dp", "fsdp")),
        P(),
        P("fsdp", None),
        P("fsdp", None),
        P(),
        P("fsdp", None),
        P(("dp", "fsdp"), None),
    )
    return jax.shard_map(
        on_device, mesh=mesh, in_specs=placed, out_specs=P(("dp", "fsdp"), None), check_vma=False
    )
```

```python
import functools

import jax
import jax.numpy as jnp
from jax import lax
from jax.experimental import pallas as pl
from jax.experimental.pallas import tpu as pltpu
from jax.sharding import PartitionSpec as P

RIDGE_TERM = 1.0
EPSILON = 1e-06
MESH = pl.DeviceIdType.MESH
PLANE = 4
LANES = 128
LAG = 4
RELAY_LAG = 4
REACH = 2
HOPS = (1, -1, 2, -2)


def remote(src, dst, send, recv, device):
    return pltpu.make_async_remote_copy(
        src_ref=src, dst_ref=dst, send_sem=send, recv_sem=recv, device_id=device, device_id_type=MESH
    )


def meet(devices):
    barrier = pltpu.get_barrier_semaphore()
    for device in devices:
        pl.semaphore_signal(barrier, inc=1, device_id=device, device_id_type=MESH)
    return barrier


def gelu(v):
    return 0.5 * v * (1.0 + jnp.tanh(0.7978845608028654 * (v + 0.044715 * (v * v * v))))


def nearest(nz):
    return [sorted((l for l in range(nz) if l != v), key=lambda l: (abs(l - v), l)) for v in range(nz)]


def pick(index, table):
    value = table[0]
    for v in range(1, len(table)):
        value = jnp.where(index == v, table[v], value)
    return value


def embed_kernel(
    n_dp, n_fsdp, width,
    hid_ref, len_hbm, ngain_hbm, up_ref, down_ref, pgain_hbm, proj_ref, own_hbm,
    out_ref,
    hid, nrm, upb, down2, pj, sa, ra, hs, s2, r2, every, u1, outgoing, choose, sizes,
    len_ref, own_ref, ngain_ref, pgain_ref,
    h_sem, lo_sem, ps, pr, zu, zd, zo, zr, xs, xr, ys, yr, ns, nr,
    dl, dns, dnr, as_, ar, s2s, r2s, s3s, r3s, js, jr, ks, kr, es, er, fs, fr, qs, qr, ts, tr,
):
    i = lax.axis_index("dp")
    j = lax.axis_index("fsdp")
    nz = n_fsdp // 2
    z = j // 2
    c = j % 2
    q = i % PLANE
    base = i - q
    rows = up_ref.shape[0]
    level_rows = 2 * rows
    chunks = upb.shape[0]
    subs = chunks // PLANE
    wide = chunks // nz
    per = subs // wide
    pass_rows, seq = hs.shape[0] // nz, hid.shape[0] // (hs.shape[0] // nz)
    half = nz * pass_rows
    ff_rows = down_ref.shape[0]
    emb = proj_ref.shape[1]
    d_rows = proj_ref.shape[0]
    part_rows = 2 * d_rows // PLANE
    qx = q + 1 - 2 * (q % 2)
    qy = q + 2 - 4 * (q // 2)
    qd = 3 - q
    partner = (i, z * 2 + 1 - c)
    near_x = (base + qx, j)
    near_y = (base + qy, j)
    peers = [(j + d) % n_fsdp for d in range(1, n_fsdp)]
    levels = [(z + d) % nz for d in range(1, nz)]
    planes = [(i + e) % n_dp for e in range(1, n_dp)]
    order = nearest(nz)
    near = [pick(z, [order[v][s] for v in range(nz)]) for s in range(nz - 1)]
    pending = []

    def along(level):
        return (i, level * 2 + c)

    def send(src, dst, ssem, rsem, device):
        copy = remote(src, dst, ssem, rsem, device)
        copy.start()
        pending.append(copy)
        return copy

    barrier = meet([(i, p) for p in peers] + [(p, j) for p in planes])

    own_k = [q * subs + s for s in range(subs)]
    x_k = [qx * subs + s for s in range(subs)]
    y_k = [qy * subs + s for s in range(subs)]
    d_k = [qd * subs + s for s in range(subs)]
    by_x = [s for s in range(subs) if s % 3 == 0]
    by_y = [s for s in range(subs) if s % 3 == 1]
    by_z = [s for s in range(subs) if s % 3 == 2]
    z_k = own_k + [d_k[s] for s in by_z]
    first = z_k + x_k + y_k + [d_k[s] for s in by_x + by_y]

    def source(core, k):
        at = ((k // wide * 2 + core) * wide + k % wide) * LANES
        return up_ref.at[:, pl.ds(pl.multiple_of(at, LANES), LANES)]

    def mine(k):
        return upb.at[k, pl.ds(pl.multiple_of(j * rows, rows), rows), :]

    def piece(k, level):
        return upb.at[k, pl.ds(pl.multiple_of(level * level_rows, level_rows), level_rows), :]

    local = []
    for n, k in enumerate(first):
        copy = pltpu.make_async_copy(source(c, k), mine(k), lo_sem.at[n])
        copy.start()
        local.append(copy)
    staged = [(hid_ref, hid), (ngain_hbm, ngain_ref), (len_hbm, len_ref), (own_hbm, own_ref), (pgain_hbm, pgain_ref)]
    staged = [pltpu.make_async_copy(src, dst, h_sem.at[n]) for n, (src, dst) in enumerate(staged)]
    for copy in staged:
        copy.start()
    pl.semaphore_wait(barrier, len(peers) + len(planes))
    swapped = []

    def swap(n):
        swapped.append(send(source(1 - c, first[n]), mine(first[n]), ps.at[n], pr.at[n], partner))

    def z_copy(t, level, hop):
        part = piece(z_k[t], level)
        sems = zu if hop == 1 else zd
        return remote(part, part, sems.at[t * nz + level], zr.at[t * nz + level], along(z + hop))

    def reaches(hop):
        return z + hop < nz if hop > 0 else z + hop >= 0

    def relays(level, hop):
        beyond = level <= z - REACH if hop > 0 else level >= z + REACH
        return jnp.logical_and(beyond, reaches(hop))

    def first_hop(t, h, e):
        core = c if e == 0 else 1 - c
        at = (t * len(HOPS) + h) * 2 + e
        return remote(
            source(core, z_k[t]), mine(z_k[t]), zo.at[at], zr.at[t * nz + z],
            (i, (z + HOPS[h]) * 2 + core),
        )

    def start_z(t):
        for h, hop in enumerate(HOPS):

            @pl.when(reaches(hop))
            def _():
                first_hop(t, h, 0).start()
                first_hop(t, h, 1).start()

    start_z(0)
    start_z(1)
    for n in range(chunks):
        swap(n)
    def proj_rows():
        return pj.at[z, pl.ds(pl.multiple_of(c * d_rows, d_rows), d_rows), :]

    def proj_part(level, plane):
        return pj.at[
            level,
            pl.ds(pl.multiple_of(plane * part_rows, part_rows), part_rows),
            pl.ds(pl.multiple_of(c * (emb // 2), emb // 2), emb // 2),
        ]

    def proj_side(level):
        return pj.at[level, :, pl.ds(pl.multiple_of(c * (emb // 2), emb // 2), emb // 2)]

    down_copy = pltpu.make_async_copy(down_ref, down2.at[c], dl.at[0])
    down_copy.start()
    proj_copy = pltpu.make_async_copy(proj_ref, proj_rows(), dl.at[1])
    proj_copy.start()
    for copy in staged:
        copy.wait()
    gain = ngain_ref[...].reshape(1, width)
    hs[...] = jnp.zeros_like(hs)

    def norm_block(p, carry):
        at = pl.ds(pl.multiple_of(p * seq, seq), seq)
        x = hid[at, :].astype(jnp.float32)
        keep = lax.broadcasted_iota(jnp.int32, (seq, 1), 0) < len_ref[p]
        scale = lax.rsqrt(jnp.sum(x * x, axis=1, keepdims=True) / width + EPSILON)
        scale = jnp.where(keep, scale, 0.0)
        nrm[c, at, :] = (x * scale * gain).astype(nrm.dtype)
        total = jnp.sum(jnp.where(keep, x, 0.0), axis=0, keepdims=True)
        hs[pl.ds(z * pass_rows + p, 1), :] = total
        return carry

    lax.fori_loop(0, pass_rows, norm_block, 0)
    nrm_copy = send(nrm.at[c], nrm.at[c], ns, nr, partner)
    down_swap = send(down_ref, down2.at[c], dns.at[0], dnr.at[0], partner)
    proj_swap = send(proj_ref, proj_rows(), dns.at[1], dnr.at[1], partner)
    row = lax.broadcasted_iota(jnp.int32, (pass_rows, LANES), 0)
    counts = jnp.zeros((pass_rows, LANES), jnp.float32)
    for p in range(pass_rows):
        counts = jnp.where(row == p, len_ref[p].astype(jnp.float32), counts)
    sizes[...] = counts
    capacity = outgoing.shape[1]
    targets = []
    for p in range(pass_rows):
        earlier = [(own_ref[p] == own_ref[o]).astype(jnp.int32) for o in range(p)]
        targets.append(own_ref[p] * capacity + sum(earlier))
    slot_at = lax.broadcasted_iota(jnp.int32, (n_dp * capacity, pass_rows), 0)
    pass_at = lax.broadcasted_iota(jnp.int32, (n_dp * capacity, pass_rows), 1)
    wanted = jnp.full((n_dp * capacity, pass_rows), -1, jnp.int32)
    for p in range(pass_rows):
        wanted = jnp.where(pass_at == p, targets[p], wanted)
    choose[...] = (slot_at == wanted).astype(jnp.float32).astype(choose.dtype)


    def along_x(slot, k, level):
        part = piece(k, level)
        return send(part, part, xs.at[slot * nz + level], xr.at[slot * nz + level], near_x)

    def along_y(slot, k, level):
        part = piece(k, level)
        return send(part, part, ys.at[slot * nz + level], yr.at[slot * nz + level], near_y)

    done = []
    x_sent, y_sent, x_relay, y_relay = {}, {}, {}, {}

    def z_step(t, s):
        level = near[s]
        z_copy(t, level, 1).wait_recv()
        for hop in (1, -1):

            @pl.when(relays(level, hop))
            def _():
                z_copy(t, level, hop).start()

        if t < subs:
            x_sent[t, s] = along_x(t, own_k[t], level)
            y_sent[t, s] = along_y(t, own_k[t], level)

    def xy_step(t, s):
        level = near[s]
        x_sent[t, s].wait_recv()
        y_sent[t, s].wait_recv()
        if t in by_x:
            x_relay[t, s] = along_x(subs + by_x.index(t), y_k[t], level)
        if t in by_y:
            y_relay[t, s] = along_y(subs + by_y.index(t), x_k[t], level)

    def compute(items):
        def slot(core, carry):
            block = [upb[quarter * subs + s] for quarter, s in items]
            block = jnp.concatenate(block, axis=1) if len(block) > 1 else block[0]
            pre = jnp.dot(nrm[core], block, preferred_element_type=jnp.float32)
            total = jnp.sum(gelu(pre).reshape(pass_rows, seq, block.shape[1]), axis=1)
            for n, (quarter, s) in enumerate(items):
                o = s % wide
                sa[quarter * per + s // wide, core, :, o * LANES : (o + 1) * LANES] = total[
                    :, n * LANES : (n + 1) * LANES
                ].astype(sa.dtype)
            return carry

        lax.fori_loop(0, 2, slot, 0)

    def act_copy(v, e):
        core = c if e == 0 else 1 - c
        return remote(
            sa.at[v, core], ra.at[c, z], as_.at[v * 2 + e], ar.at[c * nz + z], (i, v * 2 + core)
        )

    def send_acts(quarter):
        for b in range(per):
            v = quarter * per + b

            @pl.when(v == z)
            def _():
                ra[c, z] = sa[v, c]

            @pl.when(v != z)
            def _():
                act_copy(v, 0).start()

            act_copy(v, 1).start()

    def proj_out(v):
        return remote(proj_part(z, q), proj_part(z, q), s3s.at[v], r3s.at[z], along(v))

    ready = []
    left = {}

    def run(least):
        if len(ready) < least:
            return
        batch = [ready.pop(0) for _ in range(min(2, len(ready)))]
        compute([(quarter, s) for _, quarter, s in batch])
        for name, quarter, _ in batch:
            left[name] = left.get(name, subs) - 1
            if left[name] == 0:
                send_acts(quarter)

    last_slot = nz - 2
    z_steps = [(t, s) for t in range(len(z_k)) for s in range(nz - 1)]
    xy_steps = [(t, s) for t in range(subs) for s in range(nz - 1)]
    ends = [("x", t, s) for t in by_x for s in range(nz - 1)] + [("y", t, s) for t in by_y for s in range(nz - 1)]
    ends = sorted(ends, key=lambda r: (r[1], r[2]))
    at_step = {r: r[1] * (nz - 1) + r[2] + LAG + RELAY_LAG for r in ends}
    started = 2
    for n in range(max([len(z_steps), len(xy_steps) + LAG] + [m + 1 for m in at_step.values()])):
        if n == subs * (nz - 1):
            proj_copy.wait()
            proj_swap.wait_recv()
            for v in levels:
                copy = proj_out(v)
                copy.start()
                pending.append(copy)
        if n < len(z_steps):
            t, s = z_steps[n]
            z_step(t, s)
            if s == last_slot:
                if started < len(z_k):
                    start_z(started)
                    started += 1
                local[t].wait()
                swapped[t].wait_recv()
                ready.append(("own", q, t) if t < subs else ("diag", qd, by_z[t - subs]))
        if 0 <= n - LAG < len(xy_steps):
            t, s = xy_steps[n - LAG]
            xy_step(t, s)
            if s == last_slot:
                if t == 0:
                    for copy, arrived in list(zip(local, swapped))[len(z_k) :]:
                        copy.wait()
                        arrived.wait_recv()
                ready.append(("x", qx, t))
                ready.append(("y", qy, t))
        for kind, t, s in ends:
            if at_step[kind, t, s] == n:
                (x_relay if kind == "x" else y_relay)[t, s].wait_recv()
                if s == last_slot:
                    ready.append(("diag", qd, t))
        if n == nz - 1:
            nrm_copy.wait_recv()
        if n >= nz - 1:
            run(2)
    while ready:
        run(1)

    beside = [(qx, near_x), (qy, near_y), (qd, (base + qd, j))]
    proj_sent = {}
    for e, v in enumerate(near):
        remote(proj_part(v, q), proj_part(v, q), s3s.at[v], r3s.at[v], along(v)).wait_recv()
        for n, (_, device) in enumerate(beside):
            at = n * nz + v
            proj_sent[n, e] = send(proj_part(v, q), proj_part(v, q), js.at[at], jr.at[at], device)

    down_copy.wait()
    down_swap.wait_recv()
    for v in range(nz):
        for e in range(2):
            core = c if e == 0 else 1 - c
            arrival = remote(
                sa.at[v, core], ra.at[core, v], as_.at[v * 2 + e], ar.at[core * nz + v], partner
            )
            if e == 0:

                @pl.when(v != z)
                def _():
                    arrival.wait_recv()

            else:
                arrival.wait_recv()

    acts = [ra[core].reshape(half, wide * LANES)[:, :ff_rows] for core in range(2)]

    def part_copy(v):
        return remote(s2.at[v], r2.at[z], s2s.at[v], r2s.at[z], along(v))

    for b in range(2):
        at = slice(b * (width // 2), (b + 1) * (width // 2))
        part = hs[:, at]
        for core in range(2):
            part = part + jnp.dot(acts[core], down2[core, :, at], preferred_element_type=jnp.float32)
        s2[:, :, at] = part.astype(s2.dtype).reshape(nz, pass_rows, width // 2)
    for v in range(nz):

        @pl.when(v != z)
        def _():
            part_copy(v).start()

    proj_last = []
    for e, v in enumerate(near):
        for n in range(len(beside)):
            proj_sent[n, e].wait_recv()
        proj_last.append(send(proj_side(v), proj_side(v), ks.at[v], kr.at[v], partner))
    pooled = s2[z].astype(jnp.float32)
    for v in near:
        remote(s2.at[v], r2.at[v], s2s.at[v], r2s.at[v], along(v)).wait_recv()
        pooled = pooled + r2[v].astype(jnp.float32)
    counts = sizes[:, :1]
    norm = jnp.sum(pooled * pooled, axis=1, keepdims=True) / width
    scaled = pooled * lax.rsqrt(norm + EPSILON * (counts * counts)) * pgain_ref[...].reshape(1, width)
    scaled = scaled.astype(proj_ref.dtype)
    for copy in proj_last:
        copy.wait_recv()
    embedded = jnp.dot(scaled, pj[...].reshape(width, emb), preferred_element_type=jnp.float32)
    every[i, c, z] = embedded.astype(every.dtype)

    def to_level(v):
        part = every.at[i, c, z]
        return remote(part, part, es.at[v], er.at[z], along(v))

    def from_level(v):
        part = every.at[i, c, v]
        return remote(part, part, es.at[v], er.at[v], along(v))

    for v in levels:
        copy = to_level(v)
        copy.start()
        pending.append(copy)
    last = []

    def to_partner(part, n):
        last.append(send(part, part, qs.at[n], qr.at[n], partner))

    if n_dp == PLANE:
        seen = [z] + near
        across = {}
        for e in range(nz):
            if e > 0:
                from_level(seen[e]).wait_recv()
            part = every.at[i, c, seen[e]]
            for n, (_, device) in enumerate(beside):
                at = n * nz + seen[e]
                across[n, e] = send(part, part, fs.at[at], fr.at[at], device)
        to_partner(every.at[i, c], 0)
        for n, (plane, _) in enumerate(beside):
            for e in range(nz):
                across[n, e].wait_recv()
            to_partner(every.at[plane, c], n + 1)
    else:
        for v in levels:
            from_level(v).wait_recv()
        part = every.at[i, c]
        fifth = [send(part, part, fs.at[e], fr.at[e], (p, j)) for e, p in enumerate(planes)]
        to_partner(part, 0)
        for e, copy in enumerate(fifth):
            copy.wait_recv()
            to_partner(every.at[(i + n_dp - e - 1) % n_dp, c], e + 1)

    for copy in last:
        copy.wait_recv()

    bf = jnp.bfloat16
    n_rows = n_dp * n_fsdp * pass_rows
    mark = ((i * 2 + c) * nz + z) * pass_rows
    rounded = every[i, c, z].astype(jnp.float32)

    def mul(a, b):
        return jnp.dot(a.astype(bf), b, preferred_element_type=jnp.float32)

    def mul2(a, b):
        high = a.astype(bf)
        return mul(high, b) + mul(a - high.astype(jnp.float32), b)

    def eye(n):
        at = lax.broadcasted_iota(jnp.int32, (n, n), 0)
        return (at == lax.broadcasted_iota(jnp.int32, (n, n), 1)).astype(jnp.float32)

    if n_rows < emb:
        rows_all = every[...].reshape(n_rows, emb)
        average = jnp.sum(rows_all.astype(jnp.float32), axis=0, keepdims=True) / n_rows
        gram = lax.dot_general(
            rows_all, rows_all, (((1,), (1,)), ((), ())), preferred_element_type=jnp.float32
        ) / n_rows
        by_col = jnp.mean(gram, axis=0, keepdims=True)
        by_row = jnp.mean(gram, axis=1, keepdims=True)
        ridged = gram - by_col - by_row + jnp.mean(by_col) + RIDGE_TERM * eye(n_rows)
        squared = jnp.sum(ridged * ridged) + RIDGE_TERM * RIDGE_TERM * (emb - n_rows)
    else:
        def add(b, carry):
            part = every[b // 2, b % 2].reshape(half, emb)
            moment = lax.dot_general(
                part, part, (((0,), (0,)), ((), ())), preferred_element_type=jnp.float32
            )
            u1[...] += moment
            return carry + jnp.sum(part.astype(jnp.float32), axis=0, keepdims=True)

        u1[...] = jnp.zeros_like(u1)
        average = lax.fori_loop(0, n_dp * 2, add, jnp.zeros((1, emb), jnp.float32)) / n_rows
        tall = jnp.transpose(jnp.broadcast_to(average, (emb, emb)))
        ridged = u1[...] / n_rows - tall * average + RIDGE_TERM * eye(emb)
        squared = jnp.sum(ridged * ridged)
    doubled = 2.0 * lax.rsqrt(squared)
    t1 = ridged * doubled
    u1[...] = t1
    t1b = t1.astype(bf)
    t2 = 2.0 * t1 - mul(t1, t1b)
    t2b = t2.astype(bf)
    t4 = 2.0 * t2 - mul(t2, t2b)
    t4b = t4.astype(bf)
    if n_rows < emb:
        lane = lax.broadcasted_iota(jnp.int32, (pass_rows, n_rows), 1)
        here = (lane == mark + lax.broadcasted_iota(jnp.int32, (pass_rows, n_rows), 0)).astype(jnp.float32)
        mix = 2.0 * here - u1[pl.ds(pl.multiple_of(mark, pass_rows), pass_rows), :]
        times = mul
    else:
        mix = embedded - average
        mix = 2.0 * mix - mul2(mix, t1b)
        times = mul2
    mix = 2.0 * mix - times(mix, t2b)
    mix = 2.0 * mix - times(mix, t4b)
    rest = mix - times(mix, t4b)
    mix = mix + (rest - times(rest, t4b))
    if n_rows < emb:
        mixed = mul2(mix, rows_all) - jnp.sum(mix, axis=1, keepdims=True) * average
        mix = mixed + jnp.sum(mix * here, axis=1, keepdims=True) * (embedded - rounded)
    whitened = (mix * doubled).astype(bf)
    routed = jnp.dot(choose[...], whitened, preferred_element_type=jnp.float32)
    for p in range(n_dp):
        outgoing[p] = routed[p * capacity : (p + 1) * capacity].astype(bf)
    sixth = [send(outgoing.at[p], out_ref.at[i], ts.at[e], tr.at[e], (p, j)) for e, p in enumerate(planes)]
    kept = pltpu.make_async_copy(outgoing.at[i], out_ref.at[i], h_sem.at[0])
    kept.start()
    kept.wait()
    for copy in sixth:
        copy.wait_recv()

    for copy in pending:
        copy.wait_send()
    for t in range(len(z_k)):
        for h, hop in enumerate(HOPS):

            @pl.when(reaches(hop))
            def _():
                first_hop(t, h, 0).wait_send()
                first_hop(t, h, 1).wait_send()

        for level in range(nz):
            for hop in (1, -1):

                @pl.when(relays(level, hop))
                def _():
                    z_copy(t, level, hop).wait_send()

    for v in range(nz):

        @pl.when(v != z)
        def _():
            act_copy(v, 0).wait_send()
            part_copy(v).wait_send()

        act_copy(v, 1).wait_send()


def encode(hidden, lengths, norm_gain, up, down, pool_gain, proj, owners, n_dp, n_fsdp):
    tok_rows, width = hidden.shape
    pass_rows = lengths.shape[0]
    nz = n_fsdp // 2
    ff_rows = down.shape[0]
    d_rows, emb = proj.shape
    half = nz * pass_rows
    wide = -(-ff_rows // LANES)
    chunks = nz * wide
    subs = chunks // PLANE
    legs = [len([s for s in range(subs) if s % 3 == r]) for r in range(3)]
    if up.shape[1] != 2 * chunks * LANES:
        up = jnp.pad(
            up.reshape(up.shape[0], n_fsdp, ff_rows), ((0, 0), (0, 0), (0, wide * LANES - ff_rows))
        ).reshape(up.shape[0], n_fsdp * wide * LANES)
    capacity = 2 * pass_rows // n_dp
    side = min(emb, n_dp * n_fsdp * pass_rows)
    bf = jnp.bfloat16
    f32 = jnp.float32
    dma = pltpu.SemaphoreType.DMA
    hbm = pl.BlockSpec(memory_space=pl.ANY)
    in_z = (subs + legs[2]) * nz
    return pl.pallas_call(
        functools.partial(embed_kernel, n_dp, n_fsdp, width),
        out_shape=jax.ShapeDtypeStruct((n_dp, capacity, emb), bf),
        in_specs=[hbm] * 8,
        out_specs=hbm,
        scratch_shapes=[
            pltpu.VMEM((tok_rows, width), bf),
            pltpu.VMEM((2, tok_rows, width), bf),
            pltpu.VMEM((chunks, width, LANES), bf),
            pltpu.VMEM((2, ff_rows, width), bf),
            pltpu.VMEM((nz, 2 * d_rows, emb), bf),
            pltpu.VMEM((nz, 2, pass_rows, wide * LANES), bf),
            pltpu.VMEM((2, nz, pass_rows, wide * LANES), bf),
            pltpu.VMEM((half, width), f32),
            pltpu.VMEM((nz, pass_rows, width), bf),
            pltpu.VMEM((nz, pass_rows, width), bf),
            pltpu.VMEM((n_dp, 2, nz, pass_rows, emb), bf),
            pltpu.VMEM((side, side), f32),
            pltpu.VMEM((n_dp, capacity, emb), bf),
            pltpu.VMEM((n_dp * capacity, pass_rows), bf),
            pltpu.VMEM((pass_rows, LANES), f32),
            pltpu.SMEM((pass_rows,), jnp.int32),
            pltpu.SMEM((pass_rows,), jnp.int32),
            pltpu.VMEM((width,), f32),
            pltpu.VMEM((width,), f32),
            dma((5,)),
            dma((chunks,)),
            dma((chunks,)),
            dma((chunks,)),
            dma((in_z,)),
            dma((in_z,)),
            dma((in_z // nz * len(HOPS) * 2,)),
            dma((in_z,)),
            dma(((subs + legs[0]) * nz,)),
            dma(((subs + legs[0]) * nz,)),
            dma(((subs + legs[1]) * nz,)),
            dma(((subs + legs[1]) * nz,)),
            dma,
            dma,
            dma((2,)),
            dma((2,)),
            dma((2,)),
            dma((n_fsdp,)),
            dma((n_fsdp,)),
        ]
        + [dma((nz,))] * 4
        + [dma((3 * nz,))] * 2
        + [dma((nz,))] * 4
        + [dma((max(3 * nz, n_dp),))] * 2
        + [dma((n_dp,))] * 2
        + [dma((n_dp - 1,))] * 2,
        compiler_params=pltpu.CompilerParams(
            collective_id=0, has_side_effects=True, vmem_limit_bytes=60 * 1024 * 1024
        ),
        name="embed",
    )(hidden, lengths, norm_gain, up, down, pool_gain, proj, owners)


def on_device(hidden, lengths, norm_gain, up_weight, down_weight, pool_gain, proj_weight, owners):
    n_dp, n_fsdp = lax.axis_size("dp"), lax.axis_size("fsdp")
    owned = encode(
        hidden, lengths, norm_gain, up_weight, down_weight, pool_gain, proj_weight,
        owners.reshape(-1), n_dp, n_fsdp,
    )
    return owned.reshape(-1, owned.shape[2])


def solution(mesh):
    placed = (
        P(("dp", "fsdp"), None),
        P(("dp", "fsdp")),
        P(),
        P("fsdp", None),
        P("fsdp", None),
        P(),
        P("fsdp", None),
        P(("dp", "fsdp"), None),
    )
    return jax.shard_map(
        on_device, mesh=mesh, in_specs=placed, out_specs=P(("dp", "fsdp"), None), check_vma=False
    )
```

```python
import functools

import jax
import jax.numpy as jnp
from jax import lax
from jax.experimental import pallas as pl
from jax.experimental.pallas import tpu as pltpu
from jax.sharding import PartitionSpec as P

RIDGE_TERM = 1.0
EPSILON = 1e-06
MESH = pl.DeviceIdType.MESH
PLANE = 4
LANES = 128
LAG = 4
RELAY_LAG = 4
REACH = 1
HOPS = (1, -1)


def remote(src, dst, send, recv, device):
    return pltpu.make_async_remote_copy(
        src_ref=src, dst_ref=dst, send_sem=send, recv_sem=recv, device_id=device, device_id_type=MESH
    )


def meet(devices):
    barrier = pltpu.get_barrier_semaphore()
    for device in devices:
        pl.semaphore_signal(barrier, inc=1, device_id=device, device_id_type=MESH)
    return barrier


def gelu(v):
    return 0.5 * v * (1.0 + jnp.tanh(0.7978845608028654 * (v + 0.044715 * (v * v * v))))


def nearest(nz):
    return [sorted((l for l in range(nz) if l != v), key=lambda l: (abs(l - v), l)) for v in range(nz)]


def pick(index, table):
    value = table[0]
    for v in range(1, len(table)):
        value = jnp.where(index == v, table[v], value)
    return value


def embed_kernel(
    n_dp, n_fsdp, width,
    hid_ref, len_hbm, ngain_hbm, up_ref, down_ref, pgain_hbm, proj_ref, own_hbm,
    out_ref,
    hid, nrm, upb, down2, pj, sa, ra, hs, s2, r2, every, u1, outgoing, choose, sizes,
    len_ref, own_ref, ngain_ref, pgain_ref,
    h_sem, lo_sem, ps, pr, zu, zd, zo, zr, xs, xr, ys, yr, ns, nr,
    dl, dns, dnr, as_, ar, s2s, r2s, s3s, r3s, js, jr, ks, kr, es, er, fs, fr, qs, qr, ts, tr,
):
    i = lax.axis_index("dp")
    j = lax.axis_index("fsdp")
    nz = n_fsdp // 2
    z = j // 2
    c = j % 2
    q = i % PLANE
    base = i - q
    rows = up_ref.shape[0]
    level_rows = 2 * rows
    chunks = upb.shape[0]
    subs = chunks // PLANE
    wide = chunks // nz
    per = subs // wide
    pass_rows, seq = hs.shape[0] // nz, hid.shape[0] // (hs.shape[0] // nz)
    half = nz * pass_rows
    ff_rows = down_ref.shape[0]
    emb = proj_ref.shape[1]
    d_rows = proj_ref.shape[0]
    part_rows = 2 * d_rows // PLANE
    qx = q + 1 - 2 * (q % 2)
    qy = q + 2 - 4 * (q // 2)
    qd = 3 - q
    partner = (i, z * 2 + 1 - c)
    near_x = (base + qx, j)
    near_y = (base + qy, j)
    peers = [(j + d) % n_fsdp for d in range(1, n_fsdp)]
    levels = [(z + d) % nz for d in range(1, nz)]
    planes = [(i + e) % n_dp for e in range(1, n_dp)]
    order = nearest(nz)
    near = [pick(z, [order[v][s] for v in range(nz)]) for s in range(nz - 1)]
    pending = []

    def along(level):
        return (i, level * 2 + c)

    def send(src, dst, ssem, rsem, device):
        copy = remote(src, dst, ssem, rsem, device)
        copy.start()
        pending.append(copy)
        return copy

    barrier = meet([(i, p) for p in peers] + [(p, j) for p in planes])

    own_k = [q * subs + s for s in range(subs)]
    x_k = [qx * subs + s for s in range(subs)]
    y_k = [qy * subs + s for s in range(subs)]
    d_k = [qd * subs + s for s in range(subs)]
    by_x = [s for s in range(subs) if s % 3 == 0]
    by_y = [s for s in range(subs) if s % 3 == 1]
    by_z = [s for s in range(subs) if s % 3 == 2]
    z_k = own_k + [d_k[s] for s in by_z]
    first = z_k + x_k + y_k + [d_k[s] for s in by_x + by_y]

    def source(core, k):
        at = ((k // wide * 2 + core) * wide + k % wide) * LANES
        return up_ref.at[:, pl.ds(pl.multiple_of(at, LANES), LANES)]

    def mine(k):
        return upb.at[k, pl.ds(pl.multiple_of(j * rows, rows), rows), :]

    def piece(k, level):
        return upb.at[k, pl.ds(pl.multiple_of(level * level_rows, level_rows), level_rows), :]

    local = []
    for n, k in enumerate(first):
        copy = pltpu.make_async_copy(source(c, k), mine(k), lo_sem.at[n])
        copy.start()
        local.append(copy)
    staged = [(hid_ref, hid), (ngain_hbm, ngain_ref), (len_hbm, len_ref), (own_hbm, own_ref), (pgain_hbm, pgain_ref)]
    staged = [pltpu.make_async_copy(src, dst, h_sem.at[n]) for n, (src, dst) in enumerate(staged)]
    for copy in staged:
        copy.start()
    pl.semaphore_wait(barrier, len(peers) + len(planes))
    swapped = []

    def swap(n):
        swapped.append(send(source(1 - c, first[n]), mine(first[n]), ps.at[n], pr.at[n], partner))

    def z_copy(t, level, hop):
        part = piece(z_k[t], level)
        sems = zu if hop == 1 else zd
        return remote(part, part, sems.at[t * nz + level], zr.at[t * nz + level], along(z + hop))

    def reaches(hop):
        return z + hop < nz if hop > 0 else z + hop >= 0

    def relays(level, hop):
        beyond = level <= z - REACH if hop > 0 else level >= z + REACH
        return jnp.logical_and(beyond, reaches(hop))

    def first_hop(t, h, e):
        core = c if e == 0 else 1 - c
        at = (t * len(HOPS) + h) * 2 + e
        return remote(
            source(core, z_k[t]), mine(z_k[t]), zo.at[at], zr.at[t * nz + z],
            (i, (z + HOPS[h]) * 2 + core),
        )

    def start_z(t):
        for h, hop in enumerate(HOPS):

            @pl.when(reaches(hop))
            def _():
                first_hop(t, h, 0).start()
                first_hop(t, h, 1).start()

    start_z(0)
    start_z(1)
    for n in range(chunks):
        swap(n)
    def proj_rows():
        return pj.at[z, pl.ds(pl.multiple_of(c * d_rows, d_rows), d_rows), :]

    def proj_part(level, plane):
        return pj.at[
            level,
            pl.ds(pl.multiple_of(plane * part_rows, part_rows), part_rows),
            pl.ds(pl.multiple_of(c * (emb // 2), emb // 2), emb // 2),
        ]

    def proj_side(level):
        return pj.at[level, :, pl.ds(pl.multiple_of(c * (emb // 2), emb // 2), emb // 2)]

    down_copy = pltpu.make_async_copy(down_ref, down2.at[c], dl.at[0])
    down_copy.start()
    proj_copy = pltpu.make_async_copy(proj_ref, proj_rows(), dl.at[1])
    proj_copy.start()
    for copy in staged:
        copy.wait()
    gain = ngain_ref[...].reshape(1, width)
    hs[...] = jnp.zeros_like(hs)

    def norm_block(p, carry):
        at = pl.ds(pl.multiple_of(p * seq, seq), seq)
        x = hid[at, :].astype(jnp.float32)
        keep = lax.broadcasted_iota(jnp.int32, (seq, 1), 0) < len_ref[p]
        scale = lax.rsqrt(jnp.sum(x * x, axis=1, keepdims=True) / width + EPSILON)
        scale = jnp.where(keep, scale, 0.0)
        nrm[c, at, :] = (x * scale * gain).astype(nrm.dtype)
        total = jnp.sum(jnp.where(keep, x, 0.0), axis=0, keepdims=True)
        hs[pl.ds(z * pass_rows + p, 1), :] = total
        return carry

    lax.fori_loop(0, pass_rows, norm_block, 0)
    nrm_copy = send(nrm.at[c], nrm.at[c], ns, nr, partner)
    down_swap = send(down_ref, down2.at[c], dns.at[0], dnr.at[0], partner)
    proj_swap = send(proj_ref, proj_rows(), dns.at[1], dnr.at[1], partner)
    row = lax.broadcasted_iota(jnp.int32, (pass_rows, LANES), 0)
    counts = jnp.zeros((pass_rows, LANES), jnp.float32)
    for p in range(pass_rows):
        counts = jnp.where(row == p, len_ref[p].astype(jnp.float32), counts)
    sizes[...] = counts
    capacity = outgoing.shape[1]
    targets = []
    for p in range(pass_rows):
        earlier = [(own_ref[p] == own_ref[o]).astype(jnp.int32) for o in range(p)]
        targets.append(own_ref[p] * capacity + sum(earlier))
    slot_at = lax.broadcasted_iota(jnp.int32, (n_dp * capacity, pass_rows), 0)
    pass_at = lax.broadcasted_iota(jnp.int32, (n_dp * capacity, pass_rows), 1)
    wanted = jnp.full((n_dp * capacity, pass_rows), -1, jnp.int32)
    for p in range(pass_rows):
        wanted = jnp.where(pass_at == p, targets[p], wanted)
    choose[...] = (slot_at == wanted).astype(jnp.float32).astype(choose.dtype)


    def along_x(slot, k, level):
        part = piece(k, level)
        return send(part, part, xs.at[slot * nz + level], xr.at[slot * nz + level], near_x)

    def along_y(slot, k, level):
        part = piece(k, level)
        return send(part, part, ys.at[slot * nz + level], yr.at[slot * nz + level], near_y)

    done = []
    x_sent, y_sent, x_relay, y_relay = {}, {}, {}, {}

    def z_step(t, s):
        level = near[s]
        z_copy(t, level, 1).wait_recv()
        for hop in (1, -1):

            @pl.when(relays(level, hop))
            def _():
                z_copy(t, level, hop).start()

        if t < subs:
            x_sent[t, s] = along_x(t, own_k[t], level)
            y_sent[t, s] = along_y(t, own_k[t], level)

    def xy_step(t, s):
        level = near[s]
        x_sent[t, s].wait_recv()
        y_sent[t, s].wait_recv()
        if t in by_x:
            x_relay[t, s] = along_x(subs + by_x.index(t), y_k[t], level)
        if t in by_y:
            y_relay[t, s] = along_y(subs + by_y.index(t), x_k[t], level)

    def compute(items):
        def slot(core, carry):
            block = [upb[quarter * subs + s] for quarter, s in items]
            block = jnp.concatenate(block, axis=1) if len(block) > 1 else block[0]
            pre = jnp.dot(nrm[core], block, preferred_element_type=jnp.float32)
            total = jnp.sum(gelu(pre).reshape(pass_rows, seq, block.shape[1]), axis=1)
            for n, (quarter, s) in enumerate(items):
                o = s % wide
                sa[quarter * per + s // wide, core, :, o * LANES : (o + 1) * LANES] = total[
                    :, n * LANES : (n + 1) * LANES
                ].astype(sa.dtype)
            return carry

        lax.fori_loop(0, 2, slot, 0)

    def act_copy(v, e):
        core = c if e == 0 else 1 - c
        return remote(
            sa.at[v, core], ra.at[c, z], as_.at[v * 2 + e], ar.at[c * nz + z], (i, v * 2 + core)
        )

    def send_acts(quarter):
        for b in range(per):
            v = quarter * per + b

            @pl.when(v == z)
            def _():
                ra[c, z] = sa[v, c]

            @pl.when(v != z)
            def _():
                act_copy(v, 0).start()

            act_copy(v, 1).start()

    def proj_out(v):
        return remote(proj_part(z, q), proj_part(z, q), s3s.at[v], r3s.at[z], along(v))

    ready = []
    left = {}

    def run(least):
        if len(ready) < least:
            return
        batch = [ready.pop(0) for _ in range(min(2, len(ready)))]
        compute([(quarter, s) for _, quarter, s in batch])
        for name, quarter, _ in batch:
            left[name] = left.get(name, subs) - 1
            if left[name] == 0:
                send_acts(quarter)

    last_slot = nz - 2
    z_steps = [(t, s) for t in range(len(z_k)) for s in range(nz - 1)]
    xy_steps = [(t, s) for t in range(subs) for s in range(nz - 1)]
    ends = [("x", t, s) for t in by_x for s in range(nz - 1)] + [("y", t, s) for t in by_y for s in range(nz - 1)]
    ends = sorted(ends, key=lambda r: (r[1], r[2]))
    at_step = {r: r[1] * (nz - 1) + r[2] + LAG + RELAY_LAG for r in ends}
    started = 2
    for n in range(max([len(z_steps), len(xy_steps) + LAG] + [m + 1 for m in at_step.values()])):
        if n == subs * (nz - 1):
            proj_copy.wait()
            proj_swap.wait_recv()
            for v in levels:
                copy = proj_out(v)
                copy.start()
                pending.append(copy)
        if n < len(z_steps):
            t, s = z_steps[n]
            z_step(t, s)
            if s == last_slot:
                if started < len(z_k):
                    start_z(started)
                    started += 1
                local[t].wait()
                swapped[t].wait_recv()
                ready.append(("own", q, t) if t < subs else ("diag", qd, by_z[t - subs]))
        if 0 <= n - LAG < len(xy_steps):
            t, s = xy_steps[n - LAG]
            xy_step(t, s)
            if s == last_slot:
                if t == 0:
                    for copy, arrived in list(zip(local, swapped))[len(z_k) :]:
                        copy.wait()
                        arrived.wait_recv()
                ready.append(("x", qx, t))
                ready.append(("y", qy, t))
        for kind, t, s in ends:
            if at_step[kind, t, s] == n:
                (x_relay if kind == "x" else y_relay)[t, s].wait_recv()
                if s == last_slot:
                    ready.append(("diag", qd, t))
        if n == nz - 1:
            nrm_copy.wait_recv()
        if n >= nz - 1:
            run(2)
    while ready:
        run(1)

    beside = [(qx, near_x), (qy, near_y), (qd, (base + qd, j))]
    proj_sent = {}
    sent_up = len(pending)
    for e, v in enumerate(near):
        remote(proj_part(v, q), proj_part(v, q), s3s.at[v], r3s.at[v], along(v)).wait_recv()
        for n, (_, device) in enumerate(beside):
            at = n * nz + v
            proj_sent[n, e] = send(proj_part(v, q), proj_part(v, q), js.at[at], jr.at[at], device)

    down_copy.wait()
    down_swap.wait_recv()
    for v in range(nz):
        for e in range(2):
            core = c if e == 0 else 1 - c
            arrival = remote(
                sa.at[v, core], ra.at[core, v], as_.at[v * 2 + e], ar.at[core * nz + v], partner
            )
            if e == 0:

                @pl.when(v != z)
                def _():
                    arrival.wait_recv()

            else:
                arrival.wait_recv()

    acts = [ra[core].reshape(half, wide * LANES)[:, :ff_rows] for core in range(2)]

    def part_copy(b, v):
        return remote(s2.at[b, v], r2.at[b, z], s2s.at[b * nz + v], r2s.at[b * nz + z], along(v))

    def part_from(b, v):
        return remote(s2.at[b, v], r2.at[b, v], s2s.at[b * nz + v], r2s.at[b * nz + v], along(v))

    for b in range(2):
        at = slice(b * (width // 2), (b + 1) * (width // 2))
        part = hs[:, at]
        for core in range(2):
            part = part + jnp.dot(acts[core], down2[core, :, at], preferred_element_type=jnp.float32)
        s2[b] = part.astype(s2.dtype).reshape(nz, pass_rows, width // 2)
        for v in range(nz):

            @pl.when(v != z)
            def _():
                part_copy(b, v).start()

    for copy in pending[:sent_up]:
        copy.wait_send()
    for t in range(len(z_k)):
        for h, hop in enumerate(HOPS):

            @pl.when(reaches(hop))
            def _():
                first_hop(t, h, 0).wait_send()
                first_hop(t, h, 1).wait_send()

        for level in range(nz):
            for hop in (1, -1):

                @pl.when(relays(level, hop))
                def _():
                    z_copy(t, level, hop).wait_send()

    for v in range(nz):

        @pl.when(v != z)
        def _():
            act_copy(v, 0).wait_send()

        act_copy(v, 1).wait_send()

    proj_last = []
    for e, v in enumerate(near):
        for n in range(len(beside)):
            proj_sent[n, e].wait_recv()
        proj_last.append(send(proj_side(v), proj_side(v), ks.at[v], kr.at[v], partner))
    halves = []
    for b in range(2):
        total = s2[b, z].astype(jnp.float32)
        for v in near:
            part_from(b, v).wait_recv()
            total = total + r2[b, v].astype(jnp.float32)
        halves.append(total)
    pooled = jnp.concatenate(halves, axis=1)
    counts = sizes[:, :1]
    norm = jnp.sum(pooled * pooled, axis=1, keepdims=True) / width
    scaled = pooled * lax.rsqrt(norm + EPSILON * (counts * counts)) * pgain_ref[...].reshape(1, width)
    scaled = scaled.astype(proj_ref.dtype)
    for copy in proj_last:
        copy.wait_recv()
    embedded = jnp.dot(scaled, pj[...].reshape(width, emb), preferred_element_type=jnp.float32)
    every[i, c, z] = embedded.astype(every.dtype)

    def to_level(v):
        part = every.at[i, c, z]
        return remote(part, part, es.at[v], er.at[z], along(v))

    def from_level(v):
        part = every.at[i, c, v]
        return remote(part, part, es.at[v], er.at[v], along(v))

    for v in levels:
        copy = to_level(v)
        copy.start()
        pending.append(copy)
    last = []

    def to_partner(part, n):
        last.append(send(part, part, qs.at[n], qr.at[n], partner))

    if n_dp == PLANE:
        seen = [z] + near
        across = {}
        for e in range(nz):
            if e > 0:
                from_level(seen[e]).wait_recv()
            part = every.at[i, c, seen[e]]
            for n, (_, device) in enumerate(beside):
                at = n * nz + seen[e]
                across[n, e] = send(part, part, fs.at[at], fr.at[at], device)
        to_partner(every.at[i, c], 0)
        for n, (plane, _) in enumerate(beside):
            for e in range(nz):
                across[n, e].wait_recv()
            to_partner(every.at[plane, c], n + 1)
    else:
        for v in levels:
            from_level(v).wait_recv()
        part = every.at[i, c]
        fifth = [send(part, part, fs.at[e], fr.at[e], (p, j)) for e, p in enumerate(planes)]
        to_partner(part, 0)
        for e, copy in enumerate(fifth):
            copy.wait_recv()
            to_partner(every.at[(i + n_dp - e - 1) % n_dp, c], e + 1)

    for b in range(2):
        for v in range(nz):

            @pl.when(v != z)
            def _():
                part_copy(b, v).wait_send()

    for copy in last:
        copy.wait_recv()
    for copy in pending[sent_up:]:
        copy.wait_send()
    kept_up = len(pending)

    bf = jnp.bfloat16
    n_rows = n_dp * n_fsdp * pass_rows
    mark = ((i * 2 + c) * nz + z) * pass_rows
    rounded = every[i, c, z].astype(jnp.float32)

    def mul(a, b):
        return jnp.dot(a.astype(bf), b, preferred_element_type=jnp.float32)

    def mul2(a, b):
        high = a.astype(bf)
        return mul(high, b) + mul(a - high.astype(jnp.float32), b)

    def eye(n):
        at = lax.broadcasted_iota(jnp.int32, (n, n), 0)
        return (at == lax.broadcasted_iota(jnp.int32, (n, n), 1)).astype(jnp.float32)

    if n_rows < emb:
        rows_all = every[...].reshape(n_rows, emb)
        average = jnp.sum(rows_all.astype(jnp.float32), axis=0, keepdims=True) / n_rows
        gram = lax.dot_general(
            rows_all, rows_all, (((1,), (1,)), ((), ())), preferred_element_type=jnp.float32
        ) / n_rows
        by_col = jnp.mean(gram, axis=0, keepdims=True)
        by_row = jnp.mean(gram, axis=1, keepdims=True)
        ridged = gram - by_col - by_row + jnp.mean(by_col) + RIDGE_TERM * eye(n_rows)
        squared = jnp.sum(ridged * ridged) + RIDGE_TERM * RIDGE_TERM * (emb - n_rows)
    else:
        def add(b, carry):
            part = every[b // 2, b % 2].reshape(half, emb)
            moment = lax.dot_general(
                part, part, (((0,), (0,)), ((), ())), preferred_element_type=jnp.float32
            )
            u1[...] += moment
            return carry + jnp.sum(part.astype(jnp.float32), axis=0, keepdims=True)

        u1[...] = jnp.zeros_like(u1)
        average = lax.fori_loop(0, n_dp * 2, add, jnp.zeros((1, emb), jnp.float32)) / n_rows
        tall = jnp.transpose(jnp.broadcast_to(average, (emb, emb)))
        ridged = u1[...] / n_rows - tall * average + RIDGE_TERM * eye(emb)
        squared = jnp.sum(ridged * ridged)
    doubled = 2.0 * lax.rsqrt(squared)
    t1 = ridged * doubled
    u1[...] = t1
    t1b = t1.astype(bf)
    t2 = 2.0 * t1 - mul(t1, t1b)
    t2b = t2.astype(bf)
    t4 = 2.0 * t2 - mul(t2, t2b)
    t4b = t4.astype(bf)
    if n_rows < emb:
        lane = lax.broadcasted_iota(jnp.int32, (pass_rows, n_rows), 1)
        here = (lane == mark + lax.broadcasted_iota(jnp.int32, (pass_rows, n_rows), 0)).astype(jnp.float32)
        mix = 2.0 * here - u1[pl.ds(pl.multiple_of(mark, pass_rows), pass_rows), :]
        times = mul
    else:
        mix = embedded - average
        mix = 2.0 * mix - mul2(mix, t1b)
        times = mul2
    mix = 2.0 * mix - times(mix, t2b)
    mix = 2.0 * mix - times(mix, t4b)
    rest = mix - times(mix, t4b)
    mix = mix + (rest - times(rest, t4b))
    if n_rows < emb:
        mixed = mul2(mix, rows_all) - jnp.sum(mix, axis=1, keepdims=True) * average
        mix = mixed + jnp.sum(mix * here, axis=1, keepdims=True) * (embedded - rounded)
    whitened = (mix * doubled).astype(bf)
    routed = jnp.dot(choose[...], whitened, preferred_element_type=jnp.float32)
    for p in range(n_dp):
        outgoing[p] = routed[p * capacity : (p + 1) * capacity].astype(bf)
    sixth = [send(outgoing.at[p], out_ref.at[i], ts.at[e], tr.at[e], (p, j)) for e, p in enumerate(planes)]
    kept = pltpu.make_async_copy(outgoing.at[i], out_ref.at[i], h_sem.at[0])
    kept.start()
    kept.wait()
    for copy in sixth:
        copy.wait_recv()

    for copy in pending[kept_up:]:
        copy.wait_send()


def encode(hidden, lengths, norm_gain, up, down, pool_gain, proj, owners, n_dp, n_fsdp):
    tok_rows, width = hidden.shape
    pass_rows = lengths.shape[0]
    nz = n_fsdp // 2
    ff_rows = down.shape[0]
    d_rows, emb = proj.shape
    half = nz * pass_rows
    wide = -(-ff_rows // LANES)
    chunks = nz * wide
    subs = chunks // PLANE
    legs = [len([s for s in range(subs) if s % 3 == r]) for r in range(3)]
    if up.shape[1] != 2 * chunks * LANES:
        up = jnp.pad(
            up.reshape(up.shape[0], n_fsdp, ff_rows), ((0, 0), (0, 0), (0, wide * LANES - ff_rows))
        ).reshape(up.shape[0], n_fsdp * wide * LANES)
    capacity = 2 * pass_rows // n_dp
    side = min(emb, n_dp * n_fsdp * pass_rows)
    bf = jnp.bfloat16
    f32 = jnp.float32
    dma = pltpu.SemaphoreType.DMA
    hbm = pl.BlockSpec(memory_space=pl.ANY)
    in_z = (subs + legs[2]) * nz
    return pl.pallas_call(
        functools.partial(embed_kernel, n_dp, n_fsdp, width),
        out_shape=jax.ShapeDtypeStruct((n_dp, capacity, emb), bf),
        in_specs=[hbm] * 8,
        out_specs=hbm,
        scratch_shapes=[
            pltpu.VMEM((tok_rows, width), bf),
            pltpu.VMEM((2, tok_rows, width), bf),
            pltpu.VMEM((chunks, width, LANES), bf),
            pltpu.VMEM((2, ff_rows, width), bf),
            pltpu.VMEM((nz, 2 * d_rows, emb), bf),
            pltpu.VMEM((nz, 2, pass_rows, wide * LANES), bf),
            pltpu.VMEM((2, nz, pass_rows, wide * LANES), bf),
            pltpu.VMEM((half, width), f32),
            pltpu.VMEM((2, nz, pass_rows, width // 2), bf),
            pltpu.VMEM((2, nz, pass_rows, width // 2), bf),
            pltpu.VMEM((n_dp, 2, nz, pass_rows, emb), bf),
            pltpu.VMEM((side, side), f32),
            pltpu.VMEM((n_dp, capacity, emb), bf),
            pltpu.VMEM((n_dp * capacity, pass_rows), bf),
            pltpu.VMEM((pass_rows, LANES), f32),
            pltpu.SMEM((pass_rows,), jnp.int32),
            pltpu.SMEM((pass_rows,), jnp.int32),
            pltpu.VMEM((width,), f32),
            pltpu.VMEM((width,), f32),
            dma((5,)),
            dma((chunks,)),
            dma((chunks,)),
            dma((chunks,)),
            dma((in_z,)),
            dma((in_z,)),
            dma((in_z // nz * len(HOPS) * 2,)),
            dma((in_z,)),
            dma(((subs + legs[0]) * nz,)),
            dma(((subs + legs[0]) * nz,)),
            dma(((subs + legs[1]) * nz,)),
            dma(((subs + legs[1]) * nz,)),
            dma,
            dma,
            dma((2,)),
            dma((2,)),
            dma((2,)),
            dma((n_fsdp,)),
            dma((n_fsdp,)),
        ]
        + [dma((2 * nz,))] * 2
        + [dma((nz,))] * 2
        + [dma((3 * nz,))] * 2
        + [dma((nz,))] * 4
        + [dma((max(3 * nz, n_dp),))] * 2
        + [dma((n_dp,))] * 2
        + [dma((n_dp - 1,))] * 2,
        compiler_params=pltpu.CompilerParams(
            collective_id=0, has_side_effects=True, vmem_limit_bytes=60 * 1024 * 1024
        ),
        name="embed",
    )(hidden, lengths, norm_gain, up, down, pool_gain, proj, owners)


def on_device(hidden, lengths, norm_gain, up_weight, down_weight, pool_gain, proj_weight, owners):
    n_dp, n_fsdp = lax.axis_size("dp"), lax.axis_size("fsdp")
    owned = encode(
        hidden, lengths, norm_gain, up_weight, down_weight, pool_gain, proj_weight,
        owners.reshape(-1), n_dp, n_fsdp,
    )
    return owned.reshape(-1, owned.shape[2])


def solution(mesh):
    placed = (
        P(("dp", "fsdp"), None),
        P(("dp", "fsdp")),
        P(),
        P("fsdp", None),
        P("fsdp", None),
        P(),
        P("fsdp", None),
        P(("dp", "fsdp"), None),
    )
    return jax.shard_map(
        on_device, mesh=mesh, in_specs=placed, out_specs=P(("dp", "fsdp"), None), check_vma=False
    )
```

```python
import functools

import jax
import jax.numpy as jnp
from jax import lax
from jax.experimental import pallas as pl
from jax.experimental.pallas import tpu as pltpu
from jax.sharding import PartitionSpec as P

RIDGE_TERM = 1.0
EPSILON = 1e-06
MESH = pl.DeviceIdType.MESH
PLANE = 4
LANES = 128
LAG = 4
RELAY_LAG = 4
REACH = 1
HOPS = (1, -1)


def remote(src, dst, send, recv, device):
    return pltpu.make_async_remote_copy(
        src_ref=src, dst_ref=dst, send_sem=send, recv_sem=recv, device_id=device, device_id_type=MESH
    )


def meet(devices):
    barrier = pltpu.get_barrier_semaphore()
    for device in devices:
        pl.semaphore_signal(barrier, inc=1, device_id=device, device_id_type=MESH)
    return barrier


def gelu(v):
    return 0.5 * v * (1.0 + jnp.tanh(0.7978845608028654 * (v + 0.044715 * (v * v * v))))


def nearest(nz):
    return [sorted((l for l in range(nz) if l != v), key=lambda l: (abs(l - v), l)) for v in range(nz)]


def pick(index, table):
    value = table[0]
    for v in range(1, len(table)):
        value = jnp.where(index == v, table[v], value)
    return value


def embed_kernel(
    n_dp, n_fsdp, width,
    hid_ref, len_hbm, ngain_hbm, up_ref, down_ref, pgain_hbm, proj_ref, own_hbm,
    out_ref,
    hid, nrm, upb, down2, pj, sa, ra, hs, s2, r2, every, u1, outgoing, choose, sizes,
    len_ref, own_ref, ngain_ref, pgain_ref,
    h_sem, lo_sem, ps, pr, zu, zd, zo, zr, xs, xr, ys, yr, ns, nr,
    dl, dns, dnr, as_, ar, s2s, r2s, s3s, r3s, js, jr, ks, kr, es, er, fs, fr, qs, qr, ts, tr,
):
    i = lax.axis_index("dp")
    j = lax.axis_index("fsdp")
    nz = n_fsdp // 2
    z = j // 2
    c = j % 2
    q = i % PLANE
    base = i - q
    rows = up_ref.shape[0]
    level_rows = 2 * rows
    chunks = upb.shape[0]
    subs = chunks // PLANE
    wide = chunks // nz
    per = subs // wide
    pass_rows, seq = hs.shape[0] // nz, hid.shape[0] // (hs.shape[0] // nz)
    half = nz * pass_rows
    ff_rows = down_ref.shape[0]
    emb = proj_ref.shape[1]
    d_rows = proj_ref.shape[0]
    part_rows = 2 * d_rows // PLANE
    qx = q + 1 - 2 * (q % 2)
    qy = q + 2 - 4 * (q // 2)
    qd = 3 - q
    partner = (i, z * 2 + 1 - c)
    near_x = (base + qx, j)
    near_y = (base + qy, j)
    peers = [(j + d) % n_fsdp for d in range(1, n_fsdp)]
    levels = [(z + d) % nz for d in range(1, nz)]
    planes = [(i + e) % n_dp for e in range(1, n_dp)]
    order = nearest(nz)
    near = [pick(z, [order[v][s] for v in range(nz)]) for s in range(nz - 1)]
    pending = []

    def along(level):
        return (i, level * 2 + c)

    def send(src, dst, ssem, rsem, device):
        copy = remote(src, dst, ssem, rsem, device)
        copy.start()
        pending.append(copy)
        return copy

    barrier = meet([(i, p) for p in peers] + [(p, j) for p in planes])

    own_k = [q * subs + s for s in range(subs)]
    x_k = [qx * subs + s for s in range(subs)]
    y_k = [qy * subs + s for s in range(subs)]
    d_k = [qd * subs + s for s in range(subs)]
    by_x = [s for s in range(subs) if s % 3 == 0]
    by_y = [s for s in range(subs) if s % 3 == 1]
    by_z = [s for s in range(subs) if s % 3 == 2]
    z_k = own_k + [d_k[s] for s in by_z]
    first = z_k + x_k + y_k + [d_k[s] for s in by_x + by_y]

    def source(core, k):
        at = ((k // wide * 2 + core) * wide + k % wide) * LANES
        return up_ref.at[:, pl.ds(pl.multiple_of(at, LANES), LANES)]

    def mine(k):
        return upb.at[k, pl.ds(pl.multiple_of(j * rows, rows), rows), :]

    def piece(k, level):
        return upb.at[k, pl.ds(pl.multiple_of(level * level_rows, level_rows), level_rows), :]

    local = []
    for n, k in enumerate(first):
        copy = pltpu.make_async_copy(source(c, k), mine(k), lo_sem.at[n])
        copy.start()
        local.append(copy)
    staged = [(hid_ref, hid), (ngain_hbm, ngain_ref), (len_hbm, len_ref), (own_hbm, own_ref), (pgain_hbm, pgain_ref)]
    staged = [pltpu.make_async_copy(src, dst, h_sem.at[n]) for n, (src, dst) in enumerate(staged)]
    for copy in staged:
        copy.start()
    pl.semaphore_wait(barrier, len(peers) + len(planes))
    swapped = []

    def swap(n):
        swapped.append(send(source(1 - c, first[n]), mine(first[n]), ps.at[n], pr.at[n], partner))

    def z_copy(t, level, hop):
        part = piece(z_k[t], level)
        sems = zu if hop == 1 else zd
        return remote(part, part, sems.at[t * nz + level], zr.at[t * nz + level], along(z + hop))

    def reaches(hop):
        return z + hop < nz if hop > 0 else z + hop >= 0

    def relays(level, hop):
        beyond = level <= z - REACH if hop > 0 else level >= z + REACH
        return jnp.logical_and(beyond, reaches(hop))

    def first_hop(t, h, e):
        core = c if e == 0 else 1 - c
        at = (t * len(HOPS) + h) * 2 + e
        return remote(
            source(core, z_k[t]), mine(z_k[t]), zo.at[at], zr.at[t * nz + z],
            (i, (z + HOPS[h]) * 2 + core),
        )

    def start_z(t):
        for h, hop in enumerate(HOPS):

            @pl.when(reaches(hop))
            def _():
                first_hop(t, h, 0).start()
                first_hop(t, h, 1).start()

    start_z(0)
    start_z(1)
    for n in range(chunks):
        swap(n)
    def proj_rows():
        return pj.at[z, pl.ds(pl.multiple_of(c * d_rows, d_rows), d_rows), :]

    def proj_part(level, plane):
        return pj.at[
            level,
            pl.ds(pl.multiple_of(plane * part_rows, part_rows), part_rows),
            pl.ds(pl.multiple_of(c * (emb // 2), emb // 2), emb // 2),
        ]

    def proj_side(level):
        return pj.at[level, :, pl.ds(pl.multiple_of(c * (emb // 2), emb // 2), emb // 2)]

    down_copy = pltpu.make_async_copy(down_ref, down2.at[c], dl.at[0])
    down_copy.start()
    proj_copy = pltpu.make_async_copy(proj_ref, proj_rows(), dl.at[1])
    proj_copy.start()
    for copy in staged:
        copy.wait()
    gain = ngain_ref[...].reshape(1, width)
    hs[...] = jnp.zeros_like(hs)

    def norm_block(p, carry):
        at = pl.ds(pl.multiple_of(p * seq, seq), seq)
        x = hid[at, :].astype(jnp.float32)
        keep = lax.broadcasted_iota(jnp.int32, (seq, 1), 0) < len_ref[p]
        scale = lax.rsqrt(jnp.sum(x * x, axis=1, keepdims=True) / width + EPSILON)
        scale = jnp.where(keep, scale, 0.0)
        nrm[c, at, :] = (x * scale * gain).astype(nrm.dtype)
        total = jnp.sum(jnp.where(keep, x, 0.0), axis=0, keepdims=True)
        hs[pl.ds(z * pass_rows + p, 1), :] = total
        return carry

    lax.fori_loop(0, pass_rows, norm_block, 0)
    nrm_copy = send(nrm.at[c], nrm.at[c], ns, nr, partner)
    down_swap = send(down_ref, down2.at[c], dns.at[0], dnr.at[0], partner)
    proj_swap = send(proj_ref, proj_rows(), dns.at[1], dnr.at[1], partner)
    row = lax.broadcasted_iota(jnp.int32, (pass_rows, LANES), 0)
    counts = jnp.zeros((pass_rows, LANES), jnp.float32)
    for p in range(pass_rows):
        counts = jnp.where(row == p, len_ref[p].astype(jnp.float32), counts)
    sizes[...] = counts
    capacity = outgoing.shape[1]
    targets = []
    for p in range(pass_rows):
        earlier = [(own_ref[p] == own_ref[o]).astype(jnp.int32) for o in range(p)]
        targets.append(own_ref[p] * capacity + sum(earlier))
    slot_at = lax.broadcasted_iota(jnp.int32, (n_dp * capacity, pass_rows), 0)
    pass_at = lax.broadcasted_iota(jnp.int32, (n_dp * capacity, pass_rows), 1)
    wanted = jnp.full((n_dp * capacity, pass_rows), -1, jnp.int32)
    for p in range(pass_rows):
        wanted = jnp.where(pass_at == p, targets[p], wanted)
    choose[...] = (slot_at == wanted).astype(jnp.float32).astype(choose.dtype)


    def along_x(slot, k, level):
        part = piece(k, level)
        return send(part, part, xs.at[slot * nz + level], xr.at[slot * nz + level], near_x)

    def along_y(slot, k, level):
        part = piece(k, level)
        return send(part, part, ys.at[slot * nz + level], yr.at[slot * nz + level], near_y)

    done = []
    x_sent, y_sent, x_relay, y_relay = {}, {}, {}, {}

    def z_step(t, s):
        level = near[s]
        z_copy(t, level, 1).wait_recv()
        for hop in (1, -1):

            @pl.when(relays(level, hop))
            def _():
                z_copy(t, level, hop).start()

        if t < subs:
            x_sent[t, s] = along_x(t, own_k[t], level)
            y_sent[t, s] = along_y(t, own_k[t], level)

    def xy_step(t, s):
        level = near[s]
        x_sent[t, s].wait_recv()
        y_sent[t, s].wait_recv()
        if t in by_x:
            x_relay[t, s] = along_x(subs + by_x.index(t), y_k[t], level)
        if t in by_y:
            y_relay[t, s] = along_y(subs + by_y.index(t), x_k[t], level)

    def compute(items):
        def slot(core, carry):
            block = [upb[quarter * subs + s] for quarter, s in items]
            block = jnp.concatenate(block, axis=1) if len(block) > 1 else block[0]
            pre = jnp.dot(nrm[core], block, preferred_element_type=jnp.float32)
            total = jnp.sum(gelu(pre).reshape(pass_rows, seq, block.shape[1]), axis=1)
            for n, (quarter, s) in enumerate(items):
                o = s % wide
                sa[quarter * per + s // wide, core, :, o * LANES : (o + 1) * LANES] = total[
                    :, n * LANES : (n + 1) * LANES
                ].astype(sa.dtype)
            return carry

        lax.fori_loop(0, 2, slot, 0)

    def act_copy(v, e):
        core = c if e == 0 else 1 - c
        return remote(
            sa.at[v, core], ra.at[c, z], as_.at[v * 2 + e], ar.at[c * nz + z], (i, v * 2 + core)
        )

    def send_acts(quarter):
        for b in range(per):
            v = quarter * per + b

            @pl.when(v == z)
            def _():
                ra[c, z] = sa[v, c]

            @pl.when(v != z)
            def _():
                act_copy(v, 0).start()

            act_copy(v, 1).start()

    def proj_out(v):
        return remote(proj_part(z, q), proj_part(z, q), s3s.at[v], r3s.at[z], along(v))

    ready = []
    left = {}

    def run(least):
        if len(ready) < least:
            return
        batch = [ready.pop(0) for _ in range(min(2, len(ready)))]
        compute([(quarter, s) for _, quarter, s in batch])
        for name, quarter, _ in batch:
            left[name] = left.get(name, subs) - 1
            if left[name] == 0:
                send_acts(quarter)

    last_slot = nz - 2
    z_steps = [(t, s) for t in range(len(z_k)) for s in range(nz - 1)]
    xy_steps = [(t, s) for t in range(subs) for s in range(nz - 1)]
    ends = [("x", t, s) for t in by_x for s in range(nz - 1)] + [("y", t, s) for t in by_y for s in range(nz - 1)]
    ends = sorted(ends, key=lambda r: (r[1], r[2]))
    at_step = {r: r[1] * (nz - 1) + r[2] + LAG + RELAY_LAG for r in ends}
    started = 2
    for n in range(max([len(z_steps), len(xy_steps) + LAG] + [m + 1 for m in at_step.values()])):
        if n == subs * (nz - 1):
            proj_copy.wait()
            proj_swap.wait_recv()
            for v in levels:
                copy = proj_out(v)
                copy.start()
                pending.append(copy)
        if n < len(z_steps):
            t, s = z_steps[n]
            z_step(t, s)
            if s == last_slot:
                if started < len(z_k):
                    start_z(started)
                    started += 1
                local[t].wait()
                swapped[t].wait_recv()
                ready.append(("own", q, t) if t < subs else ("diag", qd, by_z[t - subs]))
        if 0 <= n - LAG < len(xy_steps):
            t, s = xy_steps[n - LAG]
            xy_step(t, s)
            if s == last_slot:
                if t == 0:
                    for copy, arrived in list(zip(local, swapped))[len(z_k) :]:
                        copy.wait()
                        arrived.wait_recv()
                ready.append(("x", qx, t))
                ready.append(("y", qy, t))
        for kind, t, s in ends:
            if at_step[kind, t, s] == n:
                (x_relay if kind == "x" else y_relay)[t, s].wait_recv()
                if s == last_slot:
                    ready.append(("diag", qd, t))
        if n == nz - 1:
            nrm_copy.wait_recv()
        if n >= nz - 1:
            run(2)
    while ready:
        run(1)

    beside = [(qx, near_x), (qy, near_y), (qd, (base + qd, j))]
    proj_sent = {}
    sent_up = len(pending)
    for e, v in enumerate(near):
        remote(proj_part(v, q), proj_part(v, q), s3s.at[v], r3s.at[v], along(v)).wait_recv()
        for n in range(2):
            at = n * nz + v
            proj_sent[n, e] = send(
                proj_part(v, q), proj_part(v, q), js.at[at], jr.at[at], beside[n][1]
            )

    down_copy.wait()
    down_swap.wait_recv()
    for v in range(nz):
        for e in range(2):
            core = c if e == 0 else 1 - c
            arrival = remote(
                sa.at[v, core], ra.at[core, v], as_.at[v * 2 + e], ar.at[core * nz + v], partner
            )
            if e == 0:

                @pl.when(v != z)
                def _():
                    arrival.wait_recv()

            else:
                arrival.wait_recv()

    acts = [ra[core].reshape(half, wide * LANES)[:, :ff_rows] for core in range(2)]

    def part_copy(b, v):
        return remote(s2.at[b, v], r2.at[b, z], s2s.at[b * nz + v], r2s.at[b * nz + z], along(v))

    def part_from(b, v):
        return remote(s2.at[b, v], r2.at[b, v], s2s.at[b * nz + v], r2s.at[b * nz + v], along(v))

    for b in range(2):
        at = slice(b * (width // 2), (b + 1) * (width // 2))
        part = hs[:, at]
        for core in range(2):
            part = part + jnp.dot(acts[core], down2[core, :, at], preferred_element_type=jnp.float32)
        s2[b] = part.astype(s2.dtype).reshape(nz, pass_rows, width // 2)
        for v in range(nz):

            @pl.when(v != z)
            def _():
                part_copy(b, v).start()

    for copy in pending[:sent_up]:
        copy.wait_send()
    for t in range(len(z_k)):
        for h, hop in enumerate(HOPS):

            @pl.when(reaches(hop))
            def _():
                first_hop(t, h, 0).wait_send()
                first_hop(t, h, 1).wait_send()

        for level in range(nz):
            for hop in (1, -1):

                @pl.when(relays(level, hop))
                def _():
                    z_copy(t, level, hop).wait_send()

    for v in range(nz):

        @pl.when(v != z)
        def _():
            act_copy(v, 0).wait_send()

        act_copy(v, 1).wait_send()

    proj_last = []
    for e, v in enumerate(near):
        for n in range(2):
            proj_sent[n, e].wait_recv()
        part = proj_part(v, beside[e % 2][0])
        at = 2 * nz + v
        proj_sent[2, e] = send(part, part, js.at[at], jr.at[at], beside[1 - e % 2][1])
    for e, v in enumerate(near):
        proj_sent[2, e].wait_recv()
        proj_last.append(send(proj_side(v), proj_side(v), ks.at[v], kr.at[v], partner))
    halves = []
    for b in range(2):
        total = s2[b, z].astype(jnp.float32)
        for v in near:
            part_from(b, v).wait_recv()
            total = total + r2[b, v].astype(jnp.float32)
        halves.append(total)
    pooled = jnp.concatenate(halves, axis=1)
    counts = sizes[:, :1]
    norm = jnp.sum(pooled * pooled, axis=1, keepdims=True) / width
    scaled = pooled * lax.rsqrt(norm + EPSILON * (counts * counts)) * pgain_ref[...].reshape(1, width)
    scaled = scaled.astype(proj_ref.dtype)
    for copy in proj_last:
        copy.wait_recv()
    embedded = jnp.dot(scaled, pj[...].reshape(width, emb), preferred_element_type=jnp.float32)
    every[i, c, z] = embedded.astype(every.dtype)

    def to_level(v):
        part = every.at[i, c, z]
        return remote(part, part, es.at[v], er.at[z], along(v))

    def from_level(v):
        part = every.at[i, c, v]
        return remote(part, part, es.at[v], er.at[v], along(v))

    for v in levels:
        copy = to_level(v)
        copy.start()
        pending.append(copy)
    last = []

    def to_partner(part, n):
        last.append(send(part, part, qs.at[n], qr.at[n], partner))

    if n_dp == PLANE:
        seen = [z] + near
        across = {}
        for e in range(nz):
            if e > 0:
                from_level(seen[e]).wait_recv()
            part = every.at[i, c, seen[e]]
            for n, (_, device) in enumerate(beside):
                at = n * nz + seen[e]
                across[n, e] = send(part, part, fs.at[at], fr.at[at], device)
        to_partner(every.at[i, c], 0)
        for n, (plane, _) in enumerate(beside):
            for e in range(nz):
                across[n, e].wait_recv()
            to_partner(every.at[plane, c], n + 1)
    else:
        for v in levels:
            from_level(v).wait_recv()
        part = every.at[i, c]
        fifth = [send(part, part, fs.at[e], fr.at[e], (p, j)) for e, p in enumerate(planes)]
        to_partner(part, 0)
        for e, copy in enumerate(fifth):
            copy.wait_recv()
            to_partner(every.at[(i + n_dp - e - 1) % n_dp, c], e + 1)

    for b in range(2):
        for v in range(nz):

            @pl.when(v != z)
            def _():
                part_copy(b, v).wait_send()

    for copy in last:
        copy.wait_recv()
    for copy in pending[sent_up:]:
        copy.wait_send()
    kept_up = len(pending)

    bf = jnp.bfloat16
    n_rows = n_dp * n_fsdp * pass_rows
    mark = ((i * 2 + c) * nz + z) * pass_rows
    rounded = every[i, c, z].astype(jnp.float32)

    def mul(a, b):
        return jnp.dot(a.astype(bf), b, preferred_element_type=jnp.float32)

    def mul2(a, b):
        high = a.astype(bf)
        return mul(high, b) + mul(a - high.astype(jnp.float32), b)

    def eye(n):
        at = lax.broadcasted_iota(jnp.int32, (n, n), 0)
        return (at == lax.broadcasted_iota(jnp.int32, (n, n), 1)).astype(jnp.float32)

    if n_rows < emb:
        rows_all = every[...].reshape(n_rows, emb)
        average = jnp.sum(rows_all.astype(jnp.float32), axis=0, keepdims=True) / n_rows
        gram = lax.dot_general(
            rows_all, rows_all, (((1,), (1,)), ((), ())), preferred_element_type=jnp.float32
        ) / n_rows
        by_col = jnp.mean(gram, axis=0, keepdims=True)
        by_row = jnp.mean(gram, axis=1, keepdims=True)
        ridged = gram - by_col - by_row + jnp.mean(by_col) + RIDGE_TERM * eye(n_rows)
        squared = jnp.sum(ridged * ridged) + RIDGE_TERM * RIDGE_TERM * (emb - n_rows)
    else:
        def add(b, carry):
            part = every[b // 2, b % 2].reshape(half, emb)
            moment = lax.dot_general(
                part, part, (((0,), (0,)), ((), ())), preferred_element_type=jnp.float32
            )
            u1[...] += moment
            return carry + jnp.sum(part.astype(jnp.float32), axis=0, keepdims=True)

        u1[...] = jnp.zeros_like(u1)
        average = lax.fori_loop(0, n_dp * 2, add, jnp.zeros((1, emb), jnp.float32)) / n_rows
        tall = jnp.transpose(jnp.broadcast_to(average, (emb, emb)))
        ridged = u1[...] / n_rows - tall * average + RIDGE_TERM * eye(emb)
        squared = jnp.sum(ridged * ridged)
    doubled = 2.0 * lax.rsqrt(squared)
    t1 = ridged * doubled
    u1[...] = t1
    t1b = t1.astype(bf)
    t2 = 2.0 * t1 - mul(t1, t1b)
    t2b = t2.astype(bf)
    t4 = 2.0 * t2 - mul(t2, t2b)
    t4b = t4.astype(bf)
    if n_rows < emb:
        lane = lax.broadcasted_iota(jnp.int32, (pass_rows, n_rows), 1)
        here = (lane == mark + lax.broadcasted_iota(jnp.int32, (pass_rows, n_rows), 0)).astype(jnp.float32)
        mix = 2.0 * here - u1[pl.ds(pl.multiple_of(mark, pass_rows), pass_rows), :]
        times = mul
    else:
        mix = embedded - average
        mix = 2.0 * mix - mul2(mix, t1b)
        times = mul2
    mix = 2.0 * mix - times(mix, t2b)
    mix = 2.0 * mix - times(mix, t4b)
    rest = mix - times(mix, t4b)
    mix = mix + (rest - times(rest, t4b))
    if n_rows < emb:
        mixed = mul2(mix, rows_all) - jnp.sum(mix, axis=1, keepdims=True) * average
        mix = mixed + jnp.sum(mix * here, axis=1, keepdims=True) * (embedded - rounded)
    whitened = (mix * doubled).astype(bf)
    routed = jnp.dot(choose[...], whitened, preferred_element_type=jnp.float32)
    for p in range(n_dp):
        outgoing[p] = routed[p * capacity : (p + 1) * capacity].astype(bf)
    sixth = [send(outgoing.at[p], out_ref.at[i], ts.at[e], tr.at[e], (p, j)) for e, p in enumerate(planes)]
    kept = pltpu.make_async_copy(outgoing.at[i], out_ref.at[i], h_sem.at[0])
    kept.start()
    kept.wait()
    for copy in sixth:
        copy.wait_recv()

    for copy in pending[kept_up:]:
        copy.wait_send()


def encode(hidden, lengths, norm_gain, up, down, pool_gain, proj, owners, n_dp, n_fsdp):
    tok_rows, width = hidden.shape
    pass_rows = lengths.shape[0]
    nz = n_fsdp // 2
    ff_rows = down.shape[0]
    d_rows, emb = proj.shape
    half = nz * pass_rows
    wide = -(-ff_rows // LANES)
    chunks = nz * wide
    subs = chunks // PLANE
    legs = [len([s for s in range(subs) if s % 3 == r]) for r in range(3)]
    if up.shape[1] != 2 * chunks * LANES:
        up = jnp.pad(
            up.reshape(up.shape[0], n_fsdp, ff_rows), ((0, 0), (0, 0), (0, wide * LANES - ff_rows))
        ).reshape(up.shape[0], n_fsdp * wide * LANES)
    capacity = 2 * pass_rows // n_dp
    side = min(emb, n_dp * n_fsdp * pass_rows)
    bf = jnp.bfloat16
    f32 = jnp.float32
    dma = pltpu.SemaphoreType.DMA
    hbm = pl.BlockSpec(memory_space=pl.ANY)
    in_z = (subs + legs[2]) * nz
    return pl.pallas_call(
        functools.partial(embed_kernel, n_dp, n_fsdp, width),
        out_shape=jax.ShapeDtypeStruct((n_dp, capacity, emb), bf),
        in_specs=[hbm] * 8,
        out_specs=hbm,
        scratch_shapes=[
            pltpu.VMEM((tok_rows, width), bf),
            pltpu.VMEM((2, tok_rows, width), bf),
            pltpu.VMEM((chunks, width, LANES), bf),
            pltpu.VMEM((2, ff_rows, width), bf),
            pltpu.VMEM((nz, 2 * d_rows, emb), bf),
            pltpu.VMEM((nz, 2, pass_rows, wide * LANES), bf),
            pltpu.VMEM((2, nz, pass_rows, wide * LANES), bf),
            pltpu.VMEM((half, width), f32),
            pltpu.VMEM((2, nz, pass_rows, width // 2), bf),
            pltpu.VMEM((2, nz, pass_rows, width // 2), bf),
            pltpu.VMEM((n_dp, 2, nz, pass_rows, emb), bf),
            pltpu.VMEM((side, side), f32),
            pltpu.VMEM((n_dp, capacity, emb), bf),
            pltpu.VMEM((n_dp * capacity, pass_rows), bf),
            pltpu.VMEM((pass_rows, LANES), f32),
            pltpu.SMEM((pass_rows,), jnp.int32),
            pltpu.SMEM((pass_rows,), jnp.int32),
            pltpu.VMEM((width,), f32),
            pltpu.VMEM((width,), f32),
            dma((5,)),
            dma((chunks,)),
            dma((chunks,)),
            dma((chunks,)),
            dma((in_z,)),
            dma((in_z,)),
            dma((in_z // nz * len(HOPS) * 2,)),
            dma((in_z,)),
            dma(((subs + legs[0]) * nz,)),
            dma(((subs + legs[0]) * nz,)),
            dma(((subs + legs[1]) * nz,)),
            dma(((subs + legs[1]) * nz,)),
            dma,
            dma,
            dma((2,)),
            dma((2,)),
            dma((2,)),
            dma((n_fsdp,)),
            dma((n_fsdp,)),
        ]
        + [dma((2 * nz,))] * 2
        + [dma((nz,))] * 2
        + [dma((3 * nz,))] * 2
        + [dma((nz,))] * 4
        + [dma((max(3 * nz, n_dp),))] * 2
        + [dma((n_dp,))] * 2
        + [dma((n_dp - 1,))] * 2,
        compiler_params=pltpu.CompilerParams(
            collective_id=0, has_side_effects=True, vmem_limit_bytes=60 * 1024 * 1024
        ),
        name="embed",
    )(hidden, lengths, norm_gain, up, down, pool_gain, proj, owners)


def on_device(hidden, lengths, norm_gain, up_weight, down_weight, pool_gain, proj_weight, owners):
    n_dp, n_fsdp = lax.axis_size("dp"), lax.axis_size("fsdp")
    owned = encode(
        hidden, lengths, norm_gain, up_weight, down_weight, pool_gain, proj_weight,
        owners.reshape(-1), n_dp, n_fsdp,
    )
    return owned.reshape(-1, owned.shape[2])


def solution(mesh):
    placed = (
        P(("dp", "fsdp"), None),
        P(("dp", "fsdp")),
        P(),
        P("fsdp", None),
        P("fsdp", None),
        P(),
        P("fsdp", None),
        P(("dp", "fsdp"), None),
    )
    return jax.shard_map(
        on_device, mesh=mesh, in_specs=placed, out_specs=P(("dp", "fsdp"), None), check_vma=False
    )
```

```python
import functools

import jax
import jax.numpy as jnp
from jax import lax
from jax.experimental import pallas as pl
from jax.experimental.pallas import tpu as pltpu
from jax.sharding import PartitionSpec as P

RIDGE_TERM = 1.0
EPSILON = 1e-06
MESH = pl.DeviceIdType.MESH
PLANE = 4
LANES = 128
LAG = 4
RELAY_LAG = 4
REACH = 1
HOPS = (1, -1)


def remote(src, dst, send, recv, device):
    return pltpu.make_async_remote_copy(
        src_ref=src, dst_ref=dst, send_sem=send, recv_sem=recv, device_id=device, device_id_type=MESH
    )


def meet(devices):
    barrier = pltpu.get_barrier_semaphore()
    for device in devices:
        pl.semaphore_signal(barrier, inc=1, device_id=device, device_id_type=MESH)
    return barrier


def gelu(v):
    return 0.5 * v * (1.0 + jnp.tanh(0.7978845608028654 * (v + 0.044715 * (v * v * v))))


def nearest(nz):
    return [sorted((l for l in range(nz) if l != v), key=lambda l: (abs(l - v), l)) for v in range(nz)]


def pick(index, table):
    value = table[0]
    for v in range(1, len(table)):
        value = jnp.where(index == v, table[v], value)
    return value


def embed_kernel(
    n_dp, n_fsdp, width,
    hid_ref, len_hbm, ngain_hbm, up_ref, down_ref, pgain_hbm, proj_ref, own_hbm,
    out_ref,
    hid, nrm, upb, down2, pj, sa, ra, hs, s2, r2, every, u1, outgoing, choose, sizes,
    len_ref, own_ref, ngain_ref, pgain_ref,
    h_sem, lo_sem, ps, pr, zu, zd, zo, zr, xs, xr, ys, yr, ns, nr,
    dl, dns, dnr, as_, ar, s2s, r2s, s3s, r3s, js, jr, ks, kr, es, er, fs, fr, qs, qr, ts, tr,
):
    i = lax.axis_index("dp")
    j = lax.axis_index("fsdp")
    nz = n_fsdp // 2
    z = j // 2
    c = j % 2
    q = i % PLANE
    base = i - q
    rows = up_ref.shape[0]
    level_rows = 2 * rows
    chunks = upb.shape[0]
    subs = chunks // PLANE
    wide = chunks // nz
    per = subs // wide
    pass_rows, seq = hs.shape[0] // nz, hid.shape[0] // (hs.shape[0] // nz)
    half = nz * pass_rows
    ff_rows = down_ref.shape[0]
    emb = proj_ref.shape[1]
    d_rows = proj_ref.shape[0]
    part_rows = 2 * d_rows // PLANE
    qx = q + 1 - 2 * (q % 2)
    qy = q + 2 - 4 * (q // 2)
    qd = 3 - q
    partner = (i, z * 2 + 1 - c)
    near_x = (base + qx, j)
    near_y = (base + qy, j)
    peers = [(j + d) % n_fsdp for d in range(1, n_fsdp)]
    levels = [(z + d) % nz for d in range(1, nz)]
    planes = [(i + e) % n_dp for e in range(1, n_dp)]
    order = nearest(nz)
    near = [pick(z, [order[v][s] for v in range(nz)]) for s in range(nz - 1)]
    pending = []

    def along(level):
        return (i, level * 2 + c)

    def send(src, dst, ssem, rsem, device):
        copy = remote(src, dst, ssem, rsem, device)
        copy.start()
        pending.append(copy)
        return copy

    barrier = meet([(i, p) for p in peers] + [(p, j) for p in planes])

    own_k = [q * subs + s for s in range(subs)]
    x_k = [qx * subs + s for s in range(subs)]
    y_k = [qy * subs + s for s in range(subs)]
    d_k = [qd * subs + s for s in range(subs)]
    by_x = [s for s in range(subs) if s % 3 == 0]
    by_y = [s for s in range(subs) if s % 3 == 1]
    by_z = [s for s in range(subs) if s % 3 == 2]
    z_k = own_k + [d_k[s] for s in by_z]
    first = z_k + x_k + y_k + [d_k[s] for s in by_x + by_y]

    def source(core, k):
        at = ((k // wide * 2 + core) * wide + k % wide) * LANES
        return up_ref.at[:, pl.ds(pl.multiple_of(at, LANES), LANES)]

    def mine(k):
        return upb.at[k, pl.ds(pl.multiple_of(j * rows, rows), rows), :]

    def piece(k, level):
        return upb.at[k, pl.ds(pl.multiple_of(level * level_rows, level_rows), level_rows), :]

    local = []
    for n, k in enumerate(first):
        copy = pltpu.make_async_copy(source(c, k), mine(k), lo_sem.at[n])
        copy.start()
        local.append(copy)
    staged = [(hid_ref, hid), (ngain_hbm, ngain_ref), (len_hbm, len_ref), (own_hbm, own_ref), (pgain_hbm, pgain_ref)]
    staged = [pltpu.make_async_copy(src, dst, h_sem.at[n]) for n, (src, dst) in enumerate(staged)]
    for copy in staged:
        copy.start()
    pl.semaphore_wait(barrier, len(peers) + len(planes))
    swapped = []

    def swap(n):
        swapped.append(send(source(1 - c, first[n]), mine(first[n]), ps.at[n], pr.at[n], partner))

    def z_copy(t, level, hop):
        part = piece(z_k[t], level)
        sems = zu if hop == 1 else zd
        return remote(part, part, sems.at[t * nz + level], zr.at[t * nz + level], along(z + hop))

    def reaches(hop):
        return z + hop < nz if hop > 0 else z + hop >= 0

    def relays(level, hop):
        beyond = level <= z - REACH if hop > 0 else level >= z + REACH
        return jnp.logical_and(beyond, reaches(hop))

    def first_hop(t, h, e):
        core = c if e == 0 else 1 - c
        at = (t * len(HOPS) + h) * 2 + e
        return remote(
            source(core, z_k[t]), mine(z_k[t]), zo.at[at], zr.at[t * nz + z],
            (i, (z + HOPS[h]) * 2 + core),
        )

    def start_z(t):
        for h, hop in enumerate(HOPS):

            @pl.when(reaches(hop))
            def _():
                first_hop(t, h, 0).start()
                first_hop(t, h, 1).start()

    start_z(0)
    start_z(1)
    for n in range(chunks):
        swap(n)
    def proj_rows():
        return pj.at[z, pl.ds(pl.multiple_of(c * d_rows, d_rows), d_rows), :]

    def proj_part(level, plane):
        return pj.at[
            level,
            pl.ds(pl.multiple_of(plane * part_rows, part_rows), part_rows),
            pl.ds(pl.multiple_of(c * (emb // 2), emb // 2), emb // 2),
        ]

    def proj_side(level):
        return pj.at[level, :, pl.ds(pl.multiple_of(c * (emb // 2), emb // 2), emb // 2)]

    down_copy = pltpu.make_async_copy(down_ref, down2.at[c], dl.at[0])
    down_copy.start()
    proj_copy = pltpu.make_async_copy(proj_ref, proj_rows(), dl.at[1])
    proj_copy.start()
    for copy in staged:
        copy.wait()
    gain = ngain_ref[...].reshape(1, width)
    hs[...] = jnp.zeros_like(hs)

    def norm_block(p, carry):
        at = pl.ds(pl.multiple_of(p * seq, seq), seq)
        x = hid[at, :].astype(jnp.float32)
        keep = lax.broadcasted_iota(jnp.int32, (seq, 1), 0) < len_ref[p]
        scale = lax.rsqrt(jnp.sum(x * x, axis=1, keepdims=True) / width + EPSILON)
        scale = jnp.where(keep, scale, 0.0)
        nrm[c, at, :] = (x * scale * gain).astype(nrm.dtype)
        total = jnp.sum(jnp.where(keep, x, 0.0), axis=0, keepdims=True)
        hs[pl.ds(z * pass_rows + p, 1), :] = total
        return carry

    lax.fori_loop(0, pass_rows, norm_block, 0)
    nrm_copy = send(nrm.at[c], nrm.at[c], ns, nr, partner)
    down_swap = send(down_ref, down2.at[c], dns.at[0], dnr.at[0], partner)
    proj_swap = send(proj_ref, proj_rows(), dns.at[1], dnr.at[1], partner)
    row = lax.broadcasted_iota(jnp.int32, (pass_rows, LANES), 0)
    counts = jnp.zeros((pass_rows, LANES), jnp.float32)
    for p in range(pass_rows):
        counts = jnp.where(row == p, len_ref[p].astype(jnp.float32), counts)
    sizes[...] = counts
    capacity = outgoing.shape[1]
    targets = []
    for p in range(pass_rows):
        earlier = [(own_ref[p] == own_ref[o]).astype(jnp.int32) for o in range(p)]
        targets.append(own_ref[p] * capacity + sum(earlier))
    slot_at = lax.broadcasted_iota(jnp.int32, (n_dp * capacity, pass_rows), 0)
    pass_at = lax.broadcasted_iota(jnp.int32, (n_dp * capacity, pass_rows), 1)
    wanted = jnp.full((n_dp * capacity, pass_rows), -1, jnp.int32)
    for p in range(pass_rows):
        wanted = jnp.where(pass_at == p, targets[p], wanted)
    choose[...] = (slot_at == wanted).astype(jnp.float32).astype(choose.dtype)


    def along_x(slot, k, level):
        part = piece(k, level)
        return send(part, part, xs.at[slot * nz + level], xr.at[slot * nz + level], near_x)

    def along_y(slot, k, level):
        part = piece(k, level)
        return send(part, part, ys.at[slot * nz + level], yr.at[slot * nz + level], near_y)

    done = []
    x_sent, y_sent, x_relay, y_relay = {}, {}, {}, {}

    def z_step(t, s):
        level = near[s]
        z_copy(t, level, 1).wait_recv()
        for hop in (1, -1):

            @pl.when(relays(level, hop))
            def _():
                z_copy(t, level, hop).start()

        if t < subs:
            x_sent[t, s] = along_x(t, own_k[t], level)
            y_sent[t, s] = along_y(t, own_k[t], level)

    def xy_step(t, s):
        level = near[s]
        x_sent[t, s].wait_recv()
        y_sent[t, s].wait_recv()
        if t in by_x:
            x_relay[t, s] = along_x(subs + by_x.index(t), y_k[t], level)
        if t in by_y:
            y_relay[t, s] = along_y(subs + by_y.index(t), x_k[t], level)

    def compute(items):
        def slot(core, carry):
            block = [upb[quarter * subs + s] for quarter, s in items]
            block = jnp.concatenate(block, axis=1) if len(block) > 1 else block[0]
            pre = jnp.dot(nrm[core], block, preferred_element_type=jnp.float32)
            total = jnp.sum(gelu(pre).reshape(pass_rows, seq, block.shape[1]), axis=1)
            for n, (quarter, s) in enumerate(items):
                o = s % wide
                sa[quarter * per + s // wide, core, :, o * LANES : (o + 1) * LANES] = total[
                    :, n * LANES : (n + 1) * LANES
                ].astype(sa.dtype)
            return carry

        lax.fori_loop(0, 2, slot, 0)

    def act_copy(v, e):
        core = c if e == 0 else 1 - c
        return remote(
            sa.at[v, core], ra.at[c, z], as_.at[v * 2 + e], ar.at[c * nz + z], (i, v * 2 + core)
        )

    def send_acts(quarter):
        for b in range(per):
            v = quarter * per + b

            @pl.when(v == z)
            def _():
                ra[c, z] = sa[v, c]

            @pl.when(v != z)
            def _():
                act_copy(v, 0).start()

            act_copy(v, 1).start()

    def proj_out(v):
        return remote(proj_part(z, q), proj_part(z, q), s3s.at[v], r3s.at[z], along(v))

    ready = []
    left = {}

    def run(least):
        if len(ready) < least:
            return
        batch = [ready.pop(0) for _ in range(min(2, len(ready)))]
        compute([(quarter, s) for _, quarter, s in batch])
        for name, quarter, _ in batch:
            left[name] = left.get(name, subs) - 1
            if left[name] == 0:
                send_acts(quarter)

    last_slot = nz - 2
    z_steps = [(t, s) for t in range(len(z_k)) for s in range(nz - 1)]
    xy_steps = [(t, s) for t in range(subs) for s in range(nz - 1)]
    ends = [("x", t, s) for t in by_x for s in range(nz - 1)] + [("y", t, s) for t in by_y for s in range(nz - 1)]
    ends = sorted(ends, key=lambda r: (r[1], r[2]))
    at_step = {r: r[1] * (nz - 1) + r[2] + LAG + RELAY_LAG for r in ends}
    started = 2
    for n in range(max([len(z_steps), len(xy_steps) + LAG] + [m + 1 for m in at_step.values()])):
        if n == subs * (nz - 1):
            proj_copy.wait()
            proj_swap.wait_recv()
            for v in levels:
                copy = proj_out(v)
                copy.start()
                pending.append(copy)
        if n < len(z_steps):
            t, s = z_steps[n]
            z_step(t, s)
            if s == last_slot:
                if started < len(z_k):
                    start_z(started)
                    started += 1
                local[t].wait()
                swapped[t].wait_recv()
                ready.append(("own", q, t) if t < subs else ("diag", qd, by_z[t - subs]))
        if 0 <= n - LAG < len(xy_steps):
            t, s = xy_steps[n - LAG]
            xy_step(t, s)
            if s == last_slot:
                if t == 0:
                    for copy, arrived in list(zip(local, swapped))[len(z_k) :]:
                        copy.wait()
                        arrived.wait_recv()
                ready.append(("x", qx, t))
                ready.append(("y", qy, t))
        for kind, t, s in ends:
            if at_step[kind, t, s] == n:
                (x_relay if kind == "x" else y_relay)[t, s].wait_recv()
                if s == last_slot:
                    ready.append(("diag", qd, t))
        if n == nz - 1:
            nrm_copy.wait_recv()
        if n >= nz - 1:
            run(2)
    while ready:
        run(1)

    beside = [(qx, near_x), (qy, near_y), (qd, (base + qd, j))]
    proj_sent = {}
    sent_up = len(pending)
    for e, v in enumerate(near):
        remote(proj_part(v, q), proj_part(v, q), s3s.at[v], r3s.at[v], along(v)).wait_recv()
        for n in range(2):
            at = n * nz + v
            proj_sent[n, e] = send(
                proj_part(v, q), proj_part(v, q), js.at[at], jr.at[at], beside[n][1]
            )

    down_copy.wait()
    down_swap.wait_recv()
    for v in range(nz):
        for e in range(2):
            core = c if e == 0 else 1 - c
            arrival = remote(
                sa.at[v, core], ra.at[core, v], as_.at[v * 2 + e], ar.at[core * nz + v], partner
            )
            if e == 0:

                @pl.when(v != z)
                def _():
                    arrival.wait_recv()

            else:
                arrival.wait_recv()

    acts = [ra[core].reshape(half, wide * LANES)[:, :ff_rows] for core in range(2)]

    def part_copy(b, v):
        return remote(s2.at[b, v], r2.at[b, z], s2s.at[b * nz + v], r2s.at[b * nz + z], along(v))

    def part_from(b, v):
        return remote(s2.at[b, v], r2.at[b, v], s2s.at[b * nz + v], r2s.at[b * nz + v], along(v))

    for b in range(2):
        at = slice(b * (width // 2), (b + 1) * (width // 2))
        part = hs[:, at]
        for core in range(2):
            part = part + jnp.dot(acts[core], down2[core, :, at], preferred_element_type=jnp.float32)
        s2[b] = part.astype(s2.dtype).reshape(nz, pass_rows, width // 2)
        for v in range(nz):

            @pl.when(v != z)
            def _():
                part_copy(b, v).start()

    for copy in pending[:sent_up]:
        copy.wait_send()
    for t in range(len(z_k)):
        for h, hop in enumerate(HOPS):

            @pl.when(reaches(hop))
            def _():
                first_hop(t, h, 0).wait_send()
                first_hop(t, h, 1).wait_send()

        for level in range(nz):
            for hop in (1, -1):

                @pl.when(relays(level, hop))
                def _():
                    z_copy(t, level, hop).wait_send()

    for v in range(nz):

        @pl.when(v != z)
        def _():
            act_copy(v, 0).wait_send()

        act_copy(v, 1).wait_send()

    proj_last = []
    for e, v in enumerate(near):
        for n in range(2):
            proj_sent[n, e].wait_recv()
        part = proj_part(v, beside[e % 2][0])
        at = 2 * nz + v
        proj_sent[2, e] = send(part, part, js.at[at], jr.at[at], beside[1 - e % 2][1])
    for e, v in enumerate(near):
        proj_sent[2, e].wait_recv()
        proj_last.append(send(proj_side(v), proj_side(v), ks.at[v], kr.at[v], partner))
    halves = []
    for b in range(2):
        total = s2[b, z].astype(jnp.float32)
        for v in near:
            part_from(b, v).wait_recv()
            total = total + r2[b, v].astype(jnp.float32)
        halves.append(total)
    pooled = jnp.concatenate(halves, axis=1)
    counts = sizes[:, :1]
    norm = jnp.sum(pooled * pooled, axis=1, keepdims=True) / width
    scaled = pooled * lax.rsqrt(norm + EPSILON * (counts * counts)) * pgain_ref[...].reshape(1, width)
    scaled = scaled.astype(proj_ref.dtype)
    for copy in proj_last:
        copy.wait_recv()
    embedded = jnp.dot(scaled, pj[...].reshape(width, emb), preferred_element_type=jnp.float32)
    every[i, c, z] = embedded.astype(every.dtype)

    def to_level(v):
        part = every.at[i, c, z]
        return remote(part, part, es.at[v], er.at[z], along(v))

    def from_level(v):
        part = every.at[i, c, v]
        return remote(part, part, es.at[v], er.at[v], along(v))

    for v in levels:
        copy = to_level(v)
        copy.start()
        pending.append(copy)
    last = []

    def to_partner(part, n):
        last.append(send(part, part, qs.at[n], qr.at[n], partner))

    if n_dp == PLANE:
        seen = [z] + near
        across = {}
        for e in range(nz):
            if e > 0:
                from_level(seen[e]).wait_recv()
            part = every.at[i, c, seen[e]]
            for n, (_, device) in enumerate(beside):
                at = n * nz + seen[e]
                across[n, e] = send(part, part, fs.at[at], fr.at[at], device)
        to_partner(every.at[i, c], 0)
        for n, (plane, _) in enumerate(beside):
            for e in range(nz):
                across[n, e].wait_recv()
            to_partner(every.at[plane, c], n + 1)
    else:
        for v in levels:
            from_level(v).wait_recv()
        part = every.at[i, c]
        fifth = [send(part, part, fs.at[e], fr.at[e], (p, j)) for e, p in enumerate(planes)]
        to_partner(part, 0)
        for e, copy in enumerate(fifth):
            copy.wait_recv()
            to_partner(every.at[(i + n_dp - e - 1) % n_dp, c], e + 1)

    for b in range(2):
        for v in range(nz):

            @pl.when(v != z)
            def _():
                part_copy(b, v).wait_send()

    for copy in last:
        copy.wait_recv()
    for copy in pending[sent_up:]:
        copy.wait_send()
    kept_up = len(pending)

    bf = jnp.bfloat16
    n_rows = n_dp * n_fsdp * pass_rows
    mark = ((i * 2 + c) * nz + z) * pass_rows
    rounded = every[i, c, z].astype(jnp.float32)

    def mul(a, b):
        return jnp.dot(a.astype(bf), b, preferred_element_type=jnp.float32)

    def mul2(a, b):
        high = a.astype(bf)
        return mul(high, b) + mul(a - high.astype(jnp.float32), b)

    def eye(n):
        at = lax.broadcasted_iota(jnp.int32, (n, n), 0)
        return (at == lax.broadcasted_iota(jnp.int32, (n, n), 1)).astype(jnp.float32)

    if n_rows < emb:
        rows_all = every[...].reshape(n_rows, emb)
        average = jnp.sum(rows_all.astype(jnp.float32), axis=0, keepdims=True) / n_rows
        gram = lax.dot_general(
            rows_all, rows_all, (((1,), (1,)), ((), ())), preferred_element_type=jnp.float32
        ) / n_rows
        by_col = jnp.mean(gram, axis=0, keepdims=True)
        by_row = jnp.mean(gram, axis=1, keepdims=True)
        ridged = gram - by_col - by_row + jnp.mean(by_col) + RIDGE_TERM * eye(n_rows)
        squared = jnp.sum(ridged * ridged) + RIDGE_TERM * RIDGE_TERM * (emb - n_rows)
    else:
        def add(b, carry):
            part = every[b // 2, b % 2].reshape(half, emb)
            moment = lax.dot_general(
                part, part, (((0,), (0,)), ((), ())), preferred_element_type=jnp.float32
            )
            u1[...] += moment
            return carry + jnp.sum(part.astype(jnp.float32), axis=0, keepdims=True)

        u1[...] = jnp.zeros_like(u1)
        average = lax.fori_loop(0, n_dp * 2, add, jnp.zeros((1, emb), jnp.float32)) / n_rows
        tall = jnp.transpose(jnp.broadcast_to(average, (emb, emb)))
        ridged = u1[...] / n_rows - tall * average + RIDGE_TERM * eye(emb)
        squared = jnp.sum(ridged * ridged)
    doubled = 2.0 * lax.rsqrt(squared)
    t1 = ridged * doubled
    u1[...] = t1
    t1b = t1.astype(bf)
    t2 = 2.0 * t1 - mul(t1, t1b)
    t2b = t2.astype(bf)
    t4 = 2.0 * t2 - mul(t2, t2b)
    t4b = t4.astype(bf)
    if n_rows < emb:
        lane = lax.broadcasted_iota(jnp.int32, (pass_rows, n_rows), 1)
        here = (lane == mark + lax.broadcasted_iota(jnp.int32, (pass_rows, n_rows), 0)).astype(jnp.float32)
        mix = 2.0 * here - u1[pl.ds(pl.multiple_of(mark, pass_rows), pass_rows), :]
        times = mul
    else:
        mix = embedded - average
        mix = 2.0 * mix - mul2(mix, t1b)
        times = mul2
    mix = 2.0 * mix - times(mix, t2b)
    mix = 2.0 * mix - times(mix, t4b)
    rest = mix - times(mix, t4b)
    mix = mix + (rest - times(rest, t4b))
    if n_rows < emb:
        mixed = mul2(mix, rows_all) - jnp.sum(mix, axis=1, keepdims=True) * average
        mix = mixed + jnp.sum(mix * here, axis=1, keepdims=True) * (embedded - rounded)
    whitened = (mix * doubled).astype(bf)
    routed = jnp.dot(choose[...], whitened, preferred_element_type=jnp.float32)
    for p in range(n_dp):
        outgoing[p] = routed[p * capacity : (p + 1) * capacity]
    sixth = [send(outgoing.at[p], out_ref.at[i], ts.at[e], tr.at[e], (p, j)) for e, p in enumerate(planes)]
    kept = pltpu.make_async_copy(outgoing.at[i], out_ref.at[i], h_sem.at[0])
    kept.start()
    kept.wait()
    for copy in sixth:
        copy.wait_recv()

    for copy in pending[kept_up:]:
        copy.wait_send()


def encode(hidden, lengths, norm_gain, up, down, pool_gain, proj, owners, n_dp, n_fsdp):
    tok_rows, width = hidden.shape
    pass_rows = lengths.shape[0]
    nz = n_fsdp // 2
    ff_rows = down.shape[0]
    d_rows, emb = proj.shape
    half = nz * pass_rows
    wide = -(-ff_rows // LANES)
    chunks = nz * wide
    subs = chunks // PLANE
    legs = [len([s for s in range(subs) if s % 3 == r]) for r in range(3)]
    if up.shape[1] != 2 * chunks * LANES:
        up = jnp.pad(
            up.reshape(up.shape[0], n_fsdp, ff_rows), ((0, 0), (0, 0), (0, wide * LANES - ff_rows))
        ).reshape(up.shape[0], n_fsdp * wide * LANES)
    capacity = 2 * pass_rows // n_dp
    side = min(emb, n_dp * n_fsdp * pass_rows)
    bf = jnp.bfloat16
    f32 = jnp.float32
    dma = pltpu.SemaphoreType.DMA
    hbm = pl.BlockSpec(memory_space=pl.ANY)
    in_z = (subs + legs[2]) * nz
    return pl.pallas_call(
        functools.partial(embed_kernel, n_dp, n_fsdp, width),
        out_shape=jax.ShapeDtypeStruct((n_dp, capacity, emb), f32),
        in_specs=[hbm] * 8,
        out_specs=hbm,
        scratch_shapes=[
            pltpu.VMEM((tok_rows, width), bf),
            pltpu.VMEM((2, tok_rows, width), bf),
            pltpu.VMEM((chunks, width, LANES), bf),
            pltpu.VMEM((2, ff_rows, width), bf),
            pltpu.VMEM((nz, 2 * d_rows, emb), bf),
            pltpu.VMEM((nz, 2, pass_rows, wide * LANES), bf),
            pltpu.VMEM((2, nz, pass_rows, wide * LANES), bf),
            pltpu.VMEM((half, width), f32),
            pltpu.VMEM((2, nz, pass_rows, width // 2), bf),
            pltpu.VMEM((2, nz, pass_rows, width // 2), bf),
            pltpu.VMEM((n_dp, 2, nz, pass_rows, emb), bf),
            pltpu.VMEM((side, side), f32),
            pltpu.VMEM((n_dp, capacity, emb), f32),
            pltpu.VMEM((n_dp * capacity, pass_rows), bf),
            pltpu.VMEM((pass_rows, LANES), f32),
            pltpu.SMEM((pass_rows,), jnp.int32),
            pltpu.SMEM((pass_rows,), jnp.int32),
            pltpu.VMEM((width,), f32),
            pltpu.VMEM((width,), f32),
            dma((5,)),
            dma((chunks,)),
            dma((chunks,)),
            dma((chunks,)),
            dma((in_z,)),
            dma((in_z,)),
            dma((in_z // nz * len(HOPS) * 2,)),
            dma((in_z,)),
            dma(((subs + legs[0]) * nz,)),
            dma(((subs + legs[0]) * nz,)),
            dma(((subs + legs[1]) * nz,)),
            dma(((subs + legs[1]) * nz,)),
            dma,
            dma,
            dma((2,)),
            dma((2,)),
            dma((2,)),
            dma((n_fsdp,)),
            dma((n_fsdp,)),
        ]
        + [dma((2 * nz,))] * 2
        + [dma((nz,))] * 2
        + [dma((3 * nz,))] * 2
        + [dma((nz,))] * 4
        + [dma((max(3 * nz, n_dp),))] * 2
        + [dma((n_dp,))] * 2
        + [dma((n_dp - 1,))] * 2,
        compiler_params=pltpu.CompilerParams(
            collective_id=0, has_side_effects=True, vmem_limit_bytes=60 * 1024 * 1024
        ),
        name="embed",
    )(hidden, lengths, norm_gain, up, down, pool_gain, proj, owners)


def on_device(hidden, lengths, norm_gain, up_weight, down_weight, pool_gain, proj_weight, owners):
    n_dp, n_fsdp = lax.axis_size("dp"), lax.axis_size("fsdp")
    owned = encode(
        hidden, lengths, norm_gain, up_weight, down_weight, pool_gain, proj_weight,
        owners.reshape(-1), n_dp, n_fsdp,
    )
    return owned.reshape(-1, owned.shape[2]).astype(jnp.bfloat16)


def solution(mesh):
    placed = (
        P(("dp", "fsdp"), None),
        P(("dp", "fsdp")),
        P(),
        P("fsdp", None),
        P("fsdp", None),
        P(),
        P("fsdp", None),
        P(("dp", "fsdp"), None),
    )
    return jax.shard_map(
        on_device, mesh=mesh, in_specs=placed, out_specs=P(("dp", "fsdp"), None), check_vma=False
    )
```

```python
import functools

import jax
import jax.numpy as jnp
from jax import lax
from jax.experimental import pallas as pl
from jax.experimental.pallas import tpu as pltpu
from jax.sharding import PartitionSpec as P

RIDGE_TERM = 1.0
EPSILON = 1e-06
MESH = pl.DeviceIdType.MESH
PLANE = 4
LANES = 128
LAG = 4
RELAY_LAG = 4
REACH = 1
HOPS = (1, -1)


def remote(src, dst, send, recv, device):
    return pltpu.make_async_remote_copy(
        src_ref=src, dst_ref=dst, send_sem=send, recv_sem=recv, device_id=device, device_id_type=MESH
    )


def meet(devices):
    barrier = pltpu.get_barrier_semaphore()
    for device in devices:
        pl.semaphore_signal(barrier, inc=1, device_id=device, device_id_type=MESH)
    return barrier


def gelu(v):
    return 0.5 * v * (1.0 + jnp.tanh(0.7978845608028654 * (v + 0.044715 * (v * v * v))))


def nearest(nz):
    return [sorted((l for l in range(nz) if l != v), key=lambda l: (abs(l - v), l)) for v in range(nz)]


def pick(index, table):
    value = table[0]
    for v in range(1, len(table)):
        value = jnp.where(index == v, table[v], value)
    return value


def embed_kernel(
    n_dp, n_fsdp, width,
    hid_ref, len_hbm, ngain_hbm, up_ref, down_ref, pgain_hbm, proj_ref, own_hbm,
    out_ref,
    hid, nrm, upb, down2, pj, sa, ra, hs, s2, r2, every, u1, outgoing, choose, sizes,
    len_ref, own_ref, ngain_ref, pgain_ref,
    h_sem, lo_sem, ps, pr, zu, zd, zo, zr, xs, xr, ys, yr, ns, nr,
    dl, dns, dnr, as_, ar, s2s, r2s, s3s, r3s, js, jr, ks, kr, es, er, fs, fr, qs, qr, ts, tr,
):
    i = lax.axis_index("dp")
    j = lax.axis_index("fsdp")
    nz = n_fsdp // 2
    z = j // 2
    c = j % 2
    q = i % PLANE
    base = i - q
    rows = up_ref.shape[0]
    level_rows = 2 * rows
    chunks = upb.shape[0]
    subs = chunks // PLANE
    wide = chunks // nz
    per = subs // wide
    pass_rows, seq = hs.shape[0] // nz, hid.shape[0] // (hs.shape[0] // nz)
    half = nz * pass_rows
    ff_rows = down_ref.shape[0]
    emb = proj_ref.shape[1]
    d_rows = proj_ref.shape[0]
    part_rows = 2 * d_rows // PLANE
    qx = q + 1 - 2 * (q % 2)
    qy = q + 2 - 4 * (q // 2)
    qd = 3 - q
    partner = (i, z * 2 + 1 - c)
    near_x = (base + qx, j)
    near_y = (base + qy, j)
    peers = [(j + d) % n_fsdp for d in range(1, n_fsdp)]
    levels = [(z + d) % nz for d in range(1, nz)]
    planes = [(i + e) % n_dp for e in range(1, n_dp)]
    order = nearest(nz)
    near = [pick(z, [order[v][s] for v in range(nz)]) for s in range(nz - 1)]
    pending = []

    def along(level):
        return (i, level * 2 + c)

    def send(src, dst, ssem, rsem, device):
        copy = remote(src, dst, ssem, rsem, device)
        copy.start()
        pending.append(copy)
        return copy

    barrier = meet([(i, p) for p in peers] + [(p, j) for p in planes])

    own_k = [q * subs + s for s in range(subs)]
    x_k = [qx * subs + s for s in range(subs)]
    y_k = [qy * subs + s for s in range(subs)]
    d_k = [qd * subs + s for s in range(subs)]
    by_x = [s for s in range(subs) if s % 3 == 0]
    by_y = [s for s in range(subs) if s % 3 == 1]
    by_z = [s for s in range(subs) if s % 3 == 2]
    z_k = own_k + [d_k[s] for s in by_z]
    first = z_k + x_k + y_k + [d_k[s] for s in by_x + by_y]

    def source(core, k):
        at = ((k // wide * 2 + core) * wide + k % wide) * LANES
        return up_ref.at[:, pl.ds(pl.multiple_of(at, LANES), LANES)]

    def mine(k):
        return upb.at[k, pl.ds(pl.multiple_of(j * rows, rows), rows), :]

    def piece(k, level):
        return upb.at[k, pl.ds(pl.multiple_of(level * level_rows, level_rows), level_rows), :]

    local = []
    for n, k in enumerate(first):
        copy = pltpu.make_async_copy(source(c, k), mine(k), lo_sem.at[n])
        copy.start()
        local.append(copy)
    staged = [(hid_ref, hid), (ngain_hbm, ngain_ref), (len_hbm, len_ref), (own_hbm, own_ref), (pgain_hbm, pgain_ref)]
    staged = [pltpu.make_async_copy(src, dst, h_sem.at[n]) for n, (src, dst) in enumerate(staged)]
    for copy in staged:
        copy.start()
    pl.semaphore_wait(barrier, len(peers) + len(planes))
    swapped = []

    def swap(n):
        swapped.append(send(source(1 - c, first[n]), mine(first[n]), ps.at[n], pr.at[n], partner))

    def z_copy(t, level, hop):
        part = piece(z_k[t], level)
        sems = zu if hop == 1 else zd
        return remote(part, part, sems.at[t * nz + level], zr.at[t * nz + level], along(z + hop))

    def reaches(hop):
        return z + hop < nz if hop > 0 else z + hop >= 0

    def relays(level, hop):
        beyond = level <= z - REACH if hop > 0 else level >= z + REACH
        return jnp.logical_and(beyond, reaches(hop))

    def first_hop(t, h, e):
        core = c if e == 0 else 1 - c
        at = (t * len(HOPS) + h) * 2 + e
        return remote(
            source(core, z_k[t]), mine(z_k[t]), zo.at[at], zr.at[t * nz + z],
            (i, (z + HOPS[h]) * 2 + core),
        )

    def start_z(t):
        for h, hop in enumerate(HOPS):

            @pl.when(reaches(hop))
            def _():
                first_hop(t, h, 0).start()
                first_hop(t, h, 1).start()

    start_z(0)
    start_z(1)
    for n in range(chunks):
        swap(n)
    def proj_rows():
        return pj.at[z, pl.ds(pl.multiple_of(c * d_rows, d_rows), d_rows), :]

    def proj_part(level, plane):
        return pj.at[
            level,
            pl.ds(pl.multiple_of(plane * part_rows, part_rows), part_rows),
            pl.ds(pl.multiple_of(c * (emb // 2), emb // 2), emb // 2),
        ]

    def proj_side(level):
        return pj.at[level, :, pl.ds(pl.multiple_of(c * (emb // 2), emb // 2), emb // 2)]

    down_copy = pltpu.make_async_copy(down_ref, down2.at[c], dl.at[0])
    down_copy.start()
    proj_copy = pltpu.make_async_copy(proj_ref, proj_rows(), dl.at[1])
    proj_copy.start()
    for copy in staged:
        copy.wait()
    gain = ngain_ref[...].reshape(1, width)
    hs[...] = jnp.zeros_like(hs)

    def norm_block(p, carry):
        at = pl.ds(pl.multiple_of(p * seq, seq), seq)
        x = hid[at, :].astype(jnp.float32)
        keep = lax.broadcasted_iota(jnp.int32, (seq, 1), 0) < len_ref[p]
        scale = lax.rsqrt(jnp.sum(x * x, axis=1, keepdims=True) / width + EPSILON)
        scale = jnp.where(keep, scale, 0.0)
        nrm[c, at, :] = (x * scale * gain).astype(nrm.dtype)
        total = jnp.sum(jnp.where(keep, x, 0.0), axis=0, keepdims=True)
        hs[pl.ds(z * pass_rows + p, 1), :] = total
        return carry

    lax.fori_loop(0, pass_rows, norm_block, 0)
    nrm_copy = send(nrm.at[c], nrm.at[c], ns, nr, partner)
    down_swap = send(down_ref, down2.at[c], dns.at[0], dnr.at[0], partner)
    proj_swap = send(proj_ref, proj_rows(), dns.at[1], dnr.at[1], partner)
    row = lax.broadcasted_iota(jnp.int32, (pass_rows, LANES), 0)
    counts = jnp.zeros((pass_rows, LANES), jnp.float32)
    for p in range(pass_rows):
        counts = jnp.where(row == p, len_ref[p].astype(jnp.float32), counts)
    sizes[...] = counts
    capacity = outgoing.shape[1]
    targets = []
    for p in range(pass_rows):
        earlier = [(own_ref[p] == own_ref[o]).astype(jnp.int32) for o in range(p)]
        targets.append(own_ref[p] * capacity + sum(earlier))
    slot_at = lax.broadcasted_iota(jnp.int32, (n_dp * capacity, pass_rows), 0)
    pass_at = lax.broadcasted_iota(jnp.int32, (n_dp * capacity, pass_rows), 1)
    wanted = jnp.full((n_dp * capacity, pass_rows), -1, jnp.int32)
    for p in range(pass_rows):
        wanted = jnp.where(pass_at == p, targets[p], wanted)
    choose[...] = (slot_at == wanted).astype(jnp.float32).astype(choose.dtype)


    def along_x(slot, k, level):
        part = piece(k, level)
        return send(part, part, xs.at[slot * nz + level], xr.at[slot * nz + level], near_x)

    def along_y(slot, k, level):
        part = piece(k, level)
        return send(part, part, ys.at[slot * nz + level], yr.at[slot * nz + level], near_y)

    done = []
    x_sent, y_sent, x_relay, y_relay = {}, {}, {}, {}

    def z_step(t, s):
        level = near[s]
        z_copy(t, level, 1).wait_recv()
        for hop in (1, -1):

            @pl.when(relays(level, hop))
            def _():
                z_copy(t, level, hop).start()

        if t < subs:
            x_sent[t, s] = along_x(t, own_k[t], level)
            y_sent[t, s] = along_y(t, own_k[t], level)

    def xy_step(t, s):
        level = near[s]
        x_sent[t, s].wait_recv()
        y_sent[t, s].wait_recv()
        if t in by_x:
            x_relay[t, s] = along_x(subs + by_x.index(t), y_k[t], level)
        if t in by_y:
            y_relay[t, s] = along_y(subs + by_y.index(t), x_k[t], level)

    def compute(items):
        def slot(core, carry):
            block = [upb[quarter * subs + s] for quarter, s in items]
            block = jnp.concatenate(block, axis=1) if len(block) > 1 else block[0]
            pre = jnp.dot(nrm[core], block, preferred_element_type=jnp.float32)
            total = jnp.sum(gelu(pre).reshape(pass_rows, seq, block.shape[1]), axis=1)
            for n, (quarter, s) in enumerate(items):
                o = s % wide
                sa[quarter * per + s // wide, core, :, o * LANES : (o + 1) * LANES] = total[
                    :, n * LANES : (n + 1) * LANES
                ].astype(sa.dtype)
            return carry

        lax.fori_loop(0, 2, slot, 0)

    def act_copy(v, e):
        core = c if e == 0 else 1 - c
        return remote(
            sa.at[v, core], ra.at[c, z], as_.at[v * 2 + e], ar.at[c * nz + z], (i, v * 2 + core)
        )

    def send_acts(quarter):
        for b in range(per):
            v = quarter * per + b

            @pl.when(v == z)
            def _():
                ra[c, z] = sa[v, c]

            @pl.when(v != z)
            def _():
                act_copy(v, 0).start()

            act_copy(v, 1).start()

    def proj_out(v):
        return remote(proj_part(z, q), proj_part(z, q), s3s.at[v], r3s.at[z], along(v))

    ready = []
    left = {}

    def run(least):
        if len(ready) < least:
            return
        batch = [ready.pop(0) for _ in range(min(2, len(ready)))]
        compute([(quarter, s) for _, quarter, s in batch])
        for name, quarter, _ in batch:
            left[name] = left.get(name, subs) - 1
            if left[name] == 0:
                send_acts(quarter)

    last_slot = nz - 2
    z_steps = [(t, s) for t in range(len(z_k)) for s in range(nz - 1)]
    xy_steps = [(t, s) for t in range(subs) for s in range(nz - 1)]
    ends = [("x", t, s) for t in by_x for s in range(nz - 1)] + [("y", t, s) for t in by_y for s in range(nz - 1)]
    ends = sorted(ends, key=lambda r: (r[1], r[2]))
    at_step = {r: r[1] * (nz - 1) + r[2] + LAG + RELAY_LAG for r in ends}
    started = 2
    for n in range(max([len(z_steps), len(xy_steps) + LAG] + [m + 1 for m in at_step.values()])):
        if n == subs * (nz - 1):
            proj_copy.wait()
            proj_swap.wait_recv()
            for v in levels:
                copy = proj_out(v)
                copy.start()
                pending.append(copy)
        if n < len(z_steps):
            t, s = z_steps[n]
            z_step(t, s)
            if s == last_slot:
                if started < len(z_k):
                    start_z(started)
                    started += 1
                local[t].wait()
                swapped[t].wait_recv()
                ready.append(("own", q, t) if t < subs else ("diag", qd, by_z[t - subs]))
        if 0 <= n - LAG < len(xy_steps):
            t, s = xy_steps[n - LAG]
            xy_step(t, s)
            if s == last_slot:
                if t == 0:
                    for copy, arrived in list(zip(local, swapped))[len(z_k) :]:
                        copy.wait()
                        arrived.wait_recv()
                ready.append(("x", qx, t))
                ready.append(("y", qy, t))
        for kind, t, s in ends:
            if at_step[kind, t, s] == n:
                (x_relay if kind == "x" else y_relay)[t, s].wait_recv()
                if s == last_slot:
                    ready.append(("diag", qd, t))
        if n == nz - 1:
            nrm_copy.wait_recv()
        if n >= nz - 1:
            run(2)
    while ready:
        run(1)

    beside = [(qx, near_x), (qy, near_y), (qd, (base + qd, j))]
    proj_sent = {}
    sent_up = len(pending)
    for e, v in enumerate(near):
        remote(proj_part(v, q), proj_part(v, q), s3s.at[v], r3s.at[v], along(v)).wait_recv()
        for n in range(2):
            at = n * nz + v
            proj_sent[n, e] = send(
                proj_part(v, q), proj_part(v, q), js.at[at], jr.at[at], beside[n][1]
            )

    down_copy.wait()
    down_swap.wait_recv()
    for v in range(nz):
        for e in range(2):
            core = c if e == 0 else 1 - c
            arrival = remote(
                sa.at[v, core], ra.at[core, v], as_.at[v * 2 + e], ar.at[core * nz + v], partner
            )
            if e == 0:

                @pl.when(v != z)
                def _():
                    arrival.wait_recv()

            else:
                arrival.wait_recv()

    acts = [ra[core].reshape(half, wide * LANES)[:, :ff_rows] for core in range(2)]

    def part_copy(b, v):
        return remote(s2.at[b, v], r2.at[b, z], s2s.at[b * nz + v], r2s.at[b * nz + z], along(v))

    def part_from(b, v):
        return remote(s2.at[b, v], r2.at[b, v], s2s.at[b * nz + v], r2s.at[b * nz + v], along(v))

    for b in range(2):
        at = slice(b * (width // 2), (b + 1) * (width // 2))
        part = hs[:, at]
        for core in range(2):
            part = part + jnp.dot(acts[core], down2[core, :, at], preferred_element_type=jnp.float32)
        s2[b] = part.astype(s2.dtype).reshape(nz, pass_rows, width // 2)
        for v in range(nz):

            @pl.when(v != z)
            def _():
                part_copy(b, v).start()

    for copy in pending[:sent_up]:
        copy.wait_send()
    for t in range(len(z_k)):
        for h, hop in enumerate(HOPS):

            @pl.when(reaches(hop))
            def _():
                first_hop(t, h, 0).wait_send()
                first_hop(t, h, 1).wait_send()

        for level in range(nz):
            for hop in (1, -1):

                @pl.when(relays(level, hop))
                def _():
                    z_copy(t, level, hop).wait_send()

    for v in range(nz):

        @pl.when(v != z)
        def _():
            act_copy(v, 0).wait_send()

        act_copy(v, 1).wait_send()

    proj_last = []
    for e, v in enumerate(near):
        for n in range(2):
            proj_sent[n, e].wait_recv()
        part = proj_part(v, beside[e % 2][0])
        at = 2 * nz + v
        proj_sent[2, e] = send(part, part, js.at[at], jr.at[at], beside[1 - e % 2][1])
    for e, v in enumerate(near):
        proj_sent[2, e].wait_recv()
        proj_last.append(send(proj_side(v), proj_side(v), ks.at[v], kr.at[v], partner))
    halves = []
    for b in range(2):
        total = s2[b, z].astype(jnp.float32)
        for v in near:
            part_from(b, v).wait_recv()
            total = total + r2[b, v].astype(jnp.float32)
        halves.append(total)
    pooled = jnp.concatenate(halves, axis=1)
    counts = sizes[:, :1]
    norm = jnp.sum(pooled * pooled, axis=1, keepdims=True) / width
    scaled = pooled * lax.rsqrt(norm + EPSILON * (counts * counts)) * pgain_ref[...].reshape(1, width)
    scaled = scaled.astype(proj_ref.dtype)
    for copy in proj_last:
        copy.wait_recv()
    embedded = jnp.dot(scaled, pj[...].reshape(width, emb), preferred_element_type=jnp.float32)
    every[i, c, z] = embedded.astype(every.dtype)

    def to_level(v):
        part = every.at[i, c, z]
        return remote(part, part, es.at[v], er.at[z], along(v))

    def from_level(v):
        part = every.at[i, c, v]
        return remote(part, part, es.at[v], er.at[v], along(v))

    for v in levels:
        copy = to_level(v)
        copy.start()
        pending.append(copy)
    last = []

    def to_partner(part, n):
        last.append(send(part, part, qs.at[n], qr.at[n], partner))

    if n_dp == PLANE:
        seen = [z] + near
        across = {}
        for e in range(nz):
            if e > 0:
                from_level(seen[e]).wait_recv()
            part = every.at[i, c, seen[e]]
            for n, (_, device) in enumerate(beside):
                at = n * nz + seen[e]
                across[n, e] = send(part, part, fs.at[at], fr.at[at], device)
        to_partner(every.at[i, c], 0)
        for n, (plane, _) in enumerate(beside):
            for e in range(nz):
                across[n, e].wait_recv()
            to_partner(every.at[plane, c], n + 1)
    else:
        for v in levels:
            from_level(v).wait_recv()
        part = every.at[i, c]
        fifth = [send(part, part, fs.at[e], fr.at[e], (p, j)) for e, p in enumerate(planes)]
        to_partner(part, 0)
        for e, copy in enumerate(fifth):
            copy.wait_recv()
            to_partner(every.at[(i + n_dp - e - 1) % n_dp, c], e + 1)

    for b in range(2):
        for v in range(nz):

            @pl.when(v != z)
            def _():
                part_copy(b, v).wait_send()

    n_rows = n_dp * n_fsdp * pass_rows

    def side(core):
        return jnp.concatenate([every[p, core].reshape(half, emb) for p in range(n_dp)], axis=0)

    def pairs(a, b):
        return lax.dot_general(a, b, (((1,), (1,)), ((), ())), preferred_element_type=jnp.float32)

    def column_sum(a):
        return jnp.sum(a.astype(jnp.float32), axis=0, keepdims=True)

    if n_rows < emb:
        mine_rows = side(c)
        mine_pairs = pairs(mine_rows, mine_rows)
        mine_sum = column_sum(mine_rows)
    for copy in last:
        copy.wait_recv()
    for copy in pending[sent_up:]:
        copy.wait_send()
    kept_up = len(pending)

    bf = jnp.bfloat16
    mark = (i * nz + z) * pass_rows
    rounded = every[i, c, z].astype(jnp.float32)

    def mul(a, b):
        return jnp.dot(a.astype(bf), b, preferred_element_type=jnp.float32)

    def mul2(a, b):
        high = a.astype(bf)
        return mul(high, b) + mul(a - high.astype(jnp.float32), b)

    def eye(n):
        at = lax.broadcasted_iota(jnp.int32, (n, n), 0)
        return (at == lax.broadcasted_iota(jnp.int32, (n, n), 1)).astype(jnp.float32)

    if n_rows < emb:
        other_rows = side(1 - c)
        rows_all = jnp.concatenate([mine_rows, other_rows], axis=0)
        average = (mine_sum + column_sum(other_rows)) / n_rows
        upper = jnp.concatenate([mine_pairs, pairs(mine_rows, other_rows)], axis=1)
        gram = jnp.concatenate([upper, pairs(other_rows, rows_all)], axis=0) / n_rows
        by_col = jnp.mean(gram, axis=0, keepdims=True)
        by_row = jnp.mean(gram, axis=1, keepdims=True)
        ridged = gram - by_col - by_row + jnp.mean(by_col) + RIDGE_TERM * eye(n_rows)
        squared = jnp.sum(ridged * ridged) + RIDGE_TERM * RIDGE_TERM * (emb - n_rows)
    else:
        def add(b, carry):
            part = every[b // 2, b % 2].reshape(half, emb)
            moment = lax.dot_general(
                part, part, (((0,), (0,)), ((), ())), preferred_element_type=jnp.float32
            )
            u1[...] += moment
            return carry + jnp.sum(part.astype(jnp.float32), axis=0, keepdims=True)

        u1[...] = jnp.zeros_like(u1)
        average = lax.fori_loop(0, n_dp * 2, add, jnp.zeros((1, emb), jnp.float32)) / n_rows
        tall = jnp.transpose(jnp.broadcast_to(average, (emb, emb)))
        ridged = u1[...] / n_rows - tall * average + RIDGE_TERM * eye(emb)
        squared = jnp.sum(ridged * ridged)
    doubled = 2.0 * lax.rsqrt(squared)
    t1 = ridged * doubled
    u1[...] = t1
    t1b = t1.astype(bf)
    t2 = 2.0 * t1 - mul(t1, t1b)
    t2b = t2.astype(bf)
    t4 = 2.0 * t2 - mul(t2, t2b)
    t4b = t4.astype(bf)
    if n_rows < emb:
        lane = lax.broadcasted_iota(jnp.int32, (pass_rows, n_rows), 1)
        here = (lane == mark + lax.broadcasted_iota(jnp.int32, (pass_rows, n_rows), 0)).astype(jnp.float32)
        mix = 2.0 * here - u1[pl.ds(pl.multiple_of(mark, pass_rows), pass_rows), :]
        times = mul
    else:
        mix = embedded - average
        mix = 2.0 * mix - mul2(mix, t1b)
        times = mul2
    mix = 2.0 * mix - times(mix, t2b)
    mix = 2.0 * mix - times(mix, t4b)
    rest = mix - times(mix, t4b)
    mix = mix + (rest - times(rest, t4b))
    if n_rows < emb:
        mixed = mul2(mix, rows_all) - jnp.sum(mix, axis=1, keepdims=True) * average
        mix = mixed + jnp.sum(mix * here, axis=1, keepdims=True) * (embedded - rounded)
    whitened = (mix * doubled).astype(bf)
    routed = jnp.dot(choose[...], whitened, preferred_element_type=jnp.float32)
    for p in range(n_dp):
        outgoing[p] = routed[p * capacity : (p + 1) * capacity]
    sixth = [send(outgoing.at[p], out_ref.at[i], ts.at[e], tr.at[e], (p, j)) for e, p in enumerate(planes)]
    kept = pltpu.make_async_copy(outgoing.at[i], out_ref.at[i], h_sem.at[0])
    kept.start()
    kept.wait()
    for copy in sixth:
        copy.wait_recv()

    for copy in pending[kept_up:]:
        copy.wait_send()


def encode(hidden, lengths, norm_gain, up, down, pool_gain, proj, owners, n_dp, n_fsdp):
    tok_rows, width = hidden.shape
    pass_rows = lengths.shape[0]
    nz = n_fsdp // 2
    ff_rows = down.shape[0]
    d_rows, emb = proj.shape
    half = nz * pass_rows
    wide = -(-ff_rows // LANES)
    chunks = nz * wide
    subs = chunks // PLANE
    legs = [len([s for s in range(subs) if s % 3 == r]) for r in range(3)]
    if up.shape[1] != 2 * chunks * LANES:
        up = jnp.pad(
            up.reshape(up.shape[0], n_fsdp, ff_rows), ((0, 0), (0, 0), (0, wide * LANES - ff_rows))
        ).reshape(up.shape[0], n_fsdp * wide * LANES)
    capacity = 2 * pass_rows // n_dp
    side = min(emb, n_dp * n_fsdp * pass_rows)
    bf = jnp.bfloat16
    f32 = jnp.float32
    dma = pltpu.SemaphoreType.DMA
    hbm = pl.BlockSpec(memory_space=pl.ANY)
    in_z = (subs + legs[2]) * nz
    return pl.pallas_call(
        functools.partial(embed_kernel, n_dp, n_fsdp, width),
        out_shape=jax.ShapeDtypeStruct((n_dp, capacity, emb), f32),
        in_specs=[hbm] * 8,
        out_specs=hbm,
        scratch_shapes=[
            pltpu.VMEM((tok_rows, width), bf),
            pltpu.VMEM((2, tok_rows, width), bf),
            pltpu.VMEM((chunks, width, LANES), bf),
            pltpu.VMEM((2, ff_rows, width), bf),
            pltpu.VMEM((nz, 2 * d_rows, emb), bf),
            pltpu.VMEM((nz, 2, pass_rows, wide * LANES), bf),
            pltpu.VMEM((2, nz, pass_rows, wide * LANES), bf),
            pltpu.VMEM((half, width), f32),
            pltpu.VMEM((2, nz, pass_rows, width // 2), bf),
            pltpu.VMEM((2, nz, pass_rows, width // 2), bf),
            pltpu.VMEM((n_dp, 2, nz, pass_rows, emb), bf),
            pltpu.VMEM((side, side), f32),
            pltpu.VMEM((n_dp, capacity, emb), f32),
            pltpu.VMEM((n_dp * capacity, pass_rows), bf),
            pltpu.VMEM((pass_rows, LANES), f32),
            pltpu.SMEM((pass_rows,), jnp.int32),
            pltpu.SMEM((pass_rows,), jnp.int32),
            pltpu.VMEM((width,), f32),
            pltpu.VMEM((width,), f32),
            dma((5,)),
            dma((chunks,)),
            dma((chunks,)),
            dma((chunks,)),
            dma((in_z,)),
            dma((in_z,)),
            dma((in_z // nz * len(HOPS) * 2,)),
            dma((in_z,)),
            dma(((subs + legs[0]) * nz,)),
            dma(((subs + legs[0]) * nz,)),
            dma(((subs + legs[1]) * nz,)),
            dma(((subs + legs[1]) * nz,)),
            dma,
            dma,
            dma((2,)),
            dma((2,)),
            dma((2,)),
            dma((n_fsdp,)),
            dma((n_fsdp,)),
        ]
        + [dma((2 * nz,))] * 2
        + [dma((nz,))] * 2
        + [dma((3 * nz,))] * 2
        + [dma((nz,))] * 4
        + [dma((max(3 * nz, n_dp),))] * 2
        + [dma((n_dp,))] * 2
        + [dma((n_dp - 1,))] * 2,
        compiler_params=pltpu.CompilerParams(
            collective_id=0, has_side_effects=True, vmem_limit_bytes=60 * 1024 * 1024
        ),
        name="embed",
    )(hidden, lengths, norm_gain, up, down, pool_gain, proj, owners)


def on_device(hidden, lengths, norm_gain, up_weight, down_weight, pool_gain, proj_weight, owners):
    n_dp, n_fsdp = lax.axis_size("dp"), lax.axis_size("fsdp")
    owned = encode(
        hidden, lengths, norm_gain, up_weight, down_weight, pool_gain, proj_weight,
        owners.reshape(-1), n_dp, n_fsdp,
    )
    return owned.reshape(-1, owned.shape[2]).astype(jnp.bfloat16)


def solution(mesh):
    placed = (
        P(("dp", "fsdp"), None),
        P(("dp", "fsdp")),
        P(),
        P("fsdp", None),
        P("fsdp", None),
        P(),
        P("fsdp", None),
        P(("dp", "fsdp"), None),
    )
    return jax.shard_map(
        on_device, mesh=mesh, in_specs=placed, out_specs=P(("dp", "fsdp"), None), check_vma=False
    )
```
